256 devices in a mesh: cell: 32 (over x, y, core), gene: 8 (over z).
Axes of the slice: x: 4, y: 4, z: 8, core: 2. Of those that a mesh axis runs over, the one named last changes fastest.
Arguments:
- counts: int32 [3072, 32768], P('gene', 'cell'), may hold values from 0 to 11
- batch_id: int32 [32768], P('cell'), may hold values from 0 to 63
- live_cells: int32 [32], P('cell'), may hold values from 256 to 1024, as said below
- knot_bin: int32 [32768], P('cell'), may hold values from 0 to 14
- depth_frac: float32 [32768], P('cell'), may hold values from 0 to 1
- cell_covariates: float32 [16, 32768], P(None, 'cell'), may hold values from -3 to 3
- coefficients: float32 [3072, 32], P('gene'), may hold values from -1.2 to 1.2
- batch_effect: float32 [3072, 64], P('gene'), may hold values from -1.8 to 1.8
- factors: bfloat16 [32768, 64], P('cell'), may hold values from -4 to 4
- loadings: bfloat16 [3072, 64], P('gene'), may hold values from -0.19921875 to 0.19921875
Outputs:
- beta_step: float32 [3072, 32], P('gene')
- factor_step: float32 [32768, 64], P('cell')
- loading_score: float32 [3072, 64], P('gene')
The draws below stay inside these ranges and needn't reach their ends.
Inputs may be any that keep to these rules, and one draw needn't show every extreme that they name: `live_cells`: each index of the cell axis has its live cells in its first slots, at least 256 of them; some index is full in every draw.
All inputs are finite; a program needn't handle non-finite values.
Results may differ from the reference program's by a relative error of at most 0.0003.
Values sent between devices are 32-bit elements; how exact they have to be, the bound alone decides.
No kernel may reach another device: no remote copies, remote signals or barrier semaphores. Data moves between devices by JAX's collectives and lax.ppermute only.
A program may use at most 64 MiB of HBM per device.

```python
import math
import jax
import jax.numpy as jnp
import numpy as np
from jax import lax

GENES = 3072
SPL = 16
COV = 16
FACTORS = 64
BATCHES = 64
CDEV = 1024
COVARS = 32
CELLS = 32768
NSHARD = 32
N_GENE = 8


def draw_live_cells(key, part):
    first_key, second_key = jax.random.split(jax.random.fold_in(key, 17))
    ladder = jax.random.randint(first_key, (NSHARD,), 0, 65)
    quarter = CDEV // 4
    live_count = quarter + (CDEV - quarter) * ladder * ladder // 4096
    chosen = jax.random.randint(second_key, (), 0, NSHARD)
    return jnp.where(jnp.arange(NSHARD, dtype=jnp.int32) == chosen, CDEV, live_count).astype(jnp.int32)


def set_ends(drawn, own_key, low, top_value):
    longest = drawn.shape.index(max(drawn.shape))
    spots = []
    for shift in (0, 1):
        where = [jax.random.randint(jax.random.fold_in(own_key, axis), (), 0, length) for axis, length in enumerate(drawn.shape)]
        where[longest] = (where[longest] + shift) % drawn.shape[longest]
        spots.append(tuple(where))
    return drawn.at[spots[0]].set(low).at[spots[1]].set(top_value)


def level_of(key, dims, cuts, low, largest):
    def one(position, shards_of):
        heights = jax.random.uniform(jax.random.fold_in(jax.random.fold_in(key, 6), position), (shards_of,), jnp.float32, low / len(cuts), largest / len(cuts))
        return jnp.repeat(jnp.exp(heights), dims[position] // shards_of).reshape((-1,) + (1,) * (len(dims) - position - 1))

    level = one(*cuts[0])
    for cut in cuts[1:]:
        level = level * one(*cut)
    return level


def rank_bounds(count, slope):
    loads = [(1 << 20) // math.isqrt(rank ** slope) + 1 for rank in range(1, count + 1)]
    scale = 1 + sum(loads) // (1 << 30)
    return np.cumsum(np.array([max(1, weight // scale) for weight in loads]))


def ranked_ids(stream_key, shape, amount, skew):
    listing = rank_bounds(amount, skew)
    lot = jax.random.randint(jax.random.fold_in(stream_key, 1), shape, 0, int(listing[amount - 1]))
    rank = jnp.searchsorted(jnp.asarray(listing, jnp.int32), lot, side="right")
    return jax.random.permutation(jax.random.fold_in(stream_key, 2), amount)[rank].astype(jnp.int32)


def scatter_about(rng, dims, deviation, most, cuts=(), kind=jnp.bfloat16):
    result = jax.random.normal(rng, dims, jnp.float32) * deviation
    if len(cuts) > 0:
        result = level_of(rng, dims, cuts, -0.22, 0.18) * result
    return jnp.clip(result, min=-most, max=most).astype(kind)


def setup_inputs(seed: int = 0) -> dict:
    splits = jax.random.split(jax.random.key(seed), 11)
    counts = set_ends(ranked_ids(splits[0], (GENES, CELLS), 12, 2), jax.random.fold_in(splits[0], 3), 0, 11).astype(jnp.int32)
    batch_id = set_ends(jax.random.randint(splits[1], (CELLS,), 0, BATCHES), jax.random.fold_in(splits[1], 1), 0, BATCHES - 1).astype(jnp.int32)
    live_cells = draw_live_cells(jax.random.fold_in(splits[10], 71), 0)
    knot_bin = set_ends(jax.random.randint(splits[3], (CELLS,), 0, SPL - 1), jax.random.fold_in(splits[3], 1), 0, (SPL - 1) - 1).astype(jnp.int32)
    depth_frac = jnp.clip(1.0 * jax.random.uniform(splits[4], (CELLS,), jnp.float32) ** level_of(splits[4], (CELLS,), ((0, 32),), -0.2, 0.2), 0.0, 1.0)
    cell_covariates = scatter_about(splits[5], (COV, CELLS), 0.5, 3.0, ((1, 32),), jnp.float32)
    coefficients = scatter_about(splits[6], (GENES, COVARS), 0.2, 1.2, ((0, 8),), jnp.float32)
    batch_effect = scatter_about(splits[7], (GENES, BATCHES), 0.3, 1.8, ((0, 8),), jnp.float32)
    factors = scatter_about(splits[8], (CELLS, FACTORS), 1.0, 4.0, ((0, 32),))
    loadings = scatter_about(splits[9], (GENES, FACTORS), 0.05, 0.19921875, ((0, 8),))
    return dict(counts=counts, batch_id=batch_id, live_cells=live_cells, knot_bin=knot_bin, depth_frac=depth_frac, cell_covariates=cell_covariates, coefficients=coefficients, batch_effect=batch_effect, factors=factors, loadings=loadings)


ridge_weight = 1.0

def design_rows(knot_bin, depth_frac, cell_covariates):
    levels = jnp.arange(SPL, dtype=jnp.int32)[:, None]
    fraction = depth_frac[None, :]
    hat_basis = jnp.where(levels == knot_bin[None, :], 1.0 - fraction, 0.0)
    hat_basis = hat_basis + jnp.where(levels == knot_bin[None, :] + 1, fraction, 0.0)
    return jnp.concatenate([hat_basis.astype(cell_covariates.dtype), cell_covariates], axis=0)

def newton_solve(gram_flat, score):
    columns = score.shape[-1]
    identity = jnp.eye(columns, dtype=gram_flat.dtype)
    system = gram_flat.reshape(-1, columns, columns) + ridge_weight * identity
    factor_lower = jnp.linalg.cholesky(system)
    middle = jax.scipy.linalg.solve_triangular(factor_lower, score[..., None], lower=True)
    return jax.scipy.linalg.solve_triangular(factor_lower, middle, lower=True, trans=1)[..., 0]

def reference(counts, batch_id, live_cells, knot_bin, depth_frac, cell_covariates, coefficients, batch_effect, factors, loadings):
    highest = lax.Precision.HIGHEST
    contract = (((1,), (1,)), ((), ()))
    totals = lax.optimization_barrier(jnp.sum(counts, axis=0)).astype(jnp.float32)
    offset = jnp.log((1.0 + totals) / GENES)
    positions = jnp.arange(CELLS, dtype=jnp.int32)
    live_mask = (positions % CDEV < live_cells[positions // CDEV]).astype(jnp.float32)
    design = design_rows(knot_bin, depth_frac, cell_covariates)
    columns = design.shape[0]
    pairs = (design[:, None, :] * design[None, :, :]).reshape(columns * columns, CELLS)
    onehot = (jnp.arange(BATCHES, dtype=jnp.int32)[:, None] == batch_id[None, :]).astype(jnp.float32)
    stacked = jnp.concatenate([design, onehot], axis=0)
    factors_wide = factors.astype(jnp.float32)
    gene_block = GENES // N_GENE

    def one_block(running, pieces):
        count_rows, coef_rows, shift_rows, load_rows = pieces
        observed = count_rows.astype(jnp.float32)
        linear = jnp.dot(jnp.concatenate([coef_rows, shift_rows], axis=1), stacked, precision=highest)
        latent = lax.dot_general(load_rows.astype(jnp.float32), factors.astype(jnp.float32), contract, preferred_element_type=jnp.float32)
        linear_pred = offset[None, :] + linear + latent
        expected = jnp.exp(linear_pred)
        weight = expected * live_mask
        residual = (observed - expected) * live_mask
        gram_part = lax.dot_general(weight, pairs, contract, precision=highest)
        score = lax.dot_general(residual, design, contract, precision=highest)
        beta_step = newton_solve(gram_part, score)
        expected_next = jnp.exp(linear_pred + jnp.dot(beta_step, design, precision=highest))
        weight_next = expected_next * live_mask
        residual_next = (observed - expected_next) * live_mask
        grad_load = jnp.dot(residual_next, factors_wide, precision=highest)
        curv_load = jnp.dot(weight_next, factors_wide * factors_wide, precision=highest)
        loads_wide = load_rows.astype(jnp.float32)
        back = (((0,), (0,)), ((), ()))
        grad_fact = running[0] + lax.dot_general(residual_next, loads_wide, back, precision=highest)
        curv_fact = running[1] + lax.dot_general(weight_next, loads_wide * loads_wide, back, precision=highest)
        return ((grad_fact, curv_fact), (beta_step, grad_load / jnp.sqrt(curv_load + 1.0)))
    pieces = (counts.reshape(N_GENE, gene_block, CELLS), coefficients.reshape(N_GENE, gene_block, columns), batch_effect.reshape(N_GENE, gene_block, BATCHES), loadings.reshape(N_GENE, gene_block, FACTORS))
    start = (jnp.zeros((CELLS, FACTORS), jnp.float32), jnp.zeros((CELLS, FACTORS), jnp.float32))
    sums, outputs = lax.scan(one_block, start, pieces)
    beta_step = outputs[0].reshape(GENES, columns)
    loading_score = outputs[1].reshape(GENES, FACTORS)
    factor_step = sums[0] / (sums[1] + 1.0)
    return (beta_step, factor_step, loading_score)
```

```python
import functools

import jax
import jax.numpy as jnp
from jax import lax
from jax.experimental import pallas as pl
from jax.experimental.pallas import tpu as pltpu
from jax.sharding import PartitionSpec as P

GENES = 3072
SPL = 16
COLS = 32
FACT = 64
CHUNK = 256
F32 = jnp.float32
BF16 = jnp.bfloat16
NN = (((1,), (0,)), ((), ()))
NT = (((1,), (1,)), ((), ()))
TN = (((0,), (0,)), ((), ()))
VMEM_LIMIT = 40 * 1024 * 1024


def dot(a, b, dims):
    return lax.dot_general(a, b, dims, preferred_element_type=F32)


def split2(x):
    hi = x.astype(BF16)
    return hi, (x - hi.astype(F32)).astype(BF16)


def split3(x):
    hi = x.astype(BF16)
    rest = x - hi.astype(F32)
    mid = rest.astype(BF16)
    return hi, mid, (rest - mid.astype(F32)).astype(BF16)


def full(shape):
    return pl.BlockSpec(shape, lambda c: (0,) * len(shape))


def lanes(rows, chunk=CHUNK):
    return pl.BlockSpec((rows, chunk), lambda c: (0, c))


def smem():
    return pl.BlockSpec(memory_space=pltpu.SMEM)


def params():
    return pltpu.CompilerParams(vmem_limit_bytes=VMEM_LIMIT)


def totals_kernel(counts_ref, out_ref, acc):
    step = pl.program_id(0)
    part = jnp.sum(counts_ref[...].astype(F32), axis=0, keepdims=True)

    @pl.when(step == 0)
    def _():
        acc[...] = part

    @pl.when(step > 0)
    def _():
        acc[...] += part

    @pl.when(step == pl.num_programs(0) - 1)
    def _():
        for i in range(8):
            row = acc[:, 128 * i : 128 * (i + 1)]
            out_ref[:, i : i + 1, :] = jnp.broadcast_to(row[None], (out_ref.shape[0], 1, 128))


def cell_totals(counts, peers):
    genes, cells = counts.shape
    return pl.pallas_call(
        totals_kernel,
        grid=(3,),
        in_specs=[pl.BlockSpec((genes // 3, cells), lambda c: (c, 0))],
        out_specs=full((peers, 8, 128)),
        out_shape=jax.ShapeDtypeStruct((peers, 8, 128), F32),
        scratch_shapes=[pltpu.VMEM((1, cells), F32)],
        compiler_params=params(),
        name="cell_totals",
    )(counts)


def prepare_kernel(
    knot_ref, frac_ref, batch_ref, cov_ref, coef_ref, shift_ref, load_ref, fact_ref,
    rest_ref, hi_ref, lo_ref, design_ref, left,
):
    @pl.when(pl.program_id(0) == 0)
    def _():
        c1, c2, c3 = split3(coef_ref[...])
        b1, b2, b3 = split3(shift_ref[...])
        left[...] = jnp.concatenate([c1, c1, c2, c2, c1, c3, b1, b2, b3, load_ref[...]], axis=0)

    knot, frac = knot_ref[...], frac_ref[...]
    width = knot.shape[1]
    cov = cov_ref[...]
    levels = lax.broadcasted_iota(jnp.int32, (SPL, width), 0)
    here, above = levels == knot, levels == knot + 1
    rest = 1.0 - frac
    hat = jnp.where(here, rest, 0.0) + jnp.where(above, frac, 0.0)
    d1, d2, d3 = split3(jnp.concatenate([hat, cov], axis=0))
    design_ref[...] = jnp.concatenate([d1, d2, d3], axis=0)
    batches = lax.broadcasted_iota(jnp.int32, (64, width), 0)
    onehot = (batches == batch_ref[...]).astype(F32).astype(BF16)
    right = jnp.concatenate(
        [d1, d2, d1, d2, d3, d1, onehot, onehot, onehot, fact_ref[...]], axis=0
    )
    rest_ref[...] = dot(left[...], right, TN)

    def put(at, value):
        hi, lo = split2(value)
        hi_ref[at : at + value.shape[0], :] = hi
        lo_ref[at : at + value.shape[0], :] = lo

    put(0, jnp.where(here, rest * rest, 0.0) + jnp.where(above, frac * frac, 0.0))
    put(16, jnp.where(here, rest * frac, 0.0))
    for p in range(SPL):
        put(32 + 16 * p, hat[p : p + 1, :] * cov)
    low, high = cov[:8], cov[8:]
    for i in range(0, 8, 2):
        put(288 + 8 * i, jnp.concatenate([low[i : i + 1] * low, low[i + 1 : i + 2] * low], axis=0))
        put(352 + 8 * i, jnp.concatenate([low[i : i + 1] * high, low[i + 1 : i + 2] * high], axis=0))
        put(416 + 8 * i, jnp.concatenate([high[i : i + 1] * high, high[i + 1 : i + 2] * high], axis=0))
    put(480, jnp.zeros((32, width), F32))


def prepare(knot, frac, batch, cov, coef, shift, load, fact):
    cells = knot.shape[1]
    genes = coef.shape[1]
    return pl.pallas_call(
        prepare_kernel,
        grid=(cells // CHUNK,),
        in_specs=[
            lanes(1), lanes(1), lanes(1), lanes(16),
            full((COLS, genes)), full((64, genes)), full((FACT, genes)), lanes(FACT),
        ],
        out_specs=[lanes(genes), lanes(512), lanes(512), lanes(96)],
        out_shape=[
            jax.ShapeDtypeStruct((genes, cells), F32),
            jax.ShapeDtypeStruct((512, cells), BF16),
            jax.ShapeDtypeStruct((512, cells), BF16),
            jax.ShapeDtypeStruct((96, cells), BF16),
        ],
        scratch_shapes=[pltpu.VMEM((448, genes), BF16)],
        compiler_params=params(),
        name="prepare",
    )(knot, frac, batch, cov, coef, shift, load, fact)


def gram_kernel(
    live_ref, tot_ref, rest_ref, counts_ref, hi_ref, lo_ref, design_ref,
    pred_ref, out_ref, offset, acc,
):
    step = pl.program_id(0)

    @pl.when(step == 0)
    def _():
        total = jnp.sum(tot_ref[...], axis=0)
        value = jnp.log((1.0 + total) / GENES)
        for i in range(8):
            offset[:, 128 * i : 128 * (i + 1)] = value[i : i + 1, :]

    at = pl.multiple_of(step * CHUNK, CHUNK)
    pred = rest_ref[...] + offset[:, pl.ds(at, CHUNK)]
    pred_ref[...] = pred
    expected = jnp.exp(pred)
    slot = lax.broadcasted_iota(jnp.int32, (1, CHUNK), 1) + at
    mask = (slot < live_ref[0]).astype(F32)
    weight = expected * mask
    residual = (counts_ref[...].astype(F32) - expected) * mask
    w1, w2 = split2(weight)
    r1, r2 = split2(residual)
    hi, lo = hi_ref[...], lo_ref[...]
    gram = dot(w1, hi, NT) + dot(w1, lo, NT) + dot(w2, hi, NT)
    blank = jnp.zeros((96, CHUNK), BF16)
    s1 = jnp.concatenate([blank, design_ref[:COLS, :]], axis=0)
    s2 = jnp.concatenate([blank, design_ref[COLS : 2 * COLS, :]], axis=0)
    score = dot(r1, s1, NT) + dot(r1, s2, NT) + dot(r2, s1, NT)

    @pl.when(step == 0)
    def _():
        acc[...] = jnp.zeros_like(acc)

    for t in range(4):
        part = gram[:, 128 * t : 128 * (t + 1)]
        acc[t] += part + score if t == 3 else part

    @pl.when(step == pl.num_programs(0) - 1)
    def _():
        for j in range(32):
            for t in range(4):
                out_ref[j, 12 * t : 12 * (t + 1), :] = acc[t, pl.ds(j, 12, stride=32), :]


def gram_sums(live, tot, rest, counts, hi, lo, design):
    genes, cells = counts.shape
    return pl.pallas_call(
        gram_kernel,
        grid=(cells // CHUNK,),
        in_specs=[
            smem(), full(tot.shape), lanes(genes), lanes(genes), lanes(512), lanes(512), lanes(96),
        ],
        out_specs=[lanes(genes), full((32, 48, 128))],
        out_shape=[
            jax.ShapeDtypeStruct((genes, cells), F32),
            jax.ShapeDtypeStruct((32, 48, 128), F32),
        ],
        scratch_shapes=[pltpu.VMEM((1, cells), F32), pltpu.VMEM((4, genes, 128), F32)],
        compiler_params=params(),
        name="gram_sums",
    )(live, tot, rest, counts, hi, lo, design)


def solve_kernel(parts_ref, out_ref, table):
    total = parts_ref[0]
    for j in range(1, 32):
        total = total + parts_ref[j]
    turned = jnp.concatenate([total, jnp.zeros((80, 128), F32)], axis=0).T
    for t in range(4):
        moved = turned if t == 0 else pltpu.roll(turned, 128 - 12 * t, axis=1)
        table[128 * t : 128 * (t + 1), :] = moved
    row16 = lax.broadcasted_iota(jnp.int32, (SPL, 128), 0)
    row32 = lax.broadcasted_iota(jnp.int32, (COLS, 128), 0)
    diag, near = table[0:16, :] + 1.0, table[16:32, :]
    below = pltpu.roll(near, 1, axis=0)
    system = []
    for j in range(SPL):
        top = jnp.where(row16 == j, diag, 0.0)
        top = jnp.where(row16 == j - 1, near, top)
        top = jnp.where(row16 == j + 1, below, top)
        system.append(jnp.concatenate([top, table[32 + 16 * j : 48 + 16 * j, :]], axis=0))
    for q in range(SPL):
        top = table[pl.ds(32 + q, 16, stride=16), :]
        if q < 8:
            first = table[288 + 8 * q : 296 + 8 * q, :]
            second = table[352 + 8 * q : 360 + 8 * q, :]
        else:
            first = table[pl.ds(344 + q, 8, stride=8), :]
            second = table[352 + 8 * q : 360 + 8 * q, :]
        column = jnp.concatenate([top, first, second], axis=0)
        system.append(jnp.where(row32 == 16 + q, column + 1.0, column))
    rhs = table[480:512, :]
    scale = jnp.zeros((COLS, 128), F32)
    for k in range(COLS):
        column = system[k]
        inverse = 1.0 / column[k : k + 1, :]
        scale = jnp.where(row32 == k, inverse, scale)
        ratio = jnp.where(row32 == k, 0.0, column * inverse)
        touched = [j for j in range(k + 1, COLS) if j >= SPL or j == k + 1]
        for j in touched:
            system[j] = system[j] - ratio * column[j : j + 1, :]
        rhs = rhs - ratio * rhs[k : k + 1, :]
    answer = rhs * scale
    flat = jnp.concatenate([answer, jnp.zeros((96, 128), F32)], axis=0).T
    line = jnp.concatenate([flat[g : g + 1, :COLS] for g in range(12)], axis=1)
    out_ref[...] = jnp.broadcast_to(line[None], out_ref.shape)


def solve(parts):
    return pl.pallas_call(
        solve_kernel,
        grid=(1,),
        in_specs=[full((32, 48, 128))],
        out_specs=full((32, 1, 384)),
        out_shape=jax.ShapeDtypeStruct((32, 1, 384), F32),
        scratch_shapes=[pltpu.VMEM((512, 128), F32)],
        compiler_params=params(),
        name="solve",
    )(parts)


def update_kernel(
    live_ref, steps_ref, pred_ref, counts_ref, design_ref, load_ref,
    expected_ref, out_ref, beta_ref, left,
):
    step = pl.program_id(0)

    @pl.when(step == 0)
    def _():
        steps = steps_ref[...]
        beta = jnp.concatenate([steps[:, COLS * g : COLS * (g + 1)] for g in range(12)], axis=0)
        b1, b2, b3 = split3(beta)
        left[...] = jnp.concatenate([b1, b1, b2, b2, b1, b3], axis=1)
        beta_ref[...] = beta.T

    at = step * CHUNK
    d1, d2, d3 = design_ref[0:32, :], design_ref[32:64, :], design_ref[64:96, :]
    change = dot(left[...], jnp.concatenate([d1, d2, d1, d2, d3, d1], axis=0), NN)
    expected = jnp.exp(pred_ref[...] + change)
    expected_ref[...] = expected
    slot = lax.broadcasted_iota(jnp.int32, (1, CHUNK), 1) + at
    mask = (slot < live_ref[0]).astype(F32)
    w1, w2 = split2(expected * mask)
    r1, r2 = split2((counts_ref[...].astype(F32) - expected) * mask)
    load = load_ref[...]
    wide = load.astype(F32)
    l1, l2 = split2(wide * wide)
    grad = dot(load, r1, NN) + dot(load, r2, NN)
    curv = dot(l1, w1, NN) + dot(l2, w1, NN) + dot(l1, w2, NN)
    for i in range(CHUNK // 128):
        out_ref[i, :FACT, :] = grad[:, 128 * i : 128 * (i + 1)]
        out_ref[i, FACT:, :] = curv[:, 128 * i : 128 * (i + 1)]


def update(live, steps, pred, counts, design, load):
    genes, cells = counts.shape
    return pl.pallas_call(
        update_kernel,
        grid=(cells // CHUNK,),
        in_specs=[
            smem(), full((32, 384)), lanes(genes), lanes(genes), lanes(96), full((FACT, genes)),
        ],
        out_specs=[
            lanes(genes),
            pl.BlockSpec((CHUNK // 128, 2 * FACT, 128), lambda c: (c, 0, 0)),
            full((COLS, genes)),
        ],
        out_shape=[
            jax.ShapeDtypeStruct((genes, cells), F32),
            jax.ShapeDtypeStruct((cells // 128, 2 * FACT, 128), F32),
            jax.ShapeDtypeStruct((COLS, genes), F32),
        ],
        scratch_shapes=[pltpu.VMEM((genes, 6 * COLS), BF16)],
        compiler_params=params(),
        name="update",
    )(live, steps, pred, counts, design, load)


def loading_kernel(live_ref, expected_ref, counts_ref, fact_ref, out_ref):
    step = pl.program_id(0)
    expected = expected_ref[...]
    slot = lax.broadcasted_iota(jnp.int32, (1, CHUNK), 1) + step * CHUNK
    mask = (slot < live_ref[0]).astype(F32)
    w1, w2 = split2(expected * mask)
    r1, r2 = split2((counts_ref[...].astype(F32) - expected) * mask)
    fact = fact_ref[...]
    wide = fact.astype(F32)
    f1, f2 = split2(wide * wide)
    grad = dot(fact, r1, NT) + dot(fact, r2, NT)
    curv = dot(f1, w1, NT) + dot(f2, w1, NT) + dot(f1, w2, NT)

    @pl.when(step == 0)
    def _():
        out_ref[...] = jnp.zeros_like(out_ref)

    for h in range(2):
        out_ref[h, :32, :] += grad[32 * h : 32 * (h + 1), :]
        out_ref[h, 32:, :] += curv[32 * h : 32 * (h + 1), :]


def loading_sums(live, expected, counts, fact):
    genes, cells = counts.shape
    return pl.pallas_call(
        loading_kernel,
        grid=(cells // CHUNK,),
        in_specs=[smem(), lanes(genes), lanes(genes), lanes(FACT)],
        out_specs=full((2, FACT, genes)),
        out_shape=jax.ShapeDtypeStruct((2, FACT, genes), F32),
        compiler_params=params(),
        name="loading_sums",
    )(live, expected, counts, fact)


def factor_kernel(parts_ref, out_ref):
    total = parts_ref[0]
    for j in range(1, parts_ref.shape[0]):
        total = total + parts_ref[j]
    value = total[:FACT, :] / (total[FACT:, :] + 1.0)
    out_ref[...] = jnp.broadcast_to(value[None], out_ref.shape)


def factor_share(parts):
    peers = parts.shape[0]
    return pl.pallas_call(
        factor_kernel,
        grid=(1,),
        in_specs=[full(parts.shape)],
        out_specs=full((peers, FACT, 128)),
        out_shape=jax.ShapeDtypeStruct((peers, FACT, 128), F32),
        compiler_params=params(),
        name="factor_share",
    )(parts)


def exchange(value, axis):
    return lax.all_to_all(value, axis, split_axis=0, concat_axis=0, tiled=True)


def partners(move):
    def index(x, y, core):
        return (x * 4 + y) * 2 + core

    return [
        (index(x, y, core), index(*move(x, y, core)))
        for x in range(4)
        for y in range(4)
        for core in range(2)
    ]


OTHER_CORE = partners(lambda x, y, c: (x, y, 1 - c))
NEIGHBOURS = (
    partners(lambda x, y, c: (x ^ 1, y, c)),
    partners(lambda x, y, c: (3 - x, y, c)),
    partners(lambda x, y, c: (x, y ^ 1, c)),
    partners(lambda x, y, c: (x, 3 - y, c)),
)


def local(
    counts, batch_id, live_cells, knot_bin, depth_frac, cell_covariates,
    coefficients, batch_effect, factors, loadings,
):
    fact, load = factors.T, loadings.T
    tot = exchange(cell_totals(counts, 8), "gene")
    rest, hi, lo, design = prepare(
        knot_bin[None], depth_frac[None], batch_id[None], cell_covariates,
        coefficients.T, batch_effect.T, load, fact,
    )
    pred, packed = gram_sums(live_cells, tot, rest, counts, hi, lo, design)
    steps = exchange(solve(exchange(packed, "cell")), "cell")
    expected, pieces, beta = update(
        live_cells, steps.reshape(32, 384), pred, counts, design, load
    )
    arrived = exchange(pieces, "gene")

    sums = loading_sums(live_cells, expected, counts, fact)
    first = lax.axis_index("cell") % 2 == 0
    kept = jnp.where(first, sums[0], sums[1])
    given = jnp.where(first, sums[1], sums[0])
    value = kept + lax.ppermute(given, "cell", OTHER_CORE)
    for pairs in NEIGHBOURS:
        value = value + lax.ppermute(value, "cell", pairs)
    mine = value[:32] / jnp.sqrt(value[32:] + 1.0)
    other = lax.ppermute(mine, "cell", OTHER_CORE)
    score = jnp.where(
        first, jnp.concatenate([mine, other]), jnp.concatenate([other, mine])
    )

    gathered = exchange(factor_share(arrived), "gene")
    factor_step = jnp.moveaxis(gathered, 0, 1).reshape(FACT, -1)
    return beta.T, factor_step.T, score.T


def solution(mesh):
    placed = (
        P("gene", "cell"),
        P("cell"),
        P("cell"),
        P("cell"),
        P("cell"),
        P(None, "cell"),
        P("gene", None),
        P("gene", None),
        P("cell", None),
        P("gene", None),
    )
    return jax.shard_map(
        local,
        mesh=mesh,
        in_specs=placed,
        out_specs=(P("gene", None), P("cell", None), P("gene", None)),
        check_vma=False,
    )
```

```python
import functools

import jax
import jax.numpy as jnp
from jax import lax
from jax.experimental import pallas as pl
from jax.experimental.pallas import tpu as pltpu
from jax.sharding import PartitionSpec as P

GENES = 3072
SPL = 16
COLS = 32
FACT = 64
CHUNK = 256
F32 = jnp.float32
BF16 = jnp.bfloat16
NN = (((1,), (0,)), ((), ()))
NT = (((1,), (1,)), ((), ()))
TN = (((0,), (0,)), ((), ()))
MIB = 1024 * 1024


def dot(a, b, dims):
    return lax.dot_general(a, b, dims, preferred_element_type=F32)


def split2(x):
    hi = x.astype(BF16)
    return hi, (x - hi.astype(F32)).astype(BF16)


def split3(x):
    hi = x.astype(BF16)
    rest = x - hi.astype(F32)
    mid = rest.astype(BF16)
    return hi, mid, (rest - mid.astype(F32)).astype(BF16)


def full(shape):
    return pl.BlockSpec(shape, lambda c: (0,) * len(shape))


def lanes(rows, chunk=CHUNK):
    return pl.BlockSpec((rows, chunk), lambda c: (0, c))


def smem():
    return pl.BlockSpec(memory_space=pltpu.SMEM)


def params(mib=60):
    return pltpu.CompilerParams(vmem_limit_bytes=mib * MIB)


def totals_kernel(counts_ref, out_ref, acc):
    step = pl.program_id(0)
    part = jnp.sum(counts_ref[...].astype(F32), axis=0, keepdims=True)

    @pl.when(step == 0)
    def _():
        acc[...] = part

    @pl.when(step > 0)
    def _():
        acc[...] += part

    @pl.when(step == pl.num_programs(0) - 1)
    def _():
        for i in range(8):
            row = acc[:, 128 * i : 128 * (i + 1)]
            out_ref[:, i : i + 1, :] = jnp.broadcast_to(row[None], (out_ref.shape[0], 1, 128))


def cell_totals(counts, peers):
    genes, cells = counts.shape
    return pl.pallas_call(
        totals_kernel,
        grid=(3,),
        in_specs=[pl.BlockSpec((genes // 3, cells), lambda c: (c, 0))],
        out_specs=full((peers, 8, 128)),
        out_shape=jax.ShapeDtypeStruct((peers, 8, 128), F32),
        scratch_shapes=[pltpu.VMEM((1, cells), F32)],
        compiler_params=params(),
        name="cell_totals",
    )(counts)


def prepare_kernel(
    knot_ref, frac_ref, batch_ref, cov_ref, coef_ref, shift_ref, load_ref, fact_ref,
    rest_ref, hi_ref, lo_ref, design_ref, left,
):
    @pl.when(pl.program_id(0) == 0)
    def _():
        c1, c2, c3 = split3(coef_ref[...])
        b1, b2, b3 = split3(shift_ref[...])
        left[...] = jnp.concatenate([c1, c1, c2, c2, c1, c3, b1, b2, b3, load_ref[...]], axis=0)

    knot, frac = knot_ref[...], frac_ref[...]
    width = knot.shape[1]
    cov = cov_ref[...]
    levels = lax.broadcasted_iota(jnp.int32, (SPL, width), 0)
    here, above = levels == knot, levels == knot + 1
    rest = 1.0 - frac
    hat = jnp.where(here, rest, 0.0) + jnp.where(above, frac, 0.0)
    d1, d2, d3 = split3(jnp.concatenate([hat, cov], axis=0))
    design_ref[...] = jnp.concatenate([d1, d2, d3], axis=0)
    batches = lax.broadcasted_iota(jnp.int32, (64, width), 0)
    onehot = (batches == batch_ref[...]).astype(F32).astype(BF16)
    right = jnp.concatenate(
        [d1, d2, d1, d2, d3, d1, onehot, onehot, onehot, fact_ref[...]], axis=0
    )
    rest_ref[...] = dot(left[...], right, TN)

    def put(at, value):
        hi, lo = split2(value)
        hi_ref[at : at + value.shape[0], :] = hi
        lo_ref[at : at + value.shape[0], :] = lo

    put(0, jnp.where(here, rest * rest, 0.0) + jnp.where(above, frac * frac, 0.0))
    put(16, jnp.where(here, rest * frac, 0.0))
    for p in range(SPL):
        put(32 + 16 * p, hat[p : p + 1, :] * cov)
    low, high = cov[:8], cov[8:]
    for i in range(0, 8, 2):
        put(288 + 8 * i, jnp.concatenate([low[i : i + 1] * low, low[i + 1 : i + 2] * low], axis=0))
        put(352 + 8 * i, jnp.concatenate([low[i : i + 1] * high, low[i + 1 : i + 2] * high], axis=0))
        put(416 + 8 * i, jnp.concatenate([high[i : i + 1] * high, high[i + 1 : i + 2] * high], axis=0))
    put(480, jnp.zeros((32, width), F32))


def prepare(knot, frac, batch, cov, coef, shift, load, fact):
    cells = knot.shape[1]
    genes = coef.shape[1]
    return pl.pallas_call(
        prepare_kernel,
        grid=(cells // CHUNK,),
        in_specs=[
            lanes(1), lanes(1), lanes(1), lanes(16),
            full((COLS, genes)), full((64, genes)), full((FACT, genes)), lanes(FACT),
        ],
        out_specs=[lanes(genes), lanes(512), lanes(512), lanes(96)],
        out_shape=[
            jax.ShapeDtypeStruct((genes, cells), F32),
            jax.ShapeDtypeStruct((512, cells), BF16),
            jax.ShapeDtypeStruct((512, cells), BF16),
            jax.ShapeDtypeStruct((96, cells), BF16),
        ],
        scratch_shapes=[pltpu.VMEM((448, genes), BF16)],
        compiler_params=params(),
        name="prepare",
    )(knot, frac, batch, cov, coef, shift, load, fact)


def gram_kernel(
    live_ref, core_ref, tot_ref, rest_ref, counts_ref, hi_ref, lo_ref, design_ref,
    pred_ref, kept_ref, given_ref, offset, acc,
):
    step = pl.program_id(0)

    @pl.when(step == 0)
    def _():
        total = jnp.sum(tot_ref[...], axis=0)
        value = jnp.log((1.0 + total) / GENES)
        for i in range(8):
            offset[:, 128 * i : 128 * (i + 1)] = value[i : i + 1, :]

    at = pl.multiple_of(step * CHUNK, CHUNK)
    pred = rest_ref[...] + offset[:, pl.ds(at, CHUNK)]
    pred_ref[...] = pred
    expected = jnp.exp(pred)
    slot = lax.broadcasted_iota(jnp.int32, (1, CHUNK), 1) + at
    mask = (slot < live_ref[0]).astype(F32)
    weight = expected * mask
    residual = (counts_ref[...].astype(F32) - expected) * mask
    w1, w2 = split2(weight)
    r1, r2 = split2(residual)
    hi, lo = hi_ref[...], lo_ref[...]
    gram = dot(w1, hi, NT) + dot(w1, lo, NT) + dot(w2, hi, NT)
    blank = jnp.zeros((96, CHUNK), BF16)
    s1 = jnp.concatenate([blank, design_ref[:COLS, :]], axis=0)
    s2 = jnp.concatenate([blank, design_ref[COLS : 2 * COLS, :]], axis=0)
    score = dot(r1, s1, NT) + dot(r1, s2, NT) + dot(r2, s1, NT)

    @pl.when(step == 0)
    def _():
        acc[...] = jnp.zeros_like(acc)

    for t in range(4):
        part = gram[:, 128 * t : 128 * (t + 1)]
        acc[t] += part + score if t == 3 else part

    @pl.when(step == pl.num_programs(0) - 1)
    def _():
        core = core_ref[0]
        for chip in range(16):
            for ref, j in ((kept_ref, 2 * chip + core), (given_ref, 2 * chip + 1 - core)):
                for t in range(4):
                    ref[chip, 12 * t : 12 * (t + 1), :] = acc[t, pl.ds(j, 12, stride=32), :]


def gram_sums(live, core, tot, rest, counts, hi, lo, design):
    genes, cells = counts.shape
    return pl.pallas_call(
        gram_kernel,
        grid=(cells // CHUNK,),
        in_specs=[
            smem(), smem(), full(tot.shape), lanes(genes), lanes(genes),
            lanes(512), lanes(512), lanes(96),
        ],
        out_specs=[lanes(genes), full((16, 48, 128)), full((16, 48, 128))],
        out_shape=[
            jax.ShapeDtypeStruct((genes, cells), F32),
            jax.ShapeDtypeStruct((16, 48, 128), F32),
            jax.ShapeDtypeStruct((16, 48, 128), F32),
        ],
        scratch_shapes=[pltpu.VMEM((1, cells), F32), pltpu.VMEM((4, genes, 128), F32)],
        compiler_params=params(50),
        name="gram_sums",
    )(live, core, tot, rest, counts, hi, lo, design)


def solve_kernel(parts_ref, out_ref, table):
    total = parts_ref[0]
    for j in range(1, parts_ref.shape[0]):
        total = total + parts_ref[j]
    turned = jnp.concatenate([total, jnp.zeros((80, 128), F32)], axis=0).T
    for t in range(4):
        moved = turned if t == 0 else pltpu.roll(turned, 128 - 12 * t, axis=1)
        table[128 * t : 128 * (t + 1), :] = moved
    row16 = lax.broadcasted_iota(jnp.int32, (SPL, 128), 0)
    row32 = lax.broadcasted_iota(jnp.int32, (COLS, 128), 0)
    diag, near = table[0:16, :] + 1.0, table[16:32, :]
    below = pltpu.roll(near, 1, axis=0)
    system = []
    for j in range(SPL):
        top = jnp.where(row16 == j, diag, 0.0)
        top = jnp.where(row16 == j - 1, near, top)
        top = jnp.where(row16 == j + 1, below, top)
        system.append(jnp.concatenate([top, table[32 + 16 * j : 48 + 16 * j, :]], axis=0))
    for q in range(SPL):
        top = table[pl.ds(32 + q, 16, stride=16), :]
        if q < 8:
            first = table[288 + 8 * q : 296 + 8 * q, :]
            second = table[352 + 8 * q : 360 + 8 * q, :]
        else:
            first = table[pl.ds(344 + q, 8, stride=8), :]
            second = table[352 + 8 * q : 360 + 8 * q, :]
        column = jnp.concatenate([top, first, second], axis=0)
        system.append(jnp.where(row32 == 16 + q, column + 1.0, column))
    rhs = table[480:512, :]
    scale = jnp.zeros((COLS, 128), F32)
    for k in range(COLS):
        column = system[k]
        inverse = 1.0 / column[k : k + 1, :]
        scale = jnp.where(row32 == k, inverse, scale)
        ratio = jnp.where(row32 == k, 0.0, column * inverse)
        touched = [j for j in range(k + 1, COLS) if j >= SPL or j == k + 1]
        for j in touched:
            system[j] = system[j] - ratio * column[j : j + 1, :]
        rhs = rhs - ratio * rhs[k : k + 1, :]
    answer = rhs * scale
    flat = jnp.concatenate([answer, jnp.zeros((96, 128), F32)], axis=0).T
    line = jnp.concatenate([flat[g : g + 1, :COLS] for g in range(12)], axis=1)
    out_ref[...] = jnp.broadcast_to(line[None], out_ref.shape)


def solve(parts):
    return pl.pallas_call(
        solve_kernel,
        grid=(1,),
        in_specs=[full(parts.shape)],
        out_specs=full((32, 1, 384)),
        out_shape=jax.ShapeDtypeStruct((32, 1, 384), F32),
        scratch_shapes=[pltpu.VMEM((512, 128), F32)],
        compiler_params=params(16),
        name="solve",
    )(parts)


def update_kernel(
    live_ref, steps_ref, pred_ref, counts_ref, design_ref, load_ref, fact_ref,
    out_ref, sums_ref, beta_ref, left,
):
    step = pl.program_id(0)

    @pl.when(step == 0)
    def _():
        steps = steps_ref[...]
        beta = jnp.concatenate([steps[:, COLS * g : COLS * (g + 1)] for g in range(12)], axis=0)
        b1, b2, b3 = split3(beta)
        left[...] = jnp.concatenate([b1, b1, b2, b2, b1, b3], axis=1)
        beta_ref[...] = beta.T
        sums_ref[...] = jnp.zeros_like(sums_ref)

    at = step * CHUNK
    d1, d2, d3 = design_ref[0:32, :], design_ref[32:64, :], design_ref[64:96, :]
    change = dot(left[...], jnp.concatenate([d1, d2, d1, d2, d3, d1], axis=0), NN)
    expected = jnp.exp(pred_ref[...] + change)
    slot = lax.broadcasted_iota(jnp.int32, (1, CHUNK), 1) + at
    mask = (slot < live_ref[0]).astype(F32)
    w1, w2 = split2(expected * mask)
    r1, r2 = split2((counts_ref[...].astype(F32) - expected) * mask)
    load = load_ref[...]
    wide = load.astype(F32)
    l1, l2 = split2(wide * wide)
    grad = dot(load, r1, NN) + dot(load, r2, NN)
    curv = dot(l1, w1, NN) + dot(l2, w1, NN) + dot(l1, w2, NN)
    for i in range(CHUNK // 128):
        out_ref[i, :FACT, :] = grad[:, 128 * i : 128 * (i + 1)]
        out_ref[i, FACT:, :] = curv[:, 128 * i : 128 * (i + 1)]
    fact = fact_ref[...]
    wide = fact.astype(F32)
    f1, f2 = split2(wide * wide)
    grad = dot(fact, r1, NT) + dot(fact, r2, NT)
    curv = dot(f1, w1, NT) + dot(f2, w1, NT) + dot(f1, w2, NT)
    for h in range(2):
        sums_ref[h, :32, :] += grad[32 * h : 32 * (h + 1), :]
        sums_ref[h, 32:, :] += curv[32 * h : 32 * (h + 1), :]


def update(live, steps, pred, counts, design, load, fact):
    genes, cells = counts.shape
    return pl.pallas_call(
        update_kernel,
        grid=(cells // CHUNK,),
        in_specs=[
            smem(), full((32, 384)), lanes(genes), lanes(genes), lanes(96),
            full((FACT, genes)), lanes(FACT),
        ],
        out_specs=[
            pl.BlockSpec((CHUNK // 128, 2 * FACT, 128), lambda c: (c, 0, 0)),
            full((2, FACT, genes)),
            full((COLS, genes)),
        ],
        out_shape=[
            jax.ShapeDtypeStruct((cells // 128, 2 * FACT, 128), F32),
            jax.ShapeDtypeStruct((2, FACT, genes), F32),
            jax.ShapeDtypeStruct((COLS, genes), F32),
        ],
        scratch_shapes=[pltpu.VMEM((genes, 6 * COLS), BF16)],
        compiler_params=params(),
        name="update",
    )(live, steps, pred, counts, design, load, fact)


def factor_kernel(parts_ref, out_ref):
    total = parts_ref[0]
    for j in range(1, parts_ref.shape[0]):
        total = total + parts_ref[j]
    value = total[:FACT, :] / (total[FACT:, :] + 1.0)
    out_ref[...] = jnp.broadcast_to(value[None], out_ref.shape)


def factor_share(parts):
    peers = parts.shape[0]
    return pl.pallas_call(
        factor_kernel,
        grid=(1,),
        in_specs=[full(parts.shape)],
        out_specs=full((peers, FACT, 128)),
        out_shape=jax.ShapeDtypeStruct((peers, FACT, 128), F32),
        compiler_params=params(16),
        name="factor_share",
    )(parts)


def exchange(value, axis, groups=None):
    return lax.all_to_all(
        value, axis, split_axis=0, concat_axis=0, tiled=True, axis_index_groups=groups
    )


def partners(move):
    def index(x, y, core):
        return (x * 4 + y) * 2 + core

    return [
        (index(x, y, core), index(*move(x, y, core)))
        for x in range(4)
        for y in range(4)
        for core in range(2)
    ]


SAME_CORE = [list(range(core, 32, 2)) for core in range(2)]
OTHER_CORE = partners(lambda x, y, c: (x, y, 1 - c))
ALONG_X = [partners(lambda x, y, c, k=k: (x ^ k, y, c)) for k in (1, 2, 3)]
ALONG_Y = [partners(lambda x, y, c, k=k: (x, y ^ k, c)) for k in (1, 2, 3)]


def local(
    counts, batch_id, live_cells, knot_bin, depth_frac, cell_covariates,
    coefficients, batch_effect, factors, loadings,
):
    fact, load = factors.T, loadings.T
    tot = exchange(cell_totals(counts, 8), "gene")
    rest, hi, lo, design = prepare(
        knot_bin[None], depth_frac[None], batch_id[None], cell_covariates,
        coefficients.T, batch_effect.T, load, fact,
    )
    core = lax.axis_index("cell") % 2
    first = core == 0
    pred, kept, given = gram_sums(
        live_cells, core[None], tot, rest, counts, hi, lo, design
    )
    packed = kept + lax.ppermute(given, "cell", OTHER_CORE)
    steps = exchange(solve(exchange(packed, "cell", SAME_CORE)), "cell")
    pieces, sums, beta = update(
        live_cells, steps.reshape(32, 384), pred, counts, design, load, fact
    )
    arrived = exchange(pieces, "gene")

    kept = jnp.where(first, sums[0], sums[1])
    given = jnp.where(first, sums[1], sums[0])
    value = kept + lax.ppermute(given, "cell", OTHER_CORE)
    for near, across, beside in (ALONG_X, ALONG_Y):
        value = (value + lax.ppermute(value, "cell", near)) + (
            lax.ppermute(value, "cell", across) + lax.ppermute(value, "cell", beside)
        )
    gathered = exchange(factor_share(arrived), "gene")
    mine = value[:32] / jnp.sqrt(value[32:] + 1.0)
    other = lax.ppermute(mine, "cell", OTHER_CORE)
    score = jnp.where(
        first, jnp.concatenate([mine, other]), jnp.concatenate([other, mine])
    )
    factor_step = jnp.moveaxis(gathered, 0, 1).reshape(FACT, -1)
    return beta.T, factor_step.T, score.T


def solution(mesh):
    placed = (
        P("gene", "cell"),
        P("cell"),
        P("cell"),
        P("cell"),
        P("cell"),
        P(None, "cell"),
        P("gene", None),
        P("gene", None),
        P("cell", None),
        P("gene", None),
    )
    return jax.shard_map(
        local,
        mesh=mesh,
        in_specs=placed,
        out_specs=(P("gene", None), P("cell", None), P("gene", None)),
        check_vma=False,
    )
```

```python
import functools

import jax
import jax.numpy as jnp
from jax import lax
from jax.experimental import pallas as pl
from jax.experimental.pallas import tpu as pltpu
from jax.sharding import PartitionSpec as P

GENES = 3072
SPL = 16
COLS = 32
FACT = 64
CHUNK = 256
F32 = jnp.float32
BF16 = jnp.bfloat16
NN = (((1,), (0,)), ((), ()))
NT = (((1,), (1,)), ((), ()))
TN = (((0,), (0,)), ((), ()))
MIB = 1024 * 1024


def dot(a, b, dims):
    return lax.dot_general(a, b, dims, preferred_element_type=F32)


def split2(x):
    hi = x.astype(BF16)
    return hi, (x - hi.astype(F32)).astype(BF16)


def split3(x):
    hi = x.astype(BF16)
    rest = x - hi.astype(F32)
    mid = rest.astype(BF16)
    return hi, mid, (rest - mid.astype(F32)).astype(BF16)


def full(shape):
    return pl.BlockSpec(shape, lambda c: (0,) * len(shape))


def lanes(rows, chunk=CHUNK):
    return pl.BlockSpec((rows, chunk), lambda c: (0, c))


def smem():
    return pl.BlockSpec(memory_space=pltpu.SMEM)


def params(mib=16):
    return pltpu.CompilerParams(vmem_limit_bytes=mib * MIB)


def totals_kernel(counts_ref, out_ref, rows, arrived):
    blocks = rows.shape[0]
    size = rows.shape[1]

    def copy(b):
        return pltpu.make_async_copy(
            counts_ref.at[pl.ds(b * size, size), :], rows.at[b], arrived.at[b]
        )

    for b in range(blocks):
        copy(b).start()
    total = jnp.zeros((8, rows.shape[2]), F32)
    for b in range(blocks):
        copy(b).wait()
        for i in range(0, size, 8):
            total = total + rows[b, i : i + 8, :].astype(F32)
    total = jnp.sum(total, axis=0, keepdims=True)
    for i in range(8):
        row = total[:, 128 * i : 128 * (i + 1)]
        out_ref[:, i : i + 1, :] = jnp.broadcast_to(row[None], (out_ref.shape[0], 1, 128))


def cell_totals(counts, peers):
    genes, cells = counts.shape
    blocks = 8
    return pl.pallas_call(
        totals_kernel,
        grid=(1,),
        in_specs=[pl.BlockSpec(memory_space=pl.ANY)],
        out_specs=full((peers, 8, 128)),
        out_shape=jax.ShapeDtypeStruct((peers, 8, 128), F32),
        scratch_shapes=[
            pltpu.VMEM((blocks, genes // blocks, cells), jnp.int32),
            pltpu.SemaphoreType.DMA((blocks,)),
        ],
        compiler_params=params(60),
        name="cell_totals",
    )(counts)


def prepare_kernel(
    knot_ref, frac_ref, batch_ref, cov_ref, coef_ref, shift_ref, load_ref, fact_ref,
    rest_ref, design_ref, left,
):
    @pl.when(pl.program_id(0) == 0)
    def _():
        c1, c2, c3 = split3(coef_ref[...])
        b1, b2, b3 = split3(shift_ref[...])
        left[...] = jnp.concatenate([c1, c1, c2, c2, c1, c3, b1, b2, b3, load_ref[...]], axis=0)

    knot, frac = knot_ref[...], frac_ref[...]
    width = knot.shape[1]
    cov = cov_ref[...]
    levels = lax.broadcasted_iota(jnp.int32, (SPL, width), 0)
    here, above = levels == knot, levels == knot + 1
    rest = 1.0 - frac
    hat = jnp.where(here, rest, 0.0) + jnp.where(above, frac, 0.0)
    d1, d2, d3 = split3(jnp.concatenate([hat, cov], axis=0))
    design_ref[...] = jnp.concatenate([d1, d2, d3], axis=0)
    batches = lax.broadcasted_iota(jnp.int32, (64, width), 0)
    onehot = (batches == batch_ref[...]).astype(F32).astype(BF16)
    right = jnp.concatenate(
        [d1, d2, d1, d2, d3, d1, onehot, onehot, onehot, fact_ref[...]], axis=0
    )
    rest_ref[...] = dot(left[...], right, TN)


def prepare(knot, frac, batch, cov, coef, shift, load, fact):
    cells = knot.shape[1]
    genes = coef.shape[1]
    return pl.pallas_call(
        prepare_kernel,
        grid=(cells // CHUNK,),
        in_specs=[
            lanes(1), lanes(1), lanes(1), lanes(16),
            full((COLS, genes)), full((64, genes)), full((FACT, genes)), lanes(FACT),
        ],
        out_specs=[lanes(genes), lanes(96)],
        out_shape=[
            jax.ShapeDtypeStruct((genes, cells), F32),
            jax.ShapeDtypeStruct((96, cells), BF16),
        ],
        scratch_shapes=[pltpu.VMEM((448, genes), BF16)],
        compiler_params=params(),
        name="prepare",
    )(knot, frac, batch, cov, coef, shift, load, fact)


def gram_kernel(
    live_ref, core_ref, tot_ref, rest_ref, counts_ref, design_ref,
    pred_ref, kept_ref, given_ref, offset, acc, hi_ref, lo_ref,
):
    step = pl.program_id(0)

    @pl.when(step == 0)
    def _():
        total = jnp.sum(tot_ref[...], axis=0)
        value = jnp.log((1.0 + total) / GENES)
        for i in range(8):
            offset[:, 128 * i : 128 * (i + 1)] = value[i : i + 1, :]

    at = pl.multiple_of(step * CHUNK, CHUNK)
    pred = rest_ref[...] + offset[:, pl.ds(at, CHUNK)]
    pred_ref[...] = pred
    expected = jnp.exp(pred)
    slot = lax.broadcasted_iota(jnp.int32, (1, CHUNK), 1) + at
    mask = (slot < live_ref[0]).astype(F32)
    weight = expected * mask
    residual = (counts_ref[...].astype(F32) - expected) * mask
    w1, w2 = split2(weight)
    r1, r2 = split2(residual)

    def put(at, value):
        hi, lo = split2(value)
        hi_ref[at : at + value.shape[0], :] = hi
        lo_ref[at : at + value.shape[0], :] = lo

    d1, d2, d3 = design_ref[0:32, :], design_ref[32:64, :], design_ref[64:96, :]
    design = (d1.astype(F32) + d2.astype(F32)) + d3.astype(F32)
    hat, cov = design[:SPL], design[SPL:]
    put(0, hat * hat)
    put(16, hat * pltpu.roll(hat, SPL - 1, axis=0))
    for p in range(SPL):
        put(32 + 16 * p, hat[p : p + 1, :] * cov)
    low, high = cov[:8], cov[8:]
    for i in range(0, 8, 2):
        put(288 + 8 * i, jnp.concatenate([low[i : i + 1] * low, low[i + 1 : i + 2] * low], axis=0))
        put(352 + 8 * i, jnp.concatenate([low[i : i + 1] * high, low[i + 1 : i + 2] * high], axis=0))
        put(416 + 8 * i, jnp.concatenate([high[i : i + 1] * high, high[i + 1 : i + 2] * high], axis=0))
    put(480, jnp.zeros((32, CHUNK), F32))
    hi, lo = hi_ref[...], lo_ref[...]
    gram = dot(w1, hi, NT) + dot(w1, lo, NT) + dot(w2, hi, NT)
    blank = jnp.zeros((96, CHUNK), BF16)
    s1 = jnp.concatenate([blank, d1], axis=0)
    s2 = jnp.concatenate([blank, d2], axis=0)
    score = dot(r1, s1, NT) + dot(r1, s2, NT) + dot(r2, s1, NT)

    @pl.when(step == 0)
    def _():
        acc[...] = jnp.zeros_like(acc)

    for t in range(4):
        part = gram[:, 128 * t : 128 * (t + 1)]
        acc[t] += part + score if t == 3 else part

    @pl.when(step == pl.num_programs(0) - 1)
    def _():
        core = core_ref[0]
        for chip in range(16):
            for ref, j in ((kept_ref, 2 * chip + core), (given_ref, 2 * chip + 1 - core)):
                for t in range(4):
                    ref[chip, 12 * t : 12 * (t + 1), :] = acc[t, pl.ds(j, 12, stride=32), :]


def gram_sums(live, core, tot, rest, counts, design):
    genes, cells = counts.shape
    return pl.pallas_call(
        gram_kernel,
        grid=(cells // CHUNK,),
        in_specs=[
            smem(), smem(), full(tot.shape), lanes(genes), lanes(genes), lanes(96),
        ],
        out_specs=[lanes(genes), full((16, 48, 128)), full((16, 48, 128))],
        out_shape=[
            jax.ShapeDtypeStruct((genes, cells), F32),
            jax.ShapeDtypeStruct((16, 48, 128), F32),
            jax.ShapeDtypeStruct((16, 48, 128), F32),
        ],
        scratch_shapes=[
            pltpu.VMEM((1, cells), F32), pltpu.VMEM((4, genes, 128), F32),
            pltpu.VMEM((512, CHUNK), BF16), pltpu.VMEM((512, CHUNK), BF16),
        ],
        compiler_params=params(),
        name="gram_sums",
    )(live, core, tot, rest, counts, design)


def solve_kernel(parts_ref, out_ref, table):
    total = parts_ref[0]
    for j in range(1, parts_ref.shape[0]):
        total = total + parts_ref[j]
    turned = jnp.concatenate([total, jnp.zeros((80, 128), F32)], axis=0).T
    for t in range(4):
        moved = turned if t == 0 else pltpu.roll(turned, 128 - 12 * t, axis=1)
        table[128 * t : 128 * (t + 1), :] = moved
    row16 = lax.broadcasted_iota(jnp.int32, (SPL, 128), 0)
    row32 = lax.broadcasted_iota(jnp.int32, (COLS, 128), 0)
    diag, near = table[0:16, :] + 1.0, table[16:32, :]
    below = pltpu.roll(near, 1, axis=0)
    system = []
    for j in range(SPL):
        top = jnp.where(row16 == j, diag, 0.0)
        top = jnp.where(row16 == j - 1, near, top)
        top = jnp.where(row16 == j + 1, below, top)
        system.append(jnp.concatenate([top, table[32 + 16 * j : 48 + 16 * j, :]], axis=0))
    for q in range(SPL):
        top = table[pl.ds(32 + q, 16, stride=16), :]
        if q < 8:
            first = table[288 + 8 * q : 296 + 8 * q, :]
            second = table[352 + 8 * q : 360 + 8 * q, :]
        else:
            first = table[pl.ds(344 + q, 8, stride=8), :]
            second = table[352 + 8 * q : 360 + 8 * q, :]
        column = jnp.concatenate([top, first, second], axis=0)
        system.append(jnp.where(row32 == 16 + q, column + 1.0, column))
    rhs = table[480:512, :]
    scale = jnp.zeros((COLS, 128), F32)
    for k in range(COLS):
        column = system[k]
        inverse = 1.0 / column[k : k + 1, :]
        scale = jnp.where(row32 == k, inverse, scale)
        ratio = jnp.where(row32 == k, 0.0, column * inverse)
        touched = [j for j in range(k + 1, COLS) if j >= SPL or j == k + 1]
        for j in touched:
            system[j] = system[j] - ratio * column[j : j + 1, :]
        rhs = rhs - ratio * rhs[k : k + 1, :]
    answer = rhs * scale
    flat = jnp.concatenate([answer, jnp.zeros((96, 128), F32)], axis=0).T
    line = jnp.concatenate([flat[g : g + 1, :COLS] for g in range(12)], axis=1)
    out_ref[...] = jnp.broadcast_to(line[None], out_ref.shape)


def solve(parts):
    return pl.pallas_call(
        solve_kernel,
        grid=(1,),
        in_specs=[full(parts.shape)],
        out_specs=full((32, 1, 384)),
        out_shape=jax.ShapeDtypeStruct((32, 1, 384), F32),
        scratch_shapes=[pltpu.VMEM((512, 128), F32)],
        compiler_params=params(),
        name="solve",
    )(parts)


def update_kernel(
    live_ref, core_ref, steps_ref, pred_ref, counts_ref, design_ref, load_ref, fact_ref,
    out_ref, kept_ref, given_ref, beta_ref, left, sums,
):
    step = pl.program_id(0)

    @pl.when(step == 0)
    def _():
        steps = steps_ref[...]
        beta = jnp.concatenate([steps[:, COLS * g : COLS * (g + 1)] for g in range(12)], axis=0)
        b1, b2, b3 = split3(beta)
        left[...] = jnp.concatenate([b1, b1, b2, b2, b1, b3], axis=1)
        beta_ref[...] = beta.T
        sums[...] = jnp.zeros_like(sums)

    at = step * CHUNK
    d1, d2, d3 = design_ref[0:32, :], design_ref[32:64, :], design_ref[64:96, :]
    change = dot(left[...], jnp.concatenate([d1, d2, d1, d2, d3, d1], axis=0), NN)
    expected = jnp.exp(pred_ref[...] + change)
    slot = lax.broadcasted_iota(jnp.int32, (1, CHUNK), 1) + at
    mask = (slot < live_ref[0]).astype(F32)
    w1, w2 = split2(expected * mask)
    r1, r2 = split2((counts_ref[...].astype(F32) - expected) * mask)
    load = load_ref[...]
    wide = load.astype(F32)
    l1, l2 = split2(wide * wide)
    grad = dot(load, r1, NN) + dot(load, r2, NN)
    curv = dot(l1, w1, NN) + dot(l2, w1, NN) + dot(l1, w2, NN)
    for i in range(CHUNK // 128):
        out_ref[i, :FACT, :] = grad[:, 128 * i : 128 * (i + 1)]
        out_ref[i, FACT:, :] = curv[:, 128 * i : 128 * (i + 1)]
    fact = fact_ref[...]
    wide = fact.astype(F32)
    f1, f2 = split2(wide * wide)
    grad = dot(fact, r1, NT) + dot(fact, r2, NT)
    curv = dot(f1, w1, NT) + dot(f2, w1, NT) + dot(f1, w2, NT)
    for h in range(2):
        sums[h, :32, :] += grad[32 * h : 32 * (h + 1), :]
        sums[h, 32:, :] += curv[32 * h : 32 * (h + 1), :]

    @pl.when(step == pl.num_programs(0) - 1)
    def _():
        kept_ref[...] = sums[core_ref[0]]
        given_ref[...] = sums[1 - core_ref[0]]


def update(live, core, steps, pred, counts, design, load, fact):
    genes, cells = counts.shape
    return pl.pallas_call(
        update_kernel,
        grid=(cells // CHUNK,),
        in_specs=[
            smem(), smem(), full((32, 384)), lanes(genes), lanes(genes), lanes(96),
            full((FACT, genes)), lanes(FACT),
        ],
        out_specs=[
            pl.BlockSpec((CHUNK // 128, 2 * FACT, 128), lambda c: (c, 0, 0)),
            full((FACT, genes)),
            full((FACT, genes)),
            full((COLS, genes)),
        ],
        out_shape=[
            pltpu.HBM((cells // 128, 2 * FACT, 128), F32),
            jax.ShapeDtypeStruct((FACT, genes), F32),
            jax.ShapeDtypeStruct((FACT, genes), F32),
            jax.ShapeDtypeStruct((COLS, genes), F32),
        ],
        scratch_shapes=[pltpu.VMEM((genes, 6 * COLS), BF16), pltpu.VMEM((2, FACT, genes), F32)],
        compiler_params=params(),
        name="update",
    )(live, core, steps, pred, counts, design, load, fact)


def score_kernel(core_ref, mine_ref, other_ref, out_ref):
    core = core_ref[0]
    for half, ref in ((core, mine_ref), (1 - core, other_ref)):
        out_ref[pl.ds(pl.multiple_of(32 * half, 32), 32), :] = ref[...]


def joined_score(core, mine, other):
    return pl.pallas_call(
        score_kernel,
        grid=(1,),
        in_specs=[smem(), full(mine.shape), full(mine.shape)],
        out_specs=full((FACT, mine.shape[1])),
        out_shape=jax.ShapeDtypeStruct((FACT, mine.shape[1]), F32),
        compiler_params=params(),
        name="joined_score",
    )(core, mine, other)


def factor_kernel(parts_ref, out_ref):
    total = parts_ref[0]
    for j in range(1, parts_ref.shape[0]):
        total = total + parts_ref[j]
    value = total[:FACT, :] / (total[FACT:, :] + 1.0)
    out_ref[...] = jnp.broadcast_to(value[None], out_ref.shape)


def factor_share(parts):
    peers = parts.shape[0]
    return pl.pallas_call(
        factor_kernel,
        grid=(1,),
        in_specs=[full(parts.shape)],
        out_specs=full((peers, FACT, 128)),
        out_shape=jax.ShapeDtypeStruct((peers, FACT, 128), F32),
        compiler_params=params(),
        name="factor_share",
    )(parts)


def exchange(value, axis, groups=None):
    return lax.all_to_all(
        value, axis, split_axis=0, concat_axis=0, tiled=True, axis_index_groups=groups
    )


def partners(move):
    def index(x, y, core):
        return (x * 4 + y) * 2 + core

    return [
        (index(x, y, core), index(*move(x, y, core)))
        for x in range(4)
        for y in range(4)
        for core in range(2)
    ]


SAME_CORE = [list(range(core, 32, 2)) for core in range(2)]
OTHER_CORE = partners(lambda x, y, c: (x, y, 1 - c))
ALONG_X = [partners(lambda x, y, c, k=k: (x ^ k, y, c)) for k in (1, 2, 3)]
ALONG_Y = [partners(lambda x, y, c, k=k: (x, y ^ k, c)) for k in (1, 3)]


def local(
    counts, batch_id, live_cells, knot_bin, depth_frac, cell_covariates,
    coefficients, batch_effect, factors, loadings,
):
    fact, load = factors.T, loadings.T
    tot = exchange(cell_totals(counts, 8), "gene")
    rest, design = prepare(
        knot_bin[None], depth_frac[None], batch_id[None], cell_covariates,
        coefficients.T, batch_effect.T, load, fact,
    )
    core = (lax.axis_index("cell") % 2)[None]
    pred, kept, given = gram_sums(
        live_cells, core, tot, rest, counts, design
    )
    packed = kept + lax.ppermute(given, "cell", OTHER_CORE)
    steps = exchange(solve(exchange(packed, "cell", SAME_CORE)), "cell")
    pieces, kept, given, beta = update(
        live_cells, core, steps.reshape(32, 384), pred, counts, design, load, fact
    )
    arrived = exchange(pieces, "gene")

    value = kept + lax.ppermute(given, "cell", OTHER_CORE)
    near, across, beside = (lax.ppermute(value, "cell", pairs) for pairs in ALONG_X)
    value = (value + near) + (across + beside)
    near = lax.ppermute(value, "cell", ALONG_Y[0])
    shared = factor_share(arrived)
    gathered = exchange(shared, "gene")
    near, _ = lax.optimization_barrier((near, shared))
    value = value + near
    value = value + lax.ppermute(value, "cell", ALONG_Y[1])
    mine = value[:32] / jnp.sqrt(value[32:] + 1.0)
    other = lax.ppermute(mine, "cell", OTHER_CORE)
    score = joined_score(core, mine, other)
    factor_step = jnp.moveaxis(gathered, 0, 1).reshape(FACT, -1)
    return beta.T, factor_step.T, score.T


def solution(mesh):
    placed = (
        P("gene", "cell"),
        P("cell"),
        P("cell"),
        P("cell"),
        P("cell"),
        P(None, "cell"),
        P("gene", None),
        P("gene", None),
        P("cell", None),
        P("gene", None),
    )
    return jax.shard_map(
        local,
        mesh=mesh,
        in_specs=placed,
        out_specs=(P("gene", None), P("cell", None), P("gene", None)),
        check_vma=False,
    )
```

```python
import functools

import jax
import jax.numpy as jnp
from jax import lax
from jax.experimental import pallas as pl
from jax.experimental.pallas import tpu as pltpu
from jax.sharding import PartitionSpec as P

GENES = 3072
SPL = 16
COLS = 32
FACT = 64
CHUNK = 256
F32 = jnp.float32
BF16 = jnp.bfloat16
NN = (((1,), (0,)), ((), ()))
NT = (((1,), (1,)), ((), ()))
TN = (((0,), (0,)), ((), ()))
MIB = 1024 * 1024


def dot(a, b, dims):
    return lax.dot_general(a, b, dims, preferred_element_type=F32)


def split2(x):
    hi = x.astype(BF16)
    return hi, (x - hi.astype(F32)).astype(BF16)


def split3(x):
    hi = x.astype(BF16)
    rest = x - hi.astype(F32)
    mid = rest.astype(BF16)
    return hi, mid, (rest - mid.astype(F32)).astype(BF16)


def full(shape):
    return pl.BlockSpec(shape, lambda c: (0,) * len(shape))


def lanes(rows, chunk=CHUNK):
    return pl.BlockSpec((rows, chunk), lambda c: (0, c))


def smem():
    return pl.BlockSpec(memory_space=pltpu.SMEM)


def params(mib=16):
    return pltpu.CompilerParams(vmem_limit_bytes=mib * MIB)


def totals_kernel(counts_ref, out_ref, rows, arrived):
    blocks = rows.shape[0]
    size = rows.shape[1]

    def copy(b):
        return pltpu.make_async_copy(
            counts_ref.at[pl.ds(b * size, size), :], rows.at[b], arrived.at[b]
        )

    for b in range(blocks):
        copy(b).start()
    total = jnp.zeros((8, rows.shape[2]), F32)
    for b in range(blocks):
        copy(b).wait()
        for i in range(0, size, 8):
            total = total + rows[b, i : i + 8, :].astype(F32)
    total = jnp.sum(total, axis=0, keepdims=True)
    for i in range(8):
        row = total[:, 128 * i : 128 * (i + 1)]
        out_ref[:, i : i + 1, :] = jnp.broadcast_to(row[None], (out_ref.shape[0], 1, 128))


def cell_totals(counts, peers):
    genes, cells = counts.shape
    blocks = 8
    return pl.pallas_call(
        totals_kernel,
        grid=(1,),
        in_specs=[pl.BlockSpec(memory_space=pl.ANY)],
        out_specs=full((peers, 8, 128)),
        out_shape=jax.ShapeDtypeStruct((peers, 8, 128), F32),
        scratch_shapes=[
            pltpu.VMEM((blocks, genes // blocks, cells), jnp.int32),
            pltpu.SemaphoreType.DMA((blocks,)),
        ],
        compiler_params=params(60),
        name="cell_totals",
    )(counts)


def prepare_kernel(
    live_ref, counts_ref, knot_hbm, frac_hbm, batch_hbm, cov_hbm, coef_hbm, shift_hbm,
    load_hbm, fact_hbm,
    rest_ref, design_ref, score_ref, by_load_ref, by_fact_ref,
    left, knot_all, frac_all, batch_all, cov_all, coef, shift, load, fact_all, score, arrived,
):
    step = pl.program_id(0)

    @pl.when(step == 0)
    def _():
        pairs = (
            (coef_hbm, coef), (shift_hbm, shift), (load_hbm, load), (fact_hbm, fact_all),
            (knot_hbm, knot_all), (frac_hbm, frac_all), (batch_hbm, batch_all), (cov_hbm, cov_all),
        )
        copies = [
            pltpu.make_async_copy(source, target, arrived.at[i])
            for i, (source, target) in enumerate(pairs)
        ]
        for copy in copies:
            copy.start()
        for copy in copies:
            copy.wait()
        c1, c2, c3 = split3(coef[...])
        b1, b2, b3 = split3(shift[...])
        left[...] = jnp.concatenate([c1, c1, c2, c2, c1, c3, b1, b2, b3, load[...]], axis=0)
        score[...] = jnp.zeros_like(score)
        by_fact_ref[...] = jnp.zeros_like(by_fact_ref)

    at = pl.multiple_of(step * CHUNK, CHUNK)
    here = pl.ds(at, CHUNK)
    knot, frac, cov, fact = knot_all[:, here], frac_all[:, here], cov_all[:, here], fact_all[:, here]
    levels = lax.broadcasted_iota(jnp.int32, (SPL, CHUNK), 0)
    hat = jnp.where(levels == knot, 1.0 - frac, 0.0) + jnp.where(levels == knot + 1, frac, 0.0)
    d1, d2, d3 = split3(jnp.concatenate([hat, cov], axis=0))
    terms = jnp.concatenate([d1, d2, d3], axis=0)
    design_ref[...] = terms
    batches = lax.broadcasted_iota(jnp.int32, (64, CHUNK), 0)
    onehot = (batches == batch_all[:, here]).astype(F32).astype(BF16)
    right = jnp.concatenate([d1, d2, d1, d2, d3, d1, onehot, onehot, onehot, fact], axis=0)
    rest_ref[...] = dot(left[...], right, TN)

    slot = lax.broadcasted_iota(jnp.int32, (1, CHUNK), 1) + at
    mask = (slot < live_ref[0]).astype(F32)
    counts = (counts_ref[...].astype(F32) * mask).astype(BF16)
    by_load_ref[...] = dot(load[...], counts, NN)
    by_fact_ref[...] += dot(fact, counts, NT)
    score[...] += dot(counts, terms, NT)

    @pl.when(step == pl.num_programs(0) - 1)
    def _():
        value = score[:, :32] + score[:, 32:64] + score[:, 64:96]
        blank = jnp.zeros((value.shape[0], 96), F32)
        score_ref[...] = jnp.concatenate([blank, value], axis=1)


def prepare(live, counts, knot, frac, batch, cov, coef, shift, load, fact):
    genes, cells = counts.shape
    small = [
        pltpu.with_memory_space_constraint(a, pltpu.HBM)
        for a in (knot, frac, batch, cov, coef, shift, load, fact)
    ]
    counts = pltpu.with_memory_space_constraint(counts, pltpu.HBM)
    return pl.pallas_call(
        prepare_kernel,
        grid=(cells // CHUNK,),
        in_specs=[smem(), lanes(genes)] + [pl.BlockSpec(memory_space=pltpu.HBM)] * 8,
        out_specs=[
            lanes(genes), lanes(96), full((genes, 128)), lanes(FACT), full((FACT, genes)),
        ],
        out_shape=[
            jax.ShapeDtypeStruct((genes, cells), F32),
            jax.ShapeDtypeStruct((96, cells), BF16),
            jax.ShapeDtypeStruct((genes, 128), F32),
            jax.ShapeDtypeStruct((FACT, cells), F32),
            jax.ShapeDtypeStruct((FACT, genes), F32),
        ],
        scratch_shapes=[pltpu.VMEM((448, genes), BF16)]
        + [pltpu.VMEM(a.shape, a.dtype) for a in small]
        + [pltpu.VMEM((genes, 96), F32), pltpu.SemaphoreType.DMA((8,))],
        compiler_params=params(),
        name="prepare",
    )(live, counts, *small)


def gram_kernel(
    live_ref, core_ref, tot_ref, rest_ref, design_ref, score_ref,
    pred_ref, kept_ref, given_ref, offset, acc, hi_ref, lo_ref,
):
    step = pl.program_id(0)

    @pl.when(step == 0)
    def _():
        total = jnp.sum(tot_ref[...], axis=0)
        value = jnp.log((1.0 + total) / GENES)
        for i in range(8):
            offset[:, 128 * i : 128 * (i + 1)] = value[i : i + 1, :]
        acc[:3] = jnp.zeros_like(acc[:3])
        acc[3] = score_ref[...]

    at = pl.multiple_of(step * CHUNK, CHUNK)
    pred = rest_ref[...] + offset[:, pl.ds(at, CHUNK)]
    pred_ref[...] = pred
    slot = lax.broadcasted_iota(jnp.int32, (1, CHUNK), 1) + at
    mask = (slot < live_ref[0]).astype(F32)
    w1, w2 = split2(jnp.exp(pred) * mask)

    def put(at, value):
        hi, lo = split2(value)
        hi_ref[at : at + value.shape[0], :] = hi
        lo_ref[at : at + value.shape[0], :] = lo

    d1, d2, d3 = design_ref[0:32, :], design_ref[32:64, :], design_ref[64:96, :]
    design = (d1.astype(F32) + d2.astype(F32)) + d3.astype(F32)
    hat, cov = design[:SPL], design[SPL:]
    put(0, hat * hat)
    put(16, hat * pltpu.roll(hat, SPL - 1, axis=0))
    for p in range(SPL):
        put(32 + 16 * p, hat[p : p + 1, :] * cov)
    low, high = cov[:8], cov[8:]
    for i in range(0, 8, 2):
        put(288 + 8 * i, jnp.concatenate([low[i : i + 1] * low, low[i + 1 : i + 2] * low], axis=0))
        put(352 + 8 * i, jnp.concatenate([low[i : i + 1] * high, low[i + 1 : i + 2] * high], axis=0))
        put(416 + 8 * i, jnp.concatenate([high[i : i + 1] * high, high[i + 1 : i + 2] * high], axis=0))
    put(480, -design)
    hi, lo = hi_ref[...], lo_ref[...]
    gram = dot(w1, hi, NT) + dot(w1, lo, NT) + dot(w2, hi, NT)
    for t in range(4):
        acc[t] += gram[:, 128 * t : 128 * (t + 1)]

    @pl.when(step == pl.num_programs(0) - 1)
    def _():
        core = core_ref[0]
        for chip in range(16):
            for ref, j in ((kept_ref, 2 * chip + core), (given_ref, 2 * chip + 1 - core)):
                for t in range(4):
                    ref[chip, 12 * t : 12 * (t + 1), :] = acc[t, pl.ds(j, 12, stride=32), :]


def gram_sums(live, core, tot, rest, design, score):
    genes, cells = rest.shape
    return pl.pallas_call(
        gram_kernel,
        grid=(cells // CHUNK,),
        in_specs=[
            smem(), smem(), full(tot.shape), lanes(genes), lanes(96), full(score.shape),
        ],
        out_specs=[lanes(genes), full((16, 48, 128)), full((16, 48, 128))],
        out_shape=[
            jax.ShapeDtypeStruct((genes, cells), F32),
            jax.ShapeDtypeStruct((16, 48, 128), F32),
            jax.ShapeDtypeStruct((16, 48, 128), F32),
        ],
        scratch_shapes=[
            pltpu.VMEM((1, cells), F32), pltpu.VMEM((4, genes, 128), F32),
            pltpu.VMEM((512, CHUNK), BF16), pltpu.VMEM((512, CHUNK), BF16),
        ],
        compiler_params=params(),
        name="gram_sums",
    )(live, core, tot, rest, design, score)


def solve_kernel(parts_ref, out_ref, table):
    total = parts_ref[0]
    for j in range(1, parts_ref.shape[0]):
        total = total + parts_ref[j]
    turned = jnp.concatenate([total, jnp.zeros((80, 128), F32)], axis=0).T
    for t in range(4):
        moved = turned if t == 0 else pltpu.roll(turned, 128 - 12 * t, axis=1)
        table[128 * t : 128 * (t + 1), :] = moved
    row16 = lax.broadcasted_iota(jnp.int32, (SPL, 128), 0)
    row32 = lax.broadcasted_iota(jnp.int32, (COLS, 128), 0)
    diag, near = table[0:16, :] + 1.0, table[16:32, :]
    below = pltpu.roll(near, 1, axis=0)
    system = []
    for j in range(SPL):
        top = jnp.where(row16 == j, diag, 0.0)
        top = jnp.where(row16 == j - 1, near, top)
        top = jnp.where(row16 == j + 1, below, top)
        system.append(jnp.concatenate([top, table[32 + 16 * j : 48 + 16 * j, :]], axis=0))
    for q in range(SPL):
        top = table[pl.ds(32 + q, 16, stride=16), :]
        if q < 8:
            first = table[288 + 8 * q : 296 + 8 * q, :]
            second = table[352 + 8 * q : 360 + 8 * q, :]
        else:
            first = table[pl.ds(344 + q, 8, stride=8), :]
            second = table[352 + 8 * q : 360 + 8 * q, :]
        column = jnp.concatenate([top, first, second], axis=0)
        system.append(jnp.where(row32 == 16 + q, column + 1.0, column))
    rhs = table[480:512, :]
    scale = jnp.zeros((COLS, 128), F32)
    for k in range(COLS):
        column = system[k]
        inverse = 1.0 / column[k : k + 1, :]
        scale = jnp.where(row32 == k, inverse, scale)
        ratio = jnp.where(row32 == k, 0.0, column * inverse)
        touched = [j for j in range(k + 1, COLS) if j >= SPL or j == k + 1]
        for j in touched:
            system[j] = system[j] - ratio * column[j : j + 1, :]
        rhs = rhs - ratio * rhs[k : k + 1, :]
    answer = rhs * scale
    flat = jnp.concatenate([answer, jnp.zeros((96, 128), F32)], axis=0).T
    line = jnp.concatenate([flat[g : g + 1, :COLS] for g in range(12)], axis=1)
    out_ref[...] = jnp.broadcast_to(line[None], out_ref.shape)


def solve(parts):
    return pl.pallas_call(
        solve_kernel,
        grid=(1,),
        in_specs=[full(parts.shape)],
        out_specs=full((32, 1, 384)),
        out_shape=jax.ShapeDtypeStruct((32, 1, 384), F32),
        scratch_shapes=[pltpu.VMEM((512, 128), F32)],
        compiler_params=params(),
        name="solve",
    )(parts)


def update_kernel(
    live_ref, core_ref, steps_ref, pred_ref, design_ref, load_ref, fact_ref,
    by_load_ref, by_fact_ref,
    out_ref, kept_ref, given_ref, beta_ref, left, loads, sums,
):
    step = pl.program_id(0)

    @pl.when(step == 0)
    def _():
        steps = steps_ref[...]
        beta = jnp.concatenate([steps[:, COLS * g : COLS * (g + 1)] for g in range(12)], axis=0)
        b1, b2, b3 = split3(beta)
        left[...] = jnp.concatenate([b1, b1, b2, b2, b1, b3], axis=1)
        beta_ref[...] = beta.T
        load = load_ref[...]
        wide = load.astype(F32)
        l1, l2 = split2(wide * wide)
        loads[...] = jnp.concatenate([load, l1, l2], axis=0)
        for h in range(2):
            sums[h, :32, :] = by_fact_ref[32 * h : 32 * (h + 1), :]
            sums[h, 32:, :] = jnp.zeros_like(sums[h, 32:, :])

    at = step * CHUNK
    d1, d2, d3 = design_ref[0:32, :], design_ref[32:64, :], design_ref[64:96, :]
    change = dot(left[...], jnp.concatenate([d1, d2, d1, d2, d3, d1], axis=0), NN)
    slot = lax.broadcasted_iota(jnp.int32, (1, CHUNK), 1) + at
    mask = (slot < live_ref[0]).astype(F32)
    w1, w2 = split2(jnp.exp(pred_ref[...] + change) * mask)
    first = dot(loads[...], w1, NN)
    second = dot(loads[: 2 * FACT], w2, NN)
    grad = by_load_ref[...] - (first[:FACT] + second[:FACT])
    curv = (first[FACT : 2 * FACT] + first[2 * FACT :]) + second[FACT:]
    for i in range(CHUNK // 128):
        out_ref[i, :FACT, :] = grad[:, 128 * i : 128 * (i + 1)]
        out_ref[i, FACT:, :] = curv[:, 128 * i : 128 * (i + 1)]
    fact = fact_ref[...]
    wide = fact.astype(F32)
    f1, f2 = split2(wide * wide)
    first = dot(jnp.concatenate([fact, f1, f2], axis=0), w1, NT)
    second = dot(jnp.concatenate([fact, f1], axis=0), w2, NT)
    grad = first[:FACT] + second[:FACT]
    curv = (first[FACT : 2 * FACT] + first[2 * FACT :]) + second[FACT:]
    for h in range(2):
        sums[h, :32, :] -= grad[32 * h : 32 * (h + 1), :]
        sums[h, 32:, :] += curv[32 * h : 32 * (h + 1), :]

    @pl.when(step == pl.num_programs(0) - 1)
    def _():
        kept_ref[...] = sums[core_ref[0]]
        given_ref[...] = sums[1 - core_ref[0]]


def update(live, core, steps, pred, design, load, fact, by_load, by_fact):
    genes, cells = pred.shape
    return pl.pallas_call(
        update_kernel,
        grid=(cells // CHUNK,),
        in_specs=[
            smem(), smem(), full((32, 384)), lanes(genes), lanes(96),
            full((FACT, genes)), lanes(FACT), lanes(FACT), full((FACT, genes)),
        ],
        out_specs=[
            pl.BlockSpec((CHUNK // 128, 2 * FACT, 128), lambda c: (c, 0, 0)),
            full((FACT, genes)),
            full((FACT, genes)),
            full((COLS, genes)),
        ],
        out_shape=[
            pltpu.HBM((cells // 128, 2 * FACT, 128), F32),
            jax.ShapeDtypeStruct((FACT, genes), F32),
            jax.ShapeDtypeStruct((FACT, genes), F32),
            jax.ShapeDtypeStruct((COLS, genes), F32),
        ],
        scratch_shapes=[
            pltpu.VMEM((genes, 6 * COLS), BF16), pltpu.VMEM((3 * FACT, genes), BF16),
            pltpu.VMEM((2, FACT, genes), F32),
        ],
        compiler_params=params(),
        name="update",
    )(live, core, steps, pred, design, load, fact, by_load, by_fact)


def score_kernel(core_ref, mine_ref, other_ref, out_ref):
    core = core_ref[0]
    for half, ref in ((core, mine_ref), (1 - core, other_ref)):
        out_ref[pl.ds(pl.multiple_of(32 * half, 32), 32), :] = ref[...]


def joined_score(core, mine, other):
    return pl.pallas_call(
        score_kernel,
        grid=(1,),
        in_specs=[smem(), full(mine.shape), full(mine.shape)],
        out_specs=full((FACT, mine.shape[1])),
        out_shape=jax.ShapeDtypeStruct((FACT, mine.shape[1]), F32),
        compiler_params=params(),
        name="joined_score",
    )(core, mine, other)


def factor_kernel(parts_ref, out_ref):
    total = parts_ref[0]
    for j in range(1, parts_ref.shape[0]):
        total = total + parts_ref[j]
    value = total[:FACT, :] / (total[FACT:, :] + 1.0)
    out_ref[...] = jnp.broadcast_to(value[None], out_ref.shape)


def factor_share(parts):
    peers = parts.shape[0]
    return pl.pallas_call(
        factor_kernel,
        grid=(1,),
        in_specs=[full(parts.shape)],
        out_specs=full((peers, FACT, 128)),
        out_shape=jax.ShapeDtypeStruct((peers, FACT, 128), F32),
        compiler_params=params(),
        name="factor_share",
    )(parts)


def exchange(value, axis, groups=None):
    return lax.all_to_all(
        value, axis, split_axis=0, concat_axis=0, tiled=True, axis_index_groups=groups
    )


def partners(move):
    def index(x, y, core):
        return (x * 4 + y) * 2 + core

    return [
        (index(x, y, core), index(*move(x, y, core)))
        for x in range(4)
        for y in range(4)
        for core in range(2)
    ]


SAME_CORE = [list(range(core, 32, 2)) for core in range(2)]
OTHER_CORE = partners(lambda x, y, c: (x, y, 1 - c))
ALONG_X = [partners(lambda x, y, c, k=k: (x ^ k, y, c)) for k in (1, 2, 3)]
ALONG_Y = [partners(lambda x, y, c, k=k: (x, y ^ k, c)) for k in (1, 3)]


def local(
    counts, batch_id, live_cells, knot_bin, depth_frac, cell_covariates,
    coefficients, batch_effect, factors, loadings,
):
    fact, load = factors.T, loadings.T
    tot = exchange(cell_totals(counts, 8), "gene")
    rest, design, score, by_load, by_fact = prepare(
        live_cells, counts, knot_bin[None], depth_frac[None], batch_id[None],
        cell_covariates, coefficients.T, batch_effect.T, load, fact,
    )
    core = (lax.axis_index("cell") % 2)[None]
    pred, kept, given = gram_sums(
        live_cells, core, tot, rest, design, score
    )
    packed = kept + lax.ppermute(given, "cell", OTHER_CORE)
    steps = exchange(solve(exchange(packed, "cell", SAME_CORE)), "cell")
    pieces, kept, given, beta = update(
        live_cells, core, steps.reshape(32, 384), pred, design, load, fact, by_load, by_fact
    )
    arrived = exchange(pieces, "gene")

    value = kept + lax.ppermute(given, "cell", OTHER_CORE)
    near, across, beside = (lax.ppermute(value, "cell", pairs) for pairs in ALONG_X)
    value = (value + near) + (across + beside)
    near = lax.ppermute(value, "cell", ALONG_Y[0])
    shared = factor_share(arrived)
    gathered = exchange(shared, "gene")
    near, _ = lax.optimization_barrier((near, shared))
    value = value + near
    value = value + lax.ppermute(value, "cell", ALONG_Y[1])
    mine = value[:32] / jnp.sqrt(value[32:] + 1.0)
    other = lax.ppermute(mine, "cell", OTHER_CORE)
    score = joined_score(core, mine, other)
    factor_step = jnp.moveaxis(gathered, 0, 1).reshape(FACT, -1)
    return beta.T, factor_step.T, score.T


def solution(mesh):
    placed = (
        P("gene", "cell"),
        P("cell"),
        P("cell"),
        P("cell"),
        P("cell"),
        P(None, "cell"),
        P("gene", None),
        P("gene", None),
        P("cell", None),
        P("gene", None),
    )
    return jax.shard_map(
        local,
        mesh=mesh,
        in_specs=placed,
        out_specs=(P("gene", None), P("cell", None), P("gene", None)),
        check_vma=False,
    )
```

```python
import functools

import jax
import jax.numpy as jnp
from jax import lax
from jax.experimental import pallas as pl
from jax.experimental.pallas import tpu as pltpu
from jax.sharding import PartitionSpec as P

GENES = 3072
SPL = 16
COLS = 32
FACT = 64
CHUNK = 256
F32 = jnp.float32
BF16 = jnp.bfloat16
NN = (((1,), (0,)), ((), ()))
NT = (((1,), (1,)), ((), ()))
TN = (((0,), (0,)), ((), ()))
MIB = 1024 * 1024


def dot(a, b, dims):
    return lax.dot_general(a, b, dims, preferred_element_type=F32)


def split2(x):
    hi = x.astype(BF16)
    return hi, (x - hi.astype(F32)).astype(BF16)


def split3(x):
    hi = x.astype(BF16)
    rest = x - hi.astype(F32)
    mid = rest.astype(BF16)
    return hi, mid, (rest - mid.astype(F32)).astype(BF16)


def full(shape):
    return pl.BlockSpec(shape, lambda c: (0,) * len(shape))


def lanes(rows, chunk=CHUNK):
    return pl.BlockSpec((rows, chunk), lambda c: (0, c))


def smem():
    return pl.BlockSpec(memory_space=pltpu.SMEM)


def vmem():
    return pl.BlockSpec(memory_space=pltpu.VMEM)


def hbm():
    return pl.BlockSpec(memory_space=pltpu.HBM)


def params(mib=16):
    return pltpu.CompilerParams(vmem_limit_bytes=mib * MIB)


def totals_kernel(counts_ref, out_ref, rows, stage, arrived, sent):
    blocks, size = rows.shape[0], rows.shape[1]

    def copy(b):
        return pltpu.make_async_copy(
            counts_ref.at[pl.ds(b * size, size), :], rows.at[b], arrived.at[b]
        )

    for b in range(blocks):
        copy(b).start()
    total = jnp.zeros((8, rows.shape[2]), F32)
    for b in range(blocks):
        copy(b).wait()
        part = rows[b, :8, :]
        for i in range(8, size, 8):
            part = part + rows[b, i : i + 8, :]
        total = total + part.astype(F32)
    total = jnp.sum(total, axis=0, keepdims=True)
    for i in range(8):
        stage[i : i + 1, :] = total[:, 128 * i : 128 * (i + 1)]
    sends = [
        pltpu.make_async_copy(stage, out_ref.at[z], sent.at[z]) for z in range(out_ref.shape[0])
    ]
    for send in sends:
        send.start()
    for send in sends:
        send.wait()


def cell_totals(counts, peers):
    genes, cells = counts.shape
    blocks = 12
    return pl.pallas_call(
        totals_kernel,
        in_specs=[hbm()],
        out_specs=hbm(),
        out_shape=pltpu.HBM((peers, 8, 128), F32),
        scratch_shapes=[
            pltpu.VMEM((blocks, genes // blocks, cells), jnp.int32),
            pltpu.VMEM((8, 128), F32),
            pltpu.SemaphoreType.DMA((blocks,)),
            pltpu.SemaphoreType.DMA((peers,)),
        ],
        compiler_params=params(),
        name="cell_totals",
    )(pltpu.with_memory_space_constraint(counts, pltpu.HBM))


def prepare_kernel(
    live_ref, counts_ref, knot_hbm, frac_hbm, batch_hbm, cov_hbm, coef_hbm, shift_hbm,
    load_hbm, fact_hbm,
    rest_ref, design_ref, score_ref, by_load_ref, by_fact_ref,
    left, knot_all, frac_all, batch_all, cov_all, coef, shift, load, fact_all, score, arrived,
):
    step = pl.program_id(0)

    @pl.when(step == 0)
    def _():
        pairs = (
            (coef_hbm, coef), (shift_hbm, shift), (load_hbm, load), (fact_hbm, fact_all),
            (knot_hbm, knot_all), (frac_hbm, frac_all), (batch_hbm, batch_all), (cov_hbm, cov_all),
        )
        copies = [
            pltpu.make_async_copy(source, target, arrived.at[i])
            for i, (source, target) in enumerate(pairs)
        ]
        for copy in copies:
            copy.start()
        for copy in copies:
            copy.wait()
        c1, c2, c3 = split3(coef[...])
        b1, b2, b3 = split3(shift[...])
        left[...] = jnp.concatenate([c1, c1, c2, c2, c1, c3, b1, b2, b3, load[...]], axis=0)
        score[...] = jnp.zeros_like(score)
        by_fact_ref[...] = jnp.zeros_like(by_fact_ref)

    at = pl.multiple_of(step * CHUNK, CHUNK)
    here = pl.ds(at, CHUNK)
    knot, frac, cov, fact = knot_all[:, here], frac_all[:, here], cov_all[:, here], fact_all[:, here]
    levels = lax.broadcasted_iota(jnp.int32, (SPL, CHUNK), 0)
    hat = jnp.where(levels == knot, 1.0 - frac, 0.0) + jnp.where(levels == knot + 1, frac, 0.0)
    d1, d2, d3 = split3(jnp.concatenate([hat, cov], axis=0))
    terms = jnp.concatenate([d1, d2, d3], axis=0)
    design_ref[...] = terms
    batches = lax.broadcasted_iota(jnp.int32, (64, CHUNK), 0)
    onehot = (batches == batch_all[:, here]).astype(F32).astype(BF16)
    right = jnp.concatenate([d1, d2, d1, d2, d3, d1, onehot, onehot, onehot, fact], axis=0)
    rest_ref[...] = dot(left[...], right, TN)

    slot = lax.broadcasted_iota(jnp.int32, (1, CHUNK), 1) + at
    mask = (slot < live_ref[0]).astype(F32)
    counts = (counts_ref[...].astype(F32) * mask).astype(BF16)
    by_load_ref[...] = dot(load[...], counts, NN)
    by_fact_ref[...] += dot(fact, counts, NT)
    score[...] += dot(counts, terms, NT)

    @pl.when(step == pl.num_programs(0) - 1)
    def _():
        value = score[:, :32] + score[:, 32:64] + score[:, 64:96]
        blank = jnp.zeros((value.shape[0], 96), F32)
        score_ref[...] = jnp.concatenate([blank, value], axis=1)


def prepare(live, counts, knot, frac, batch, cov, coef, shift, load, fact):
    genes, cells = counts.shape
    small = [
        pltpu.with_memory_space_constraint(a, pltpu.HBM)
        for a in (knot, frac, batch, cov, coef, shift, load, fact)
    ]
    counts = pltpu.with_memory_space_constraint(counts, pltpu.HBM)
    return pl.pallas_call(
        prepare_kernel,
        grid=(cells // CHUNK,),
        in_specs=[smem(), lanes(genes)] + [pl.BlockSpec(memory_space=pltpu.HBM)] * 8,
        out_specs=[
            lanes(genes), lanes(96), full((genes, 128)), lanes(FACT), full((FACT, genes)),
        ],
        out_shape=[
            jax.ShapeDtypeStruct((genes, cells), F32),
            jax.ShapeDtypeStruct((96, cells), BF16),
            jax.ShapeDtypeStruct((genes, 128), F32),
            jax.ShapeDtypeStruct((FACT, cells), F32),
            jax.ShapeDtypeStruct((FACT, genes), F32),
        ],
        scratch_shapes=[pltpu.VMEM((448, genes), BF16)]
        + [pltpu.VMEM(a.shape, a.dtype) for a in small]
        + [pltpu.VMEM((genes, 96), F32), pltpu.SemaphoreType.DMA((8,))],
        compiler_params=params(),
        name="prepare",
    )(live, counts, *small)


def gram_kernel(
    live_ref, core_ref, tot_ref, rest_ref, design_ref, score_ref,
    pred_ref, kept_ref, given_ref, offset, acc, terms_hi, terms_lo,
):
    total = jnp.sum(tot_ref[...], axis=0)
    value = jnp.log((1.0 + total) / GENES)
    for i in range(8):
        offset[:, 128 * i : 128 * (i + 1)] = value[i : i + 1, :]

    for at in range(0, rest_ref.shape[1], CHUNK):
        here = pl.ds(at, CHUNK)
        hi_ref, lo_ref = terms_hi.at[:, here], terms_lo.at[:, here]

        def put(row, value):
            hi, lo = split2(value)
            hi_ref[row : row + value.shape[0], :] = hi
            lo_ref[row : row + value.shape[0], :] = lo

        d1, d2, d3 = (design_ref[32 * i : 32 * (i + 1), here] for i in range(3))
        design = (d1.astype(F32) + d2.astype(F32)) + d3.astype(F32)
        hat, cov = design[:SPL], design[SPL:]
        put(0, hat * hat)
        put(16, hat * pltpu.roll(hat, SPL - 1, axis=0))
        for p in range(SPL):
            put(32 + 16 * p, hat[p : p + 1, :] * cov)
        low, high = cov[:8], cov[8:]
        for i in range(0, 8, 2):
            for row, left, right in ((288, low, low), (352, low, high), (416, high, high)):
                both = [left[i : i + 1] * right, left[i + 1 : i + 2] * right]
                put(row + 8 * i, jnp.concatenate(both, axis=0))
        put(480, -design)

        pred = rest_ref[:, here] + offset[:, here]
        pred_ref[:, here] = pred
        slot = lax.broadcasted_iota(jnp.int32, (1, CHUNK), 1) + at
        mask = (slot < live_ref[0]).astype(F32)
        w1, w2 = split2(jnp.exp(pred) * mask)
        hi, lo = hi_ref[...], lo_ref[...]
        gram = dot(w1, hi, NT) + dot(w1, lo, NT) + dot(w2, hi, NT)
        for t in range(4):
            part = gram[:, 128 * t : 128 * (t + 1)]
            if at > 0:
                acc[t] += part
            else:
                acc[t] = part + score_ref[...] if t == 3 else part

    core = core_ref[0]
    for chip in range(16):
        for ref, j in ((kept_ref, 2 * chip + core), (given_ref, 2 * chip + 1 - core)):
            for t in range(4):
                ref[chip, 12 * t : 12 * (t + 1), :] = acc[t, pl.ds(j, 12, stride=32), :]


def gram_sums(live, core, tot, rest, design, score):
    genes, cells = rest.shape
    return pl.pallas_call(
        gram_kernel,
        in_specs=[smem(), smem(), vmem(), vmem(), vmem(), vmem()],
        out_specs=[vmem(), vmem(), vmem()],
        out_shape=[
            jax.ShapeDtypeStruct((genes, cells), F32),
            jax.ShapeDtypeStruct((16, 48, 128), F32),
            jax.ShapeDtypeStruct((16, 48, 128), F32),
        ],
        scratch_shapes=[
            pltpu.VMEM((1, cells), F32), pltpu.VMEM((4, genes, 128), F32),
            pltpu.VMEM((512, cells), BF16), pltpu.VMEM((512, cells), BF16),
        ],
        compiler_params=params(),
        name="gram_sums",
    )(live, core, tot, rest, design, score)


def solve_kernel(parts_ref, out_ref, table):
    total = parts_ref[0]
    for j in range(1, parts_ref.shape[0]):
        total = total + parts_ref[j]
    turned = jnp.concatenate([total, jnp.zeros((80, 128), F32)], axis=0).T
    for t in range(4):
        moved = turned if t == 0 else pltpu.roll(turned, 128 - 12 * t, axis=1)
        table[128 * t : 128 * (t + 1), :] = moved
    row16 = lax.broadcasted_iota(jnp.int32, (SPL, 128), 0)
    row32 = lax.broadcasted_iota(jnp.int32, (COLS, 128), 0)
    diag, near = table[0:16, :] + 1.0, table[16:32, :]
    below = pltpu.roll(near, 1, axis=0)
    system = []
    for j in range(SPL):
        top = jnp.where(row16 == j, diag, 0.0)
        top = jnp.where(row16 == j - 1, near, top)
        top = jnp.where(row16 == j + 1, below, top)
        system.append(jnp.concatenate([top, table[32 + 16 * j : 48 + 16 * j, :]], axis=0))
    for q in range(SPL):
        top = table[pl.ds(32 + q, 16, stride=16), :]
        if q < 8:
            first = table[288 + 8 * q : 296 + 8 * q, :]
            second = table[352 + 8 * q : 360 + 8 * q, :]
        else:
            first = table[pl.ds(344 + q, 8, stride=8), :]
            second = table[352 + 8 * q : 360 + 8 * q, :]
        column = jnp.concatenate([top, first, second], axis=0)
        system.append(jnp.where(row32 == 16 + q, column + 1.0, column))
    rhs = table[480:512, :]
    scale = jnp.zeros((COLS, 128), F32)
    for k in range(COLS):
        column = system[k]
        inverse = 1.0 / column[k : k + 1, :]
        scale = jnp.where(row32 == k, inverse, scale)
        ratio = jnp.where(row32 == k, 0.0, column * inverse)
        touched = [j for j in range(k + 1, COLS) if j >= SPL or j == k + 1]
        for j in touched:
            system[j] = system[j] - ratio * column[j : j + 1, :]
        rhs = rhs - ratio * rhs[k : k + 1, :]
    answer = rhs * scale
    flat = jnp.concatenate([answer, jnp.zeros((96, 128), F32)], axis=0).T
    line = jnp.concatenate([flat[g : g + 1, :COLS] for g in range(12)], axis=1)
    out_ref[...] = jnp.broadcast_to(line[None], out_ref.shape)


def solve(parts):
    return pl.pallas_call(
        solve_kernel,
        in_specs=[vmem()],
        out_specs=vmem(),
        out_shape=jax.ShapeDtypeStruct((32, 1, 384), F32),
        scratch_shapes=[pltpu.VMEM((512, 128), F32)],
        compiler_params=params(),
        name="solve",
    )(parts)


def update_kernel(
    live_ref, core_ref, steps_ref, pred_ref, design_ref, load_ref, fact_ref,
    by_load_ref, by_fact_ref,
    out_hbm, kept_ref, given_ref, beta_hbm, left, loads, sums, out, beta_out, sent,
):
    steps = steps_ref[...]
    beta = jnp.concatenate([steps[:, COLS * g : COLS * (g + 1)] for g in range(12)], axis=0)
    b1, b2, b3 = split3(beta)
    left[...] = jnp.concatenate([b1, b1, b2, b2, b1, b3], axis=1)
    load = load_ref[...]
    wide = load.astype(F32)
    l1, l2 = split2(wide * wide)
    loads[...] = jnp.concatenate([load, l1, l2], axis=0)

    cells = pred_ref.shape[1]
    sends = []
    for at in range(0, cells, CHUNK):
        here = pl.ds(at, CHUNK)
        d1, d2, d3 = (design_ref[32 * i : 32 * (i + 1), here] for i in range(3))
        change = dot(left[...], jnp.concatenate([d1, d2, d1, d2, d3, d1], axis=0), NN)
        slot = lax.broadcasted_iota(jnp.int32, (1, CHUNK), 1) + at
        mask = (slot < live_ref[0]).astype(F32)
        w1, w2 = split2(jnp.exp(pred_ref[:, here] + change) * mask)
        first = dot(loads[...], w1, NN)
        second = dot(loads[: 2 * FACT], w2, NN)
        grad = by_load_ref[:, here] - (first[:FACT] + second[:FACT])
        curv = (first[FACT : 2 * FACT] + first[2 * FACT :]) + second[FACT:]
        for z in range(8):
            out[z, :8, here] = grad[8 * z : 8 * (z + 1), :]
            out[z, 8:, here] = curv[8 * z : 8 * (z + 1), :]
        send = pltpu.make_async_copy(
            out.at[:, :, here], out_hbm.at[:, :, here], sent.at[at // CHUNK]
        )
        send.start()
        sends.append(send)
        fact = fact_ref[:, here]
        wide = fact.astype(F32)
        f1, f2 = split2(wide * wide)
        first = dot(jnp.concatenate([fact, f1, f2], axis=0), w1, NT)
        second = dot(jnp.concatenate([fact, f1], axis=0), w2, NT)
        grad = first[:FACT] + second[:FACT]
        curv = (first[FACT : 2 * FACT] + first[2 * FACT :]) + second[FACT:]
        for h in range(2):
            rows = slice(32 * h, 32 * (h + 1))
            if at > 0:
                sums[h, :32, :] -= grad[rows]
                sums[h, 32:, :] += curv[rows]
            else:
                sums[h, :32, :] = by_fact_ref[rows, :] - grad[rows]
                sums[h, 32:, :] = curv[rows]

    beta_out[...] = beta.T
    send = pltpu.make_async_copy(beta_out, beta_hbm, sent.at[cells // CHUNK])
    send.start()
    sends.append(send)
    kept_ref[...] = sums[core_ref[0]]
    given_ref[...] = sums[1 - core_ref[0]]
    for send in sends:
        send.wait()


def update(live, core, steps, pred, design, load, fact, by_load, by_fact):
    genes, cells = pred.shape
    return pl.pallas_call(
        update_kernel,
        in_specs=[smem(), smem()] + [vmem()] * 7,
        out_specs=[hbm(), vmem(), vmem(), hbm()],
        out_shape=[
            pltpu.HBM((8, 16, cells), F32),
            jax.ShapeDtypeStruct((FACT, genes), F32),
            jax.ShapeDtypeStruct((FACT, genes), F32),
            pltpu.HBM((COLS, genes), F32),
        ],
        scratch_shapes=[
            pltpu.VMEM((genes, 6 * COLS), BF16), pltpu.VMEM((3 * FACT, genes), BF16),
            pltpu.VMEM((2, FACT, genes), F32), pltpu.VMEM((8, 16, cells), F32),
            pltpu.VMEM((COLS, genes), F32),
            pltpu.SemaphoreType.DMA((cells // CHUNK + 1,)),
        ],
        compiler_params=params(),
        name="update",
    )(live, core, steps, pred, design, load, fact, by_load, by_fact)


def score_kernel(core_ref, mine_ref, other_ref, out_ref):
    core = core_ref[0]
    for half, ref in ((core, mine_ref), (1 - core, other_ref)):
        out_ref[pl.ds(pl.multiple_of(32 * half, 32), 32), :] = ref[...]


def joined_score(core, mine, other):
    return pl.pallas_call(
        score_kernel,
        grid=(1,),
        in_specs=[smem(), full(mine.shape), full(mine.shape)],
        out_specs=full((FACT, mine.shape[1])),
        out_shape=jax.ShapeDtypeStruct((FACT, mine.shape[1]), F32),
        compiler_params=params(),
        name="joined_score",
    )(core, mine, other)


def factor_kernel(parts_ref, out_hbm, stage, sent):
    total = parts_ref[0]
    for j in range(1, parts_ref.shape[0]):
        total = total + parts_ref[j]
    stage[...] = total[:8, :] / (total[8:, :] + 1.0)
    sends = [
        pltpu.make_async_copy(stage, out_hbm.at[z], sent.at[z]) for z in range(out_hbm.shape[0])
    ]
    for send in sends:
        send.start()
    for send in sends:
        send.wait()


def factor_share(parts):
    peers, _, cells = parts.shape
    return pl.pallas_call(
        factor_kernel,
        in_specs=[vmem()],
        out_specs=hbm(),
        out_shape=pltpu.HBM((peers, 8, cells), F32),
        scratch_shapes=[pltpu.VMEM((8, cells), F32), pltpu.SemaphoreType.DMA((peers,))],
        compiler_params=params(),
        name="factor_share",
    )(parts)


def exchange(value, axis, groups=None):
    return lax.all_to_all(
        value, axis, split_axis=0, concat_axis=0, tiled=True, axis_index_groups=groups
    )


def partners(move):
    def index(x, y, core):
        return (x * 4 + y) * 2 + core

    return [
        (index(x, y, core), index(*move(x, y, core)))
        for x in range(4)
        for y in range(4)
        for core in range(2)
    ]


SAME_CORE = [list(range(core, 32, 2)) for core in range(2)]
OTHER_CORE = partners(lambda x, y, c: (x, y, 1 - c))
ALONG_X = [partners(lambda x, y, c, k=k: (x ^ k, y, c)) for k in (1, 2, 3)]
ALONG_Y = [partners(lambda x, y, c, k=k: (x, y ^ k, c)) for k in (1, 3)]


def local(
    counts, batch_id, live_cells, knot_bin, depth_frac, cell_covariates,
    coefficients, batch_effect, factors, loadings,
):
    fact, load = factors.T, loadings.T
    tot = exchange(cell_totals(counts, 8), "gene")
    rest, design, score, by_load, by_fact = prepare(
        live_cells, counts, knot_bin[None], depth_frac[None], batch_id[None],
        cell_covariates, coefficients.T, batch_effect.T, load, fact,
    )
    core = (lax.axis_index("cell") % 2)[None]
    pred, kept, given = gram_sums(
        live_cells, core, tot, rest, design, score
    )
    packed = kept + lax.ppermute(given, "cell", OTHER_CORE)
    steps = exchange(solve(exchange(packed, "cell", SAME_CORE)), "cell")
    pieces, kept, given, beta = update(
        live_cells, core, steps.reshape(32, 384), pred, design, load, fact, by_load, by_fact
    )
    arrived = exchange(pieces, "gene")

    value = kept + lax.ppermute(given, "cell", OTHER_CORE)
    near, across, beside = (lax.ppermute(value, "cell", pairs) for pairs in ALONG_X)
    value = (value + near) + (across + beside)
    near = lax.ppermute(value, "cell", ALONG_Y[0])
    shared = factor_share(arrived)
    gathered = exchange(shared, "gene")
    near, _ = lax.optimization_barrier((near, shared))
    value = value + near
    value = value + lax.ppermute(value, "cell", ALONG_Y[1])
    mine = value[:32] / jnp.sqrt(value[32:] + 1.0)
    other = lax.ppermute(mine, "cell", OTHER_CORE)
    score = joined_score(core, mine, other)
    factor_step = gathered.reshape(FACT, -1)
    return beta.T, factor_step.T, score.T


def solution(mesh):
    placed = (
        P("gene", "cell"),
        P("cell"),
        P("cell"),
        P("cell"),
        P("cell"),
        P(None, "cell"),
        P("gene", None),
        P("gene", None),
        P("cell", None),
        P("gene", None),
    )
    return jax.shard_map(
        local,
        mesh=mesh,
        in_specs=placed,
        out_specs=(P("gene", None), P("cell", None), P("gene", None)),
        check_vma=False,
    )
```

```python
import functools

import jax
import jax.numpy as jnp
from jax import lax
from jax.experimental import pallas as pl
from jax.experimental.pallas import tpu as pltpu
from jax.sharding import PartitionSpec as P

GENES = 3072
SPL = 16
COLS = 32
FACT = 64
CHUNK = 256
F32 = jnp.float32
BF16 = jnp.bfloat16
NN = (((1,), (0,)), ((), ()))
NT = (((1,), (1,)), ((), ()))
TN = (((0,), (0,)), ((), ()))
MIB = 1024 * 1024


def dot(a, b, dims):
    return lax.dot_general(a, b, dims, preferred_element_type=F32)


def split2(x):
    hi = x.astype(BF16)
    return hi, (x - hi.astype(F32)).astype(BF16)


def split3(x):
    hi = x.astype(BF16)
    rest = x - hi.astype(F32)
    mid = rest.astype(BF16)
    return hi, mid, (rest - mid.astype(F32)).astype(BF16)


def full(shape):
    return pl.BlockSpec(shape, lambda c: (0,) * len(shape))


def lanes(rows, chunk=CHUNK):
    return pl.BlockSpec((rows, chunk), lambda c: (0, c))


def smem():
    return pl.BlockSpec(memory_space=pltpu.SMEM)


def vmem():
    return pl.BlockSpec(memory_space=pltpu.VMEM)


def hbm():
    return pl.BlockSpec(memory_space=pltpu.HBM)


def params(mib=16):
    return pltpu.CompilerParams(vmem_limit_bytes=mib * MIB)


def totals_kernel(counts_ref, out_ref, rows, stage, arrived, sent):
    blocks, size = rows.shape[0], rows.shape[1]

    def copy(b):
        return pltpu.make_async_copy(
            counts_ref.at[pl.ds(b * size, size), :], rows.at[b], arrived.at[b]
        )

    for b in range(blocks):
        copy(b).start()
    total = jnp.zeros((8, rows.shape[2]), F32)
    for b in range(blocks):
        copy(b).wait()
        part = rows[b, :8, :]
        for i in range(8, size, 8):
            part = part + rows[b, i : i + 8, :]
        total = total + part.astype(F32)
    total = jnp.sum(total, axis=0, keepdims=True)
    for i in range(8):
        stage[i : i + 1, :] = total[:, 128 * i : 128 * (i + 1)]
    sends = [
        pltpu.make_async_copy(stage, out_ref.at[z], sent.at[z]) for z in range(out_ref.shape[0])
    ]
    for send in sends:
        send.start()
    for send in sends:
        send.wait()


def cell_totals(counts, peers):
    genes, cells = counts.shape
    blocks = 12
    return pl.pallas_call(
        totals_kernel,
        in_specs=[hbm()],
        out_specs=hbm(),
        out_shape=pltpu.HBM((peers, 8, 128), F32),
        scratch_shapes=[
            pltpu.VMEM((blocks, genes // blocks, cells), jnp.int32),
            pltpu.VMEM((8, 128), F32),
            pltpu.SemaphoreType.DMA((blocks,)),
            pltpu.SemaphoreType.DMA((peers,)),
        ],
        compiler_params=params(),
        name="cell_totals",
    )(pltpu.with_memory_space_constraint(counts, pltpu.HBM))


def prepare_kernel(
    live_ref, counts_ref, knot_hbm, frac_hbm, batch_hbm, cov_hbm, coef_hbm, shift_hbm,
    load_hbm, fact_hbm,
    rest_ref, design_ref, score_ref, by_load_ref, by_fact_ref,
    left, knot_all, frac_all, batch_all, cov_all, coef, shift, load, fact_all, score, arrived,
):
    step = pl.program_id(0)

    @pl.when(step == 0)
    def _():
        pairs = (
            (coef_hbm, coef), (shift_hbm, shift), (load_hbm, load), (fact_hbm, fact_all),
            (knot_hbm, knot_all), (frac_hbm, frac_all), (batch_hbm, batch_all), (cov_hbm, cov_all),
        )
        copies = [
            pltpu.make_async_copy(source, target, arrived.at[i])
            for i, (source, target) in enumerate(pairs)
        ]
        for copy in copies:
            copy.start()
        for copy in copies:
            copy.wait()
        c1, c2, c3 = split3(coef[...])
        b1, b2, b3 = split3(shift[...])
        left[...] = jnp.concatenate([c1, c1, c2, c2, c1, c3, b1, b2, b3, load[...]], axis=0)
        score[...] = jnp.zeros_like(score)
        by_fact_ref[...] = jnp.zeros_like(by_fact_ref)

    at = pl.multiple_of(step * CHUNK, CHUNK)
    here = pl.ds(at, CHUNK)
    knot, frac, cov, fact = knot_all[:, here], frac_all[:, here], cov_all[:, here], fact_all[:, here]
    levels = lax.broadcasted_iota(jnp.int32, (SPL, CHUNK), 0)
    hat = jnp.where(levels == knot, 1.0 - frac, 0.0) + jnp.where(levels == knot + 1, frac, 0.0)
    d1, d2, d3 = split3(jnp.concatenate([hat, cov], axis=0))
    terms = jnp.concatenate([d1, d2, d3], axis=0)
    design_ref[...] = terms
    batches = lax.broadcasted_iota(jnp.int32, (64, CHUNK), 0)
    onehot = (batches == batch_all[:, here]).astype(F32).astype(BF16)
    right = jnp.concatenate([d1, d2, d1, d2, d3, d1, onehot, onehot, onehot, fact], axis=0)
    rest_ref[...] = dot(left[...], right, TN)

    slot = lax.broadcasted_iota(jnp.int32, (1, CHUNK), 1) + at
    mask = (slot < live_ref[0]).astype(F32)
    counts = (counts_ref[...].astype(F32) * mask).astype(BF16)
    by_load_ref[...] = dot(load[...], counts, NN)
    by_fact_ref[...] += dot(fact, counts, NT)
    score[...] += dot(counts, terms, NT)

    @pl.when(step == pl.num_programs(0) - 1)
    def _():
        value = score[:, :32] + score[:, 32:64] + score[:, 64:96]
        blank = jnp.zeros((value.shape[0], 96), F32)
        score_ref[...] = jnp.concatenate([blank, value], axis=1)


def prepare(live, counts, knot, frac, batch, cov, coef, shift, load, fact):
    genes, cells = counts.shape
    small = [
        pltpu.with_memory_space_constraint(a, pltpu.HBM)
        for a in (knot, frac, batch, cov, coef, shift, load, fact)
    ]
    counts = pltpu.with_memory_space_constraint(counts, pltpu.HBM)
    return pl.pallas_call(
        prepare_kernel,
        grid=(cells // CHUNK,),
        in_specs=[smem(), lanes(genes)] + [pl.BlockSpec(memory_space=pltpu.HBM)] * 8,
        out_specs=[
            lanes(genes), lanes(96), full((genes, 128)), lanes(FACT), full((FACT, genes)),
        ],
        out_shape=[
            jax.ShapeDtypeStruct((genes, cells), F32),
            jax.ShapeDtypeStruct((96, cells), BF16),
            jax.ShapeDtypeStruct((genes, 128), F32),
            jax.ShapeDtypeStruct((FACT, cells), F32),
            jax.ShapeDtypeStruct((FACT, genes), F32),
        ],
        scratch_shapes=[pltpu.VMEM((448, genes), BF16)]
        + [pltpu.VMEM(a.shape, a.dtype) for a in small]
        + [pltpu.VMEM((genes, 96), F32), pltpu.SemaphoreType.DMA((8,))],
        compiler_params=params(),
        name="prepare",
    )(live, counts, *small)


def gram_kernel(
    live_ref, core_ref, tot_ref, rest_ref, design_ref, score_ref,
    pred_ref, kept_ref, given_ref, offset, acc, terms_hi, terms_lo,
):
    total = jnp.sum(tot_ref[...], axis=0)
    value = jnp.log((1.0 + total) / GENES)
    for i in range(8):
        offset[:, 128 * i : 128 * (i + 1)] = value[i : i + 1, :]

    for at in range(0, rest_ref.shape[1], CHUNK):
        here = pl.ds(at, CHUNK)
        hi_ref, lo_ref = terms_hi.at[:, here], terms_lo.at[:, here]

        def put(row, value):
            hi, lo = split2(value)
            hi_ref[row : row + value.shape[0], :] = hi
            lo_ref[row : row + value.shape[0], :] = lo

        d1, d2, d3 = (design_ref[32 * i : 32 * (i + 1), here] for i in range(3))
        design = (d1.astype(F32) + d2.astype(F32)) + d3.astype(F32)
        hat, cov = design[:SPL], design[SPL:]
        put(0, hat * hat)
        put(16, hat * pltpu.roll(hat, SPL - 1, axis=0))
        for p in range(SPL):
            put(32 + 16 * p, hat[p : p + 1, :] * cov)
        low, high = cov[:8], cov[8:]
        for i in range(0, 8, 2):
            for row, left, right in ((288, low, low), (352, low, high), (416, high, high)):
                both = [left[i : i + 1] * right, left[i + 1 : i + 2] * right]
                put(row + 8 * i, jnp.concatenate(both, axis=0))
        put(480, -design)

        pred = rest_ref[:, here] + offset[:, here]
        pred_ref[:, here] = pred
        slot = lax.broadcasted_iota(jnp.int32, (1, CHUNK), 1) + at
        mask = (slot < live_ref[0]).astype(F32)
        w1, w2 = split2(jnp.exp(pred) * mask)
        hi, lo = hi_ref[...], lo_ref[...]
        gram = dot(w1, hi, NT) + dot(w1, lo, NT) + dot(w2, hi, NT)
        for t in range(4):
            part = gram[:, 128 * t : 128 * (t + 1)]
            if at > 0:
                acc[t] += part
            else:
                acc[t] = part + score_ref[...] if t == 3 else part

    core = core_ref[0]
    for chip in range(16):
        for ref, j in ((kept_ref, 16 * core + chip), (given_ref, 16 * (1 - core) + chip)):
            for t in range(4):
                ref[chip, 12 * t : 12 * (t + 1), :] = acc[t, pl.ds(j, 12, stride=32), :]


def gram_sums(live, core, tot, rest, design, score):
    genes, cells = rest.shape
    return pl.pallas_call(
        gram_kernel,
        in_specs=[smem(), smem(), vmem(), vmem(), vmem(), vmem()],
        out_specs=[vmem(), vmem(), vmem()],
        out_shape=[
            jax.ShapeDtypeStruct((genes, cells), F32),
            jax.ShapeDtypeStruct((16, 48, 128), F32),
            jax.ShapeDtypeStruct((16, 48, 128), F32),
        ],
        scratch_shapes=[
            pltpu.VMEM((1, cells), F32), pltpu.VMEM((4, genes, 128), F32),
            pltpu.VMEM((512, cells), BF16), pltpu.VMEM((512, cells), BF16),
        ],
        compiler_params=params(),
        name="gram_sums",
    )(live, core, tot, rest, design, score)


def solve_kernel(parts_ref, out_ref, table):
    total = parts_ref[0]
    for j in range(1, parts_ref.shape[0]):
        total = total + parts_ref[j]
    turned = jnp.concatenate([total, jnp.zeros((80, 128), F32)], axis=0).T
    for t in range(4):
        moved = turned if t == 0 else pltpu.roll(turned, 128 - 12 * t, axis=1)
        table[128 * t : 128 * (t + 1), :] = moved
    row16 = lax.broadcasted_iota(jnp.int32, (SPL, 128), 0)
    row32 = lax.broadcasted_iota(jnp.int32, (COLS, 128), 0)
    diag, near = table[0:16, :] + 1.0, table[16:32, :]
    below = pltpu.roll(near, 1, axis=0)
    system = []
    for j in range(SPL):
        top = jnp.where(row16 == j, diag, 0.0)
        top = jnp.where(row16 == j - 1, near, top)
        top = jnp.where(row16 == j + 1, below, top)
        system.append(jnp.concatenate([top, table[32 + 16 * j : 48 + 16 * j, :]], axis=0))
    for q in range(SPL):
        top = table[pl.ds(32 + q, 16, stride=16), :]
        if q < 8:
            first = table[288 + 8 * q : 296 + 8 * q, :]
            second = table[352 + 8 * q : 360 + 8 * q, :]
        else:
            first = table[pl.ds(344 + q, 8, stride=8), :]
            second = table[352 + 8 * q : 360 + 8 * q, :]
        column = jnp.concatenate([top, first, second], axis=0)
        system.append(jnp.where(row32 == 16 + q, column + 1.0, column))
    rhs = table[480:512, :]
    scale = jnp.zeros((COLS, 128), F32)
    for k in range(COLS):
        column = system[k]
        inverse = 1.0 / column[k : k + 1, :]
        scale = jnp.where(row32 == k, inverse, scale)
        ratio = jnp.where(row32 == k, 0.0, column * inverse)
        touched = [j for j in range(k + 1, COLS) if j >= SPL or j == k + 1]
        for j in touched:
            system[j] = system[j] - ratio * column[j : j + 1, :]
        rhs = rhs - ratio * rhs[k : k + 1, :]
    answer = rhs * scale
    flat = jnp.concatenate([answer, jnp.zeros((96, 128), F32)], axis=0).T
    line = jnp.concatenate([flat[g : g + 1, :COLS] for g in range(12)], axis=1)
    out_ref[...] = jnp.broadcast_to(line[None], out_ref.shape)


def solve(parts):
    return pl.pallas_call(
        solve_kernel,
        in_specs=[vmem()],
        out_specs=vmem(),
        out_shape=jax.ShapeDtypeStruct((32, 1, 384), F32),
        scratch_shapes=[pltpu.VMEM((512, 128), F32)],
        compiler_params=params(),
        name="solve",
    )(parts)


def update_kernel(
    live_ref, core_ref, steps_ref, pred_ref, design_ref, load_ref, fact_ref,
    by_load_ref, by_fact_ref,
    out_hbm, kept_ref, given_ref, beta_hbm, left, loads, sums, out, beta_out, sent,
):
    steps = steps_ref[...]
    beta = jnp.concatenate([steps[:, COLS * g : COLS * (g + 1)] for g in range(12)], axis=0)
    b1, b2, b3 = split3(beta)
    left[...] = jnp.concatenate([b1, b1, b2, b2, b1, b3], axis=1)
    load = load_ref[...]
    wide = load.astype(F32)
    l1, l2 = split2(wide * wide)
    loads[...] = jnp.concatenate([load, l1, l2], axis=0)

    cells = pred_ref.shape[1]
    sends = []
    for at in range(0, cells, CHUNK):
        here = pl.ds(at, CHUNK)
        d1, d2, d3 = (design_ref[32 * i : 32 * (i + 1), here] for i in range(3))
        change = dot(left[...], jnp.concatenate([d1, d2, d1, d2, d3, d1], axis=0), NN)
        slot = lax.broadcasted_iota(jnp.int32, (1, CHUNK), 1) + at
        mask = (slot < live_ref[0]).astype(F32)
        w1, w2 = split2(jnp.exp(pred_ref[:, here] + change) * mask)
        first = dot(loads[...], w1, NN)
        second = dot(loads[: 2 * FACT], w2, NN)
        grad = by_load_ref[:, here] - (first[:FACT] + second[:FACT])
        curv = (first[FACT : 2 * FACT] + first[2 * FACT :]) + second[FACT:]
        for z in range(8):
            out[z, :8, here] = grad[8 * z : 8 * (z + 1), :]
            out[z, 8:, here] = curv[8 * z : 8 * (z + 1), :]
        send = pltpu.make_async_copy(
            out.at[:, :, here], out_hbm.at[:, :, here], sent.at[at // CHUNK]
        )
        send.start()
        sends.append(send)
        fact = fact_ref[:, here]
        wide = fact.astype(F32)
        f1, f2 = split2(wide * wide)
        first = dot(jnp.concatenate([fact, f1, f2], axis=0), w1, NT)
        second = dot(jnp.concatenate([fact, f1], axis=0), w2, NT)
        grad = first[:FACT] + second[:FACT]
        curv = (first[FACT : 2 * FACT] + first[2 * FACT :]) + second[FACT:]
        for h in range(2):
            rows = slice(32 * h, 32 * (h + 1))
            if at > 0:
                sums[h, :32, :] -= grad[rows]
                sums[h, 32:, :] += curv[rows]
            else:
                sums[h, :32, :] = by_fact_ref[rows, :] - grad[rows]
                sums[h, 32:, :] = curv[rows]

    beta_out[...] = beta.T
    send = pltpu.make_async_copy(beta_out, beta_hbm, sent.at[cells // CHUNK])
    send.start()
    sends.append(send)
    kept_ref[...] = sums[core_ref[0]]
    given_ref[...] = sums[1 - core_ref[0]]
    for send in sends:
        send.wait()


def update(live, core, steps, pred, design, load, fact, by_load, by_fact):
    genes, cells = pred.shape
    return pl.pallas_call(
        update_kernel,
        in_specs=[smem(), smem()] + [vmem()] * 7,
        out_specs=[hbm(), vmem(), vmem(), hbm()],
        out_shape=[
            pltpu.HBM((8, 16, cells), F32),
            jax.ShapeDtypeStruct((FACT, genes), F32),
            jax.ShapeDtypeStruct((FACT, genes), F32),
            pltpu.HBM((COLS, genes), F32),
        ],
        scratch_shapes=[
            pltpu.VMEM((genes, 6 * COLS), BF16), pltpu.VMEM((3 * FACT, genes), BF16),
            pltpu.VMEM((2, FACT, genes), F32), pltpu.VMEM((8, 16, cells), F32),
            pltpu.VMEM((COLS, genes), F32),
            pltpu.SemaphoreType.DMA((cells // CHUNK + 1,)),
        ],
        compiler_params=params(),
        name="update",
    )(live, core, steps, pred, design, load, fact, by_load, by_fact)


def score_kernel(core_ref, mine_ref, other_ref, out_ref):
    core = core_ref[0]
    for half, ref in ((core, mine_ref), (1 - core, other_ref)):
        out_ref[pl.ds(pl.multiple_of(32 * half, 32), 32), :] = ref[...]


def joined_score(core, mine, other):
    return pl.pallas_call(
        score_kernel,
        grid=(1,),
        in_specs=[smem(), full(mine.shape), full(mine.shape)],
        out_specs=full((FACT, mine.shape[1])),
        out_shape=jax.ShapeDtypeStruct((FACT, mine.shape[1]), F32),
        compiler_params=params(),
        name="joined_score",
    )(core, mine, other)


def factor_kernel(parts_ref, out_hbm, stage, sent):
    total = parts_ref[0]
    for j in range(1, parts_ref.shape[0]):
        total = total + parts_ref[j]
    stage[...] = total[:8, :] / (total[8:, :] + 1.0)
    sends = [
        pltpu.make_async_copy(stage, out_hbm.at[z], sent.at[z]) for z in range(out_hbm.shape[0])
    ]
    for send in sends:
        send.start()
    for send in sends:
        send.wait()


def factor_share(parts):
    peers, _, cells = parts.shape
    return pl.pallas_call(
        factor_kernel,
        in_specs=[vmem()],
        out_specs=hbm(),
        out_shape=pltpu.HBM((peers, 8, cells), F32),
        scratch_shapes=[pltpu.VMEM((8, cells), F32), pltpu.SemaphoreType.DMA((peers,))],
        compiler_params=params(),
        name="factor_share",
    )(parts)


def settle_kernel(value_ref, out_hbm, sent):
    sends = [
        pltpu.make_async_copy(value_ref.at[z], out_hbm.at[z], sent.at[z])
        for z in range(value_ref.shape[0])
    ]
    for send in sends:
        send.start()
    for send in sends:
        send.wait()


def settled(value):
    return pl.pallas_call(
        settle_kernel,
        in_specs=[vmem()],
        out_specs=hbm(),
        out_shape=pltpu.HBM(value.shape, value.dtype),
        scratch_shapes=[pltpu.SemaphoreType.DMA((value.shape[0],))],
        compiler_params=params(),
        name="settled",
    )(value)


def exchange(value, axis, groups=None):
    return lax.all_to_all(
        value, axis, split_axis=0, concat_axis=0, tiled=True, axis_index_groups=groups
    )


def partners(move):
    def index(x, y, core):
        return (x * 4 + y) * 2 + core

    return [
        (index(x, y, core), index(*move(x, y, core)))
        for x in range(4)
        for y in range(4)
        for core in range(2)
    ]


SAME_CORE = [[(4 * x + y) * 2 + core for y in range(4) for x in range(4)] for core in range(2)]
CORE_FIRST = [SAME_CORE[0] + SAME_CORE[1]]
RING = [[3, 4, 2, 5, 1, 6, 0, 7]]
OTHER_CORE = partners(lambda x, y, c: (x, y, 1 - c))
ALONG_X = [partners(lambda x, y, c, k=k: (x ^ k, y, c)) for k in (1, 2, 3)]
ALONG_Y = [partners(lambda x, y, c, k=k: (x, y ^ k, c)) for k in (1, 3)]


def local(
    counts, batch_id, live_cells, knot_bin, depth_frac, cell_covariates,
    coefficients, batch_effect, factors, loadings,
):
    fact, load = factors.T, loadings.T
    tot = exchange(cell_totals(counts, 8), "gene")
    rest, design, score, by_load, by_fact = prepare(
        live_cells, counts, knot_bin[None], depth_frac[None], batch_id[None],
        cell_covariates, coefficients.T, batch_effect.T, load, fact,
    )
    core = (lax.axis_index("cell") % 2)[None]
    pred, kept, given = gram_sums(
        live_cells, core, tot, rest, design, score
    )
    packed = kept + lax.ppermute(given, "cell", OTHER_CORE)
    steps = exchange(solve(exchange(packed, "cell", SAME_CORE)), "cell", CORE_FIRST)
    pieces, kept, given, beta = update(
        live_cells, core, steps.reshape(32, 384), pred, design, load, fact, by_load, by_fact
    )
    arrived = exchange(pieces, "gene", RING)

    value = kept + lax.ppermute(given, "cell", OTHER_CORE)
    near, across, beside = (lax.ppermute(value, "cell", pairs) for pairs in ALONG_X)
    value = (value + near) + (across + beside)
    near = lax.ppermute(value, "cell", ALONG_Y[0])
    shared = factor_share(arrived)
    gathered = settled(exchange(shared, "gene", RING))
    near, _ = lax.optimization_barrier((near, shared))
    value = value + near
    value = value + lax.ppermute(value, "cell", ALONG_Y[1])
    mine = value[:32] / jnp.sqrt(value[32:] + 1.0)
    other = lax.ppermute(mine, "cell", OTHER_CORE)
    score = joined_score(core, mine, other)
    factor_step = gathered.reshape(FACT, -1)
    return beta.T, factor_step.T, score.T


def solution(mesh):
    placed = (
        P("gene", "cell"),
        P("cell"),
        P("cell"),
        P("cell"),
        P("cell"),
        P(None, "cell"),
        P("gene", None),
        P("gene", None),
        P("cell", None),
        P("gene", None),
    )
    return jax.shard_map(
        local,
        mesh=mesh,
        in_specs=placed,
        out_specs=(P("gene", None), P("cell", None), P("gene", None)),
        check_vma=False,
    )
```

```python
import functools

import jax
import jax.numpy as jnp
from jax import lax
from jax.experimental import pallas as pl
from jax.experimental.pallas import tpu as pltpu
from jax.sharding import PartitionSpec as P

GENES = 3072
SPL = 16
COLS = 32
FACT = 64
CHUNK = 256
F32 = jnp.float32
BF16 = jnp.bfloat16
NN = (((1,), (0,)), ((), ()))
NT = (((1,), (1,)), ((), ()))
TN = (((0,), (0,)), ((), ()))
MIB = 1024 * 1024


def dot(a, b, dims):
    return lax.dot_general(a, b, dims, preferred_element_type=F32)


def split2(x):
    hi = x.astype(BF16)
    return hi, (x - hi.astype(F32)).astype(BF16)


def split3(x):
    hi = x.astype(BF16)
    rest = x - hi.astype(F32)
    mid = rest.astype(BF16)
    return hi, mid, (rest - mid.astype(F32)).astype(BF16)


def full(shape):
    return pl.BlockSpec(shape, lambda c: (0,) * len(shape))


def lanes(rows, chunk=CHUNK):
    return pl.BlockSpec((rows, chunk), lambda c: (0, c))


def smem():
    return pl.BlockSpec(memory_space=pltpu.SMEM)


def vmem():
    return pl.BlockSpec(memory_space=pltpu.VMEM)


def hbm():
    return pl.BlockSpec(memory_space=pltpu.HBM)


def params(mib=16):
    return pltpu.CompilerParams(vmem_limit_bytes=mib * MIB)


def totals_kernel(counts_ref, out_ref, rows, stage, arrived, sent):
    blocks, size = rows.shape[0], rows.shape[1]

    def copy(b):
        return pltpu.make_async_copy(
            counts_ref.at[pl.ds(b * size, size), :], rows.at[b], arrived.at[b]
        )

    for b in range(blocks):
        copy(b).start()
    total = jnp.zeros((8, rows.shape[2]), F32)
    for b in range(blocks):
        copy(b).wait()
        part = rows[b, :8, :]
        for i in range(8, size, 8):
            part = part + rows[b, i : i + 8, :]
        total = total + part.astype(F32)
    total = jnp.sum(total, axis=0, keepdims=True)
    for i in range(8):
        stage[i : i + 1, :] = total[:, 128 * i : 128 * (i + 1)]
    sends = [
        pltpu.make_async_copy(stage, out_ref.at[z], sent.at[z]) for z in range(out_ref.shape[0])
    ]
    for send in sends:
        send.start()
    for send in sends:
        send.wait()


def cell_totals(counts, peers):
    genes, cells = counts.shape
    blocks = 12
    return pl.pallas_call(
        totals_kernel,
        in_specs=[hbm()],
        out_specs=hbm(),
        out_shape=pltpu.HBM((peers, 8, 128), F32),
        scratch_shapes=[
            pltpu.VMEM((blocks, genes // blocks, cells), jnp.int32),
            pltpu.VMEM((8, 128), F32),
            pltpu.SemaphoreType.DMA((blocks,)),
            pltpu.SemaphoreType.DMA((peers,)),
        ],
        compiler_params=params(),
        name="cell_totals",
    )(pltpu.with_memory_space_constraint(counts, pltpu.HBM))


def prepare_kernel(
    live_ref, counts_hbm, knot_hbm, frac_hbm, batch_hbm, cov_hbm, coef_hbm, shift_hbm,
    load_hbm, fact_hbm,
    rest_ref, design_ref, score_ref, by_load_ref, by_fact_ref,
    counts_all, knot_all, frac_all, batch_all, cov_all, coef, shift, load, fact_all, arrived,
):
    pairs = (
        (knot_hbm, knot_all), (frac_hbm, frac_all), (batch_hbm, batch_all), (cov_hbm, cov_all),
        (coef_hbm, coef), (shift_hbm, shift), (load_hbm, load), (fact_hbm, fact_all),
    )
    copies = [
        pltpu.make_async_copy(source, target, arrived.at[i])
        for i, (source, target) in enumerate(pairs)
    ]
    cells = rest_ref.shape[1]
    blocks = [
        pltpu.make_async_copy(
            counts_hbm.at[:, pl.ds(at, CHUNK)], counts_all.at[:, pl.ds(at, CHUNK)],
            arrived.at[len(pairs) + at // CHUNK],
        )
        for at in range(0, cells, CHUNK)
    ]
    for copy in copies + blocks:
        copy.start()
    for copy in copies:
        copy.wait()
    c1, c2, c3 = split3(coef[...])
    b1, b2, b3 = split3(shift[...])
    left = jnp.concatenate([c1, c1, c2, c2, c1, c3, b1, b2, b3, load[...]], axis=0)
    score, by_fact = 0.0, 0.0
    for at in range(0, cells, CHUNK):
        here = pl.ds(at, CHUNK)
        knot, frac = knot_all[:, here], frac_all[:, here]
        cov, fact = cov_all[:, here], fact_all[:, here]
        levels = lax.broadcasted_iota(jnp.int32, (SPL, CHUNK), 0)
        hat = jnp.where(levels == knot, 1.0 - frac, 0.0)
        hat = hat + jnp.where(levels == knot + 1, frac, 0.0)
        d1, d2, d3 = split3(jnp.concatenate([hat, cov], axis=0))
        terms = jnp.concatenate([d1, d2, d3], axis=0)
        design_ref[:, here] = terms
        batches = lax.broadcasted_iota(jnp.int32, (64, CHUNK), 0)
        onehot = (batches == batch_all[:, here]).astype(F32).astype(BF16)
        right = jnp.concatenate([d1, d2, d1, d2, d3, d1, onehot, onehot, onehot, fact], axis=0)
        rest_ref[:, here] = dot(left, right, TN)

        blocks[at // CHUNK].wait()
        slot = lax.broadcasted_iota(jnp.int32, (1, CHUNK), 1) + at
        mask = (slot < live_ref[0]).astype(F32)
        counts = (counts_all[:, here].astype(F32) * mask).astype(BF16)
        by_load_ref[:, here] = dot(load[...], counts, NN)
        by_fact = by_fact + dot(fact, counts, NT)
        score = score + dot(counts, terms, NT)
    by_fact_ref[...] = by_fact
    value = score[:, :32] + score[:, 32:64] + score[:, 64:96]
    blank = jnp.zeros((value.shape[0], 96), F32)
    score_ref[...] = jnp.concatenate([blank, value], axis=1)


def prepare(live, counts, knot, frac, batch, cov, coef, shift, load, fact):
    genes, cells = counts.shape
    arrays = [
        pltpu.with_memory_space_constraint(a, pltpu.HBM)
        for a in (counts, knot, frac, batch, cov, coef, shift, load, fact)
    ]
    return pl.pallas_call(
        prepare_kernel,
        in_specs=[smem()] + [hbm()] * len(arrays),
        out_specs=[vmem()] * 5,
        out_shape=[
            jax.ShapeDtypeStruct((genes, cells), F32),
            jax.ShapeDtypeStruct((96, cells), BF16),
            jax.ShapeDtypeStruct((genes, 128), F32),
            jax.ShapeDtypeStruct((FACT, cells), F32),
            jax.ShapeDtypeStruct((FACT, genes), F32),
        ],
        scratch_shapes=[pltpu.VMEM(a.shape, a.dtype) for a in arrays]
        + [pltpu.SemaphoreType.DMA((len(arrays) - 1 + cells // CHUNK,))],
        compiler_params=params(),
        name="prepare",
    )(live, *arrays)


def gram_kernel(
    live_ref, core_ref, tot_ref, rest_ref, design_ref, score_ref,
    pred_ref, kept_ref, given_ref, offset, acc, terms_hi, terms_lo,
):
    total = jnp.sum(tot_ref[...], axis=0)
    value = jnp.log((1.0 + total) / GENES)
    for i in range(8):
        offset[:, 128 * i : 128 * (i + 1)] = value[i : i + 1, :]

    for at in range(0, rest_ref.shape[1], CHUNK):
        here = pl.ds(at, CHUNK)
        hi_ref, lo_ref = terms_hi.at[:, here], terms_lo.at[:, here]

        def put(row, value):
            hi, lo = split2(value)
            hi_ref[row : row + value.shape[0], :] = hi
            lo_ref[row : row + value.shape[0], :] = lo

        d1, d2, d3 = (design_ref[32 * i : 32 * (i + 1), here] for i in range(3))
        design = (d1.astype(F32) + d2.astype(F32)) + d3.astype(F32)
        hat, cov = design[:SPL], design[SPL:]
        put(0, hat * hat)
        put(16, hat * pltpu.roll(hat, SPL - 1, axis=0))
        for p in range(SPL):
            put(32 + 16 * p, hat[p : p + 1, :] * cov)
        low, high = cov[:8], cov[8:]
        for i in range(0, 8, 2):
            for row, left, right in ((288, low, low), (352, low, high), (416, high, high)):
                both = [left[i : i + 1] * right, left[i + 1 : i + 2] * right]
                put(row + 8 * i, jnp.concatenate(both, axis=0))
        put(480, -design)

        pred = rest_ref[:, here] + offset[:, here]
        pred_ref[:, here] = pred
        slot = lax.broadcasted_iota(jnp.int32, (1, CHUNK), 1) + at
        mask = (slot < live_ref[0]).astype(F32)
        w1, w2 = split2(jnp.exp(pred) * mask)
        hi, lo = hi_ref[...], lo_ref[...]
        gram = dot(w1, hi, NT) + dot(w1, lo, NT) + dot(w2, hi, NT)
        for t in range(4):
            part = gram[:, 128 * t : 128 * (t + 1)]
            if at > 0:
                acc[t] += part
            else:
                acc[t] = part + score_ref[...] if t == 3 else part

    core = core_ref[0]
    for chip in range(16):
        for ref, j in ((kept_ref, 16 * core + chip), (given_ref, 16 * (1 - core) + chip)):
            for t in range(4):
                ref[chip, 12 * t : 12 * (t + 1), :] = acc[t, pl.ds(j, 12, stride=32), :]


def gram_sums(live, core, tot, rest, design, score):
    genes, cells = rest.shape
    return pl.pallas_call(
        gram_kernel,
        in_specs=[smem(), smem(), vmem(), vmem(), vmem(), vmem()],
        out_specs=[vmem(), vmem(), vmem()],
        out_shape=[
            jax.ShapeDtypeStruct((genes, cells), F32),
            jax.ShapeDtypeStruct((16, 48, 128), F32),
            jax.ShapeDtypeStruct((16, 48, 128), F32),
        ],
        scratch_shapes=[
            pltpu.VMEM((1, cells), F32), pltpu.VMEM((4, genes, 128), F32),
            pltpu.VMEM((512, cells), BF16), pltpu.VMEM((512, cells), BF16),
        ],
        compiler_params=params(),
        name="gram_sums",
    )(live, core, tot, rest, design, score)


def solve_kernel(parts_ref, out_ref, table):
    total = parts_ref[0]
    for j in range(1, parts_ref.shape[0]):
        total = total + parts_ref[j]
    turned = jnp.concatenate([total, jnp.zeros((80, 128), F32)], axis=0).T
    for t in range(4):
        moved = turned if t == 0 else pltpu.roll(turned, 128 - 12 * t, axis=1)
        table[128 * t : 128 * (t + 1), :] = moved
    row16 = lax.broadcasted_iota(jnp.int32, (SPL, 128), 0)
    row32 = lax.broadcasted_iota(jnp.int32, (COLS, 128), 0)
    diag, near = table[0:16, :] + 1.0, table[16:32, :]
    below = pltpu.roll(near, 1, axis=0)
    system = []
    for j in range(SPL):
        top = jnp.where(row16 == j, diag, 0.0)
        top = jnp.where(row16 == j - 1, near, top)
        top = jnp.where(row16 == j + 1, below, top)
        system.append(jnp.concatenate([top, table[32 + 16 * j : 48 + 16 * j, :]], axis=0))
    for q in range(SPL):
        top = table[pl.ds(32 + q, 16, stride=16), :]
        if q < 8:
            first = table[288 + 8 * q : 296 + 8 * q, :]
            second = table[352 + 8 * q : 360 + 8 * q, :]
        else:
            first = table[pl.ds(344 + q, 8, stride=8), :]
            second = table[352 + 8 * q : 360 + 8 * q, :]
        column = jnp.concatenate([top, first, second], axis=0)
        system.append(jnp.where(row32 == 16 + q, column + 1.0, column))
    rhs = table[480:512, :]
    scale = jnp.zeros((COLS, 128), F32)
    for k in range(COLS):
        column = system[k]
        inverse = 1.0 / column[k : k + 1, :]
        scale = jnp.where(row32 == k, inverse, scale)
        ratio = jnp.where(row32 == k, 0.0, column * inverse)
        touched = [j for j in range(k + 1, COLS) if j >= SPL or j == k + 1]
        for j in touched:
            system[j] = system[j] - ratio * column[j : j + 1, :]
        rhs = rhs - ratio * rhs[k : k + 1, :]
    answer = rhs * scale
    flat = jnp.concatenate([answer, jnp.zeros((96, 128), F32)], axis=0).T
    line = jnp.concatenate([flat[g : g + 1, :COLS] for g in range(12)], axis=1)
    out_ref[...] = jnp.broadcast_to(line[None], out_ref.shape)


def solve(parts):
    return pl.pallas_call(
        solve_kernel,
        in_specs=[vmem()],
        out_specs=vmem(),
        out_shape=jax.ShapeDtypeStruct((32, 1, 384), F32),
        scratch_shapes=[pltpu.VMEM((512, 128), F32)],
        compiler_params=params(),
        name="solve",
    )(parts)


def update_kernel(
    live_ref, core_ref, steps_ref, pred_ref, design_ref, load_ref, fact_ref,
    by_load_ref, by_fact_ref,
    out_hbm, kept_ref, given_ref, beta_hbm, left, loads, sums, out, beta_out, sent,
):
    steps = steps_ref[...]
    beta = jnp.concatenate([steps[:, COLS * g : COLS * (g + 1)] for g in range(12)], axis=0)
    b1, b2, b3 = split3(beta)
    left[...] = jnp.concatenate([b1, b1, b2, b2, b1, b3], axis=1)
    load = load_ref[...]
    wide = load.astype(F32)
    l1, l2 = split2(wide * wide)
    loads[...] = jnp.concatenate([load, l1, l2], axis=0)

    cells = pred_ref.shape[1]
    sends = []
    for at in range(0, cells, CHUNK):
        here = pl.ds(at, CHUNK)
        d1, d2, d3 = (design_ref[32 * i : 32 * (i + 1), here] for i in range(3))
        change = dot(left[...], jnp.concatenate([d1, d2, d1, d2, d3, d1], axis=0), NN)
        slot = lax.broadcasted_iota(jnp.int32, (1, CHUNK), 1) + at
        mask = (slot < live_ref[0]).astype(F32)
        w1, w2 = split2(jnp.exp(pred_ref[:, here] + change) * mask)
        first = dot(loads[...], w1, NN)
        second = dot(loads[: 2 * FACT], w2, NN)
        grad = by_load_ref[:, here] - (first[:FACT] + second[:FACT])
        curv = (first[FACT : 2 * FACT] + first[2 * FACT :]) + second[FACT:]
        for z in range(8):
            out[z, :8, here] = grad[8 * z : 8 * (z + 1), :]
            out[z, 8:, here] = curv[8 * z : 8 * (z + 1), :]
        send = pltpu.make_async_copy(
            out.at[:, :, here], out_hbm.at[:, :, here], sent.at[at // CHUNK]
        )
        send.start()
        sends.append(send)
        fact = fact_ref[:, here]
        wide = fact.astype(F32)
        f1, f2 = split2(wide * wide)
        first = dot(jnp.concatenate([fact, f1, f2], axis=0), w1, NT)
        second = dot(jnp.concatenate([fact, f1], axis=0), w2, NT)
        grad = first[:FACT] + second[:FACT]
        curv = (first[FACT : 2 * FACT] + first[2 * FACT :]) + second[FACT:]
        for h in range(2):
            rows = slice(32 * h, 32 * (h + 1))
            if at > 0:
                sums[h, :32, :] -= grad[rows]
                sums[h, 32:, :] += curv[rows]
            else:
                sums[h, :32, :] = by_fact_ref[rows, :] - grad[rows]
                sums[h, 32:, :] = curv[rows]

    beta_out[...] = beta.T
    send = pltpu.make_async_copy(beta_out, beta_hbm, sent.at[cells // CHUNK])
    send.start()
    sends.append(send)
    kept_ref[...] = sums[core_ref[0]]
    given_ref[...] = sums[1 - core_ref[0]]
    for send in sends:
        send.wait()


def update(live, core, steps, pred, design, load, fact, by_load, by_fact):
    genes, cells = pred.shape
    return pl.pallas_call(
        update_kernel,
        in_specs=[smem(), smem()] + [vmem()] * 7,
        out_specs=[hbm(), vmem(), vmem(), hbm()],
        out_shape=[
            pltpu.HBM((8, 16, cells), F32),
            jax.ShapeDtypeStruct((FACT, genes), F32),
            jax.ShapeDtypeStruct((FACT, genes), F32),
            pltpu.HBM((COLS, genes), F32),
        ],
        scratch_shapes=[
            pltpu.VMEM((genes, 6 * COLS), BF16), pltpu.VMEM((3 * FACT, genes), BF16),
            pltpu.VMEM((2, FACT, genes), F32), pltpu.VMEM((8, 16, cells), F32),
            pltpu.VMEM((COLS, genes), F32),
            pltpu.SemaphoreType.DMA((cells // CHUNK + 1,)),
        ],
        compiler_params=params(),
        name="update",
    )(live, core, steps, pred, design, load, fact, by_load, by_fact)


def score_kernel(core_ref, mine_ref, other_ref, out_hbm, sent):
    core = core_ref[0]
    sends = [
        pltpu.make_async_copy(
            ref, out_hbm.at[pl.ds(pl.multiple_of(32 * half, 32), 32), :], sent.at[i]
        )
        for i, (half, ref) in enumerate(((core, mine_ref), (1 - core, other_ref)))
    ]
    for send in sends:
        send.start()
    for send in sends:
        send.wait()


def joined_score(core, mine, other):
    return pl.pallas_call(
        score_kernel,
        in_specs=[smem(), vmem(), vmem()],
        out_specs=hbm(),
        out_shape=pltpu.HBM((FACT, mine.shape[1]), F32),
        scratch_shapes=[pltpu.SemaphoreType.DMA((2,))],
        compiler_params=params(),
        name="joined_score",
    )(core, mine, other)


def factor_kernel(parts_ref, out_hbm, stage, sent):
    total = parts_ref[0]
    for j in range(1, parts_ref.shape[0]):
        total = total + parts_ref[j]
    stage[...] = total[:8, :] / (total[8:, :] + 1.0)
    sends = [
        pltpu.make_async_copy(stage, out_hbm.at[z], sent.at[z]) for z in range(out_hbm.shape[0])
    ]
    for send in sends:
        send.start()
    for send in sends:
        send.wait()


def factor_share(parts):
    peers, _, cells = parts.shape
    return pl.pallas_call(
        factor_kernel,
        in_specs=[vmem()],
        out_specs=hbm(),
        out_shape=pltpu.HBM((peers, 8, cells), F32),
        scratch_shapes=[pltpu.VMEM((8, cells), F32), pltpu.SemaphoreType.DMA((peers,))],
        compiler_params=params(),
        name="factor_share",
    )(parts)


def settle_kernel(value_ref, out_hbm, sent):
    sends = [
        pltpu.make_async_copy(value_ref.at[z], out_hbm.at[z], sent.at[z])
        for z in range(value_ref.shape[0])
    ]
    for send in sends:
        send.start()
    for send in sends:
        send.wait()


def settled(value):
    return pl.pallas_call(
        settle_kernel,
        in_specs=[vmem()],
        out_specs=hbm(),
        out_shape=pltpu.HBM(value.shape, value.dtype),
        scratch_shapes=[pltpu.SemaphoreType.DMA((value.shape[0],))],
        compiler_params=params(),
        name="settled",
    )(value)


def exchange(value, axis, groups=None):
    return lax.all_to_all(
        value, axis, split_axis=0, concat_axis=0, tiled=True, axis_index_groups=groups
    )


def partners(move):
    def index(x, y, core):
        return (x * 4 + y) * 2 + core

    return [
        (index(x, y, core), index(*move(x, y, core)))
        for x in range(4)
        for y in range(4)
        for core in range(2)
    ]


SAME_CORE = [[(4 * x + y) * 2 + core for y in range(4) for x in range(4)] for core in range(2)]
CORE_FIRST = [SAME_CORE[0] + SAME_CORE[1]]
RING = [[3, 4, 2, 5, 1, 6, 0, 7]]
OTHER_CORE = partners(lambda x, y, c: (x, y, 1 - c))
ALONG_X = [partners(lambda x, y, c, k=k: (x ^ k, y, c)) for k in (1, 2, 3)]
ALONG_Y = [partners(lambda x, y, c, k=k: (x, y ^ k, c)) for k in (1, 3)]


def local(
    counts, batch_id, live_cells, knot_bin, depth_frac, cell_covariates,
    coefficients, batch_effect, factors, loadings,
):
    fact, load = factors.T, loadings.T
    tot = exchange(cell_totals(counts, 8), "gene", RING)
    rest, design, score, by_load, by_fact = prepare(
        live_cells, counts, knot_bin[None], depth_frac[None], batch_id[None],
        cell_covariates, coefficients.T, batch_effect.T, load, fact,
    )
    core = (lax.axis_index("cell") % 2)[None]
    pred, kept, given = gram_sums(
        live_cells, core, tot, rest, design, score
    )
    packed = kept + lax.ppermute(given, "cell", OTHER_CORE)
    steps = exchange(solve(exchange(packed, "cell", SAME_CORE)), "cell", CORE_FIRST)
    pieces, kept, given, beta = update(
        live_cells, core, steps.reshape(32, 384), pred, design, load, fact, by_load, by_fact
    )
    arrived = exchange(pieces, "gene", RING)

    value = kept + lax.ppermute(given, "cell", OTHER_CORE)
    near, across, beside = (lax.ppermute(value, "cell", pairs) for pairs in ALONG_X)
    value = (value + near) + (across + beside)
    near = lax.ppermute(value, "cell", ALONG_Y[0])
    shared = factor_share(arrived)
    gathered = settled(exchange(shared, "gene", RING))
    near, _ = lax.optimization_barrier((near, shared))
    value = value + near
    value = value + lax.ppermute(value, "cell", ALONG_Y[1])
    mine = value[:32] / jnp.sqrt(value[32:] + 1.0)
    other = lax.ppermute(mine, "cell", OTHER_CORE)
    score = joined_score(core, mine, other)
    factor_step = gathered.reshape(FACT, -1)
    return beta.T, factor_step.T, score.T


def solution(mesh):
    placed = (
        P("gene", "cell"),
        P("cell"),
        P("cell"),
        P("cell"),
        P("cell"),
        P(None, "cell"),
        P("gene", None),
        P("gene", None),
        P("cell", None),
        P("gene", None),
    )
    return jax.shard_map(
        local,
        mesh=mesh,
        in_specs=placed,
        out_specs=(P("gene", None), P("cell", None), P("gene", None)),
        check_vma=False,
    )
```

```python
import functools

import jax
import jax.numpy as jnp
from jax import lax
from jax.experimental import pallas as pl
from jax.experimental.pallas import tpu as pltpu
from jax.sharding import PartitionSpec as P

GENES = 3072
SPL = 16
COLS = 32
FACT = 64
CHUNK = 256
F32 = jnp.float32
BF16 = jnp.bfloat16
NN = (((1,), (0,)), ((), ()))
NT = (((1,), (1,)), ((), ()))
TN = (((0,), (0,)), ((), ()))
MIB = 1024 * 1024


def dot(a, b, dims):
    return lax.dot_general(a, b, dims, preferred_element_type=F32)


def split2(x):
    hi = x.astype(BF16)
    return hi, (x - hi.astype(F32)).astype(BF16)


def split3(x):
    hi = x.astype(BF16)
    rest = x - hi.astype(F32)
    mid = rest.astype(BF16)
    return hi, mid, (rest - mid.astype(F32)).astype(BF16)


def smem():
    return pl.BlockSpec(memory_space=pltpu.SMEM)


def vmem():
    return pl.BlockSpec(memory_space=pltpu.VMEM)


def hbm():
    return pl.BlockSpec(memory_space=pltpu.HBM)


def params(mib=16):
    return pltpu.CompilerParams(vmem_limit_bytes=mib * MIB)


def totals_kernel(counts_ref, out_ref, rows, stage, arrived, sent):
    blocks, size = rows.shape[0], rows.shape[1]

    def copy(b):
        return pltpu.make_async_copy(
            counts_ref.at[pl.ds(b * size, size), :], rows.at[b], arrived.at[b]
        )

    for b in range(blocks):
        copy(b).start()
    total = jnp.zeros((8, rows.shape[2]), F32)
    for b in range(blocks):
        copy(b).wait()
        part = rows[b, :8, :]
        for i in range(8, size, 8):
            part = part + rows[b, i : i + 8, :]
        total = total + part.astype(F32)
    total = jnp.sum(total, axis=0, keepdims=True)
    for i in range(8):
        stage[i : i + 1, :] = total[:, 128 * i : 128 * (i + 1)]
    sends = [
        pltpu.make_async_copy(stage, out_ref.at[z], sent.at[z]) for z in range(out_ref.shape[0])
    ]
    for send in sends:
        send.start()
    for send in sends:
        send.wait()


def cell_totals(counts, peers):
    genes, cells = counts.shape
    blocks = 12
    return pl.pallas_call(
        totals_kernel,
        in_specs=[hbm()],
        out_specs=hbm(),
        out_shape=pltpu.HBM((peers, 8, 128), F32),
        scratch_shapes=[
            pltpu.VMEM((blocks, genes // blocks, cells), jnp.int32),
            pltpu.VMEM((8, 128), F32),
            pltpu.SemaphoreType.DMA((blocks,)),
            pltpu.SemaphoreType.DMA((peers,)),
        ],
        compiler_params=params(),
        name="cell_totals",
    )(pltpu.with_memory_space_constraint(counts, pltpu.HBM))


def prepare_kernel(
    live_ref, counts_hbm, knot_hbm, frac_hbm, batch_hbm, cov_hbm, coef_hbm, shift_hbm,
    load_hbm, fact_hbm,
    rest_ref, design_ref, score_ref, by_load_ref, by_fact_ref,
    counts_all, knot_all, frac_all, batch_all, cov_all, coef, shift, load, fact_all, arrived,
):
    pairs = (
        (knot_hbm, knot_all), (frac_hbm, frac_all), (batch_hbm, batch_all), (cov_hbm, cov_all),
        (coef_hbm, coef), (shift_hbm, shift), (load_hbm, load), (fact_hbm, fact_all),
    )
    copies = [
        pltpu.make_async_copy(source, target, arrived.at[i])
        for i, (source, target) in enumerate(pairs)
    ]
    cells = rest_ref.shape[1]
    blocks = [
        pltpu.make_async_copy(
            counts_hbm.at[:, pl.ds(at, CHUNK)], counts_all.at[:, pl.ds(at, CHUNK)],
            arrived.at[len(pairs) + at // CHUNK],
        )
        for at in range(0, cells, CHUNK)
    ]
    for copy in copies + blocks:
        copy.start()
    for copy in copies:
        copy.wait()
    c1, c2, c3 = split3(coef[...])
    b1, b2, b3 = split3(shift[...])
    left = jnp.concatenate([c1, c1, c2, c2, c1, c3, b1, b2, b3, load[...]], axis=0)
    score, by_fact = 0.0, 0.0
    for at in range(0, cells, CHUNK):
        here = pl.ds(at, CHUNK)
        knot, frac = knot_all[:, here], frac_all[:, here]
        cov, fact = cov_all[:, here], fact_all[:, here]
        levels = lax.broadcasted_iota(jnp.int32, (SPL, CHUNK), 0)
        hat = jnp.where(levels == knot, 1.0 - frac, 0.0)
        hat = hat + jnp.where(levels == knot + 1, frac, 0.0)
        d1, d2, d3 = split3(jnp.concatenate([hat, cov], axis=0))
        terms = jnp.concatenate([d1, d2, d3], axis=0)
        design_ref[:, here] = terms
        batches = lax.broadcasted_iota(jnp.int32, (64, CHUNK), 0)
        onehot = (batches == batch_all[:, here]).astype(F32).astype(BF16)
        right = jnp.concatenate([d1, d2, d1, d2, d3, d1, onehot, onehot, onehot, fact], axis=0)
        rest_ref[:, here] = dot(left, right, TN)

        blocks[at // CHUNK].wait()
        slot = lax.broadcasted_iota(jnp.int32, (1, CHUNK), 1) + at
        mask = (slot < live_ref[0]).astype(F32)
        counts = (counts_all[:, here].astype(F32) * mask).astype(BF16)
        by_load_ref[:, here] = dot(load[...], counts, NN)
        by_fact = by_fact + dot(fact, counts, NT)
        score = score + dot(counts, terms, NT)
    by_fact_ref[...] = by_fact
    value = score[:, :32] + score[:, 32:64] + score[:, 64:96]
    blank = jnp.zeros((value.shape[0], 96), F32)
    score_ref[...] = jnp.concatenate([blank, value], axis=1)


def prepare(live, counts, knot, frac, batch, cov, coef, shift, load, fact):
    genes, cells = counts.shape
    arrays = [
        pltpu.with_memory_space_constraint(a, pltpu.HBM)
        for a in (counts, knot, frac, batch, cov, coef, shift, load, fact)
    ]
    return pl.pallas_call(
        prepare_kernel,
        in_specs=[smem()] + [hbm()] * len(arrays),
        out_specs=[vmem()] * 5,
        out_shape=[
            jax.ShapeDtypeStruct((genes, cells), F32),
            jax.ShapeDtypeStruct((96, cells), BF16),
            jax.ShapeDtypeStruct((genes, 128), F32),
            jax.ShapeDtypeStruct((FACT, cells), F32),
            jax.ShapeDtypeStruct((FACT, genes), F32),
        ],
        scratch_shapes=[pltpu.VMEM(a.shape, a.dtype) for a in arrays]
        + [pltpu.SemaphoreType.DMA((len(arrays) - 1 + cells // CHUNK,))],
        compiler_params=params(),
        name="prepare",
    )(live, *arrays)


def gram_kernel(
    live_ref, core_ref, tot_ref, rest_ref, design_ref, score_ref,
    pred_ref, kept_ref, given_ref, offset, acc, terms_hi, terms_lo,
):
    total = jnp.sum(tot_ref[...], axis=0)
    value = jnp.log((1.0 + total) / GENES)
    for i in range(8):
        offset[:, 128 * i : 128 * (i + 1)] = value[i : i + 1, :]

    for at in range(0, rest_ref.shape[1], CHUNK):
        here = pl.ds(at, CHUNK)
        hi_ref, lo_ref = terms_hi.at[:, here], terms_lo.at[:, here]

        def put(row, value):
            hi, lo = split2(value)
            hi_ref[row : row + value.shape[0], :] = hi
            lo_ref[row : row + value.shape[0], :] = lo

        d1, d2, d3 = (design_ref[32 * i : 32 * (i + 1), here] for i in range(3))
        design = (d1.astype(F32) + d2.astype(F32)) + d3.astype(F32)
        hat, cov = design[:SPL], design[SPL:]
        put(0, hat * hat)
        put(16, hat * pltpu.roll(hat, SPL - 1, axis=0))
        for p in range(SPL):
            put(32 + 16 * p, hat[p : p + 1, :] * cov)
        low, high = cov[:8], cov[8:]
        for i in range(0, 8, 2):
            for row, left, right in ((288, low, low), (352, low, high), (416, high, high)):
                both = [left[i : i + 1] * right, left[i + 1 : i + 2] * right]
                put(row + 8 * i, jnp.concatenate(both, axis=0))
        put(480, -design)

        pred = rest_ref[:, here] + offset[:, here]
        pred_ref[:, here] = pred
        slot = lax.broadcasted_iota(jnp.int32, (1, CHUNK), 1) + at
        mask = (slot < live_ref[0]).astype(F32)
        w1, w2 = split2(jnp.exp(pred) * mask)
        hi, lo = hi_ref[...], lo_ref[...]
        gram = dot(w1, hi, NT) + dot(w1, lo, NT) + dot(w2, hi, NT)
        for t in range(4):
            part = gram[:, 128 * t : 128 * (t + 1)]
            if at > 0:
                acc[t] += part
            else:
                acc[t] = part + score_ref[...] if t == 3 else part

    core = core_ref[0]
    for chip in range(16):
        for ref, j in ((kept_ref, 16 * core + chip), (given_ref, 16 * (1 - core) + chip)):
            for t in range(4):
                ref[chip, 12 * t : 12 * (t + 1), :] = acc[t, pl.ds(j, 12, stride=32), :]


def gram_sums(live, core, tot, rest, design, score):
    genes, cells = rest.shape
    return pl.pallas_call(
        gram_kernel,
        in_specs=[smem(), smem(), vmem(), vmem(), vmem(), vmem()],
        out_specs=[vmem(), vmem(), vmem()],
        out_shape=[
            jax.ShapeDtypeStruct((genes, cells), F32),
            jax.ShapeDtypeStruct((16, 48, 128), F32),
            jax.ShapeDtypeStruct((16, 48, 128), F32),
        ],
        scratch_shapes=[
            pltpu.VMEM((1, cells), F32), pltpu.VMEM((4, genes, 128), F32),
            pltpu.VMEM((512, cells), BF16), pltpu.VMEM((512, cells), BF16),
        ],
        compiler_params=params(),
        name="gram_sums",
    )(live, core, tot, rest, design, score)


def solve_kernel(parts_ref, out_ref, table):
    total = parts_ref[0]
    for j in range(1, parts_ref.shape[0]):
        total = total + parts_ref[j]
    turned = jnp.concatenate([total, jnp.zeros((80, 128), F32)], axis=0).T
    for t in range(4):
        moved = turned if t == 0 else pltpu.roll(turned, 128 - 12 * t, axis=1)
        table[128 * t : 128 * (t + 1), :] = moved
    row16 = lax.broadcasted_iota(jnp.int32, (SPL, 128), 0)
    row32 = lax.broadcasted_iota(jnp.int32, (COLS, 128), 0)
    diag, near = table[0:16, :] + 1.0, table[16:32, :]
    below = pltpu.roll(near, 1, axis=0)
    system = []
    for j in range(SPL):
        top = jnp.where(row16 == j, diag, 0.0)
        top = jnp.where(row16 == j - 1, near, top)
        top = jnp.where(row16 == j + 1, below, top)
        system.append(jnp.concatenate([top, table[32 + 16 * j : 48 + 16 * j, :]], axis=0))
    for q in range(SPL):
        top = table[pl.ds(32 + q, 16, stride=16), :]
        if q < 8:
            first = table[288 + 8 * q : 296 + 8 * q, :]
            second = table[352 + 8 * q : 360 + 8 * q, :]
        else:
            first = table[pl.ds(344 + q, 8, stride=8), :]
            second = table[352 + 8 * q : 360 + 8 * q, :]
        column = jnp.concatenate([top, first, second], axis=0)
        system.append(jnp.where(row32 == 16 + q, column + 1.0, column))
    rhs = table[480:512, :]
    scale = jnp.zeros((COLS, 128), F32)
    for k in range(COLS):
        column = system[k]
        inverse = 1.0 / column[k : k + 1, :]
        scale = jnp.where(row32 == k, inverse, scale)
        ratio = jnp.where(row32 == k, 0.0, column * inverse)
        touched = [j for j in range(k + 1, COLS) if j >= SPL or j == k + 1]
        for j in touched:
            system[j] = system[j] - ratio * column[j : j + 1, :]
        rhs = rhs - ratio * rhs[k : k + 1, :]
    answer = rhs * scale
    flat = jnp.concatenate([answer, jnp.zeros((96, 128), F32)], axis=0).T
    line = jnp.concatenate([flat[g : g + 1, :COLS] for g in range(12)], axis=1)
    out_ref[...] = jnp.broadcast_to(line[None], out_ref.shape)


def solve(parts):
    return pl.pallas_call(
        solve_kernel,
        in_specs=[vmem()],
        out_specs=vmem(),
        out_shape=jax.ShapeDtypeStruct((32, 1, 384), F32),
        scratch_shapes=[pltpu.VMEM((512, 128), F32)],
        compiler_params=params(),
        name="solve",
    )(parts)


def update_kernel(
    live_ref, core_ref, steps_ref, pred_ref, design_ref, load_ref, fact_ref,
    by_load_ref, by_fact_ref,
    out_hbm, kept_ref, given_ref, beta_hbm, left, loads, sums, out, beta_out, sent,
):
    steps = steps_ref[...]
    beta = jnp.concatenate([steps[:, COLS * g : COLS * (g + 1)] for g in range(12)], axis=0)
    b1, b2, b3 = split3(beta)
    left[...] = jnp.concatenate([b1, b1, b2, b2, b1, b3], axis=1)
    load = load_ref[...]
    wide = load.astype(F32)
    l1, l2 = split2(wide * wide)
    loads[...] = jnp.concatenate([load, l1, l2], axis=0)

    cells = pred_ref.shape[1]
    sends = []
    for at in range(0, cells, CHUNK):
        here = pl.ds(at, CHUNK)
        d1, d2, d3 = (design_ref[32 * i : 32 * (i + 1), here] for i in range(3))
        change = dot(left[...], jnp.concatenate([d1, d2, d1, d2, d3, d1], axis=0), NN)
        slot = lax.broadcasted_iota(jnp.int32, (1, CHUNK), 1) + at
        mask = (slot < live_ref[0]).astype(F32)
        w1, w2 = split2(jnp.exp(pred_ref[:, here] + change) * mask)
        first = dot(loads[...], w1, NN)
        second = dot(loads[: 2 * FACT], w2, NN)
        grad = by_load_ref[:, here] - (first[:FACT] + second[:FACT])
        curv = (first[FACT : 2 * FACT] + first[2 * FACT :]) + second[FACT:]
        for z in range(8):
            out[z, :8, here] = grad[8 * z : 8 * (z + 1), :]
            out[z, 8:, here] = curv[8 * z : 8 * (z + 1), :]
        send = pltpu.make_async_copy(
            out.at[:, :, here], out_hbm.at[:, :, here], sent.at[at // CHUNK]
        )
        send.start()
        sends.append(send)
        fact = fact_ref[:, here]
        wide = fact.astype(F32)
        f1, f2 = split2(wide * wide)
        first = dot(jnp.concatenate([fact, f1, f2], axis=0), w1, NT)
        second = dot(jnp.concatenate([fact, f1], axis=0), w2, NT)
        grad = first[:FACT] + second[:FACT]
        curv = (first[FACT : 2 * FACT] + first[2 * FACT :]) + second[FACT:]
        for h in range(2):
            rows = slice(32 * h, 32 * (h + 1))
            if at > 0:
                sums[h, :32, :] -= grad[rows]
                sums[h, 32:, :] += curv[rows]
            else:
                sums[h, :32, :] = by_fact_ref[rows, :] - grad[rows]
                sums[h, 32:, :] = curv[rows]

    beta_out[...] = beta.T
    send = pltpu.make_async_copy(beta_out, beta_hbm, sent.at[cells // CHUNK])
    send.start()
    sends.append(send)
    kept_ref[...] = sums[core_ref[0]]
    given_ref[...] = sums[1 - core_ref[0]]
    for send in sends:
        send.wait()


def update(live, core, steps, pred, design, load, fact, by_load, by_fact):
    genes, cells = pred.shape
    return pl.pallas_call(
        update_kernel,
        in_specs=[smem(), smem()] + [vmem()] * 7,
        out_specs=[hbm(), vmem(), vmem(), hbm()],
        out_shape=[
            pltpu.HBM((8, 16, cells), F32),
            jax.ShapeDtypeStruct((FACT, genes), F32),
            jax.ShapeDtypeStruct((FACT, genes), F32),
            pltpu.HBM((COLS, genes), F32),
        ],
        scratch_shapes=[
            pltpu.VMEM((genes, 6 * COLS), BF16), pltpu.VMEM((3 * FACT, genes), BF16),
            pltpu.VMEM((2, FACT, genes), F32), pltpu.VMEM((8, 16, cells), F32),
            pltpu.VMEM((COLS, genes), F32),
            pltpu.SemaphoreType.DMA((cells // CHUNK + 1,)),
        ],
        compiler_params=params(),
        name="update",
    )(live, core, steps, pred, design, load, fact, by_load, by_fact)


def score_kernel(core_ref, mine_ref, other_ref, out_hbm, sent):
    core = core_ref[0]
    sends = [
        pltpu.make_async_copy(
            ref, out_hbm.at[pl.ds(pl.multiple_of(32 * half, 32), 32), :], sent.at[i]
        )
        for i, (half, ref) in enumerate(((core, mine_ref), (1 - core, other_ref)))
    ]
    for send in sends:
        send.start()
    for send in sends:
        send.wait()


def joined_score(core, mine, other):
    return pl.pallas_call(
        score_kernel,
        in_specs=[smem(), vmem(), vmem()],
        out_specs=hbm(),
        out_shape=pltpu.HBM((FACT, mine.shape[1]), F32),
        scratch_shapes=[pltpu.SemaphoreType.DMA((2,))],
        compiler_params=params(),
        name="joined_score",
    )(core, mine, other)


def factor_kernel(parts_ref, out_hbm, stage, sent):
    total = parts_ref[0]
    for j in range(1, parts_ref.shape[0]):
        total = total + parts_ref[j]
    stage[...] = total[:8, :] / (total[8:, :] + 1.0)
    sends = [
        pltpu.make_async_copy(stage, out_hbm.at[z], sent.at[z]) for z in range(out_hbm.shape[0])
    ]
    for send in sends:
        send.start()
    for send in sends:
        send.wait()


def factor_share(parts):
    peers, _, cells = parts.shape
    return pl.pallas_call(
        factor_kernel,
        in_specs=[vmem()],
        out_specs=hbm(),
        out_shape=pltpu.HBM((peers, 8, cells), F32),
        scratch_shapes=[pltpu.VMEM((8, cells), F32), pltpu.SemaphoreType.DMA((peers,))],
        compiler_params=params(),
        name="factor_share",
    )(parts)


def settle_kernel(value_ref, out_hbm, sent):
    sends = [
        pltpu.make_async_copy(value_ref.at[z], out_hbm.at[z], sent.at[z])
        for z in range(value_ref.shape[0])
    ]
    for send in sends:
        send.start()
    for send in sends:
        send.wait()


def settled(value):
    return pl.pallas_call(
        settle_kernel,
        in_specs=[vmem()],
        out_specs=hbm(),
        out_shape=pltpu.HBM(value.shape, value.dtype),
        scratch_shapes=[pltpu.SemaphoreType.DMA((value.shape[0],))],
        compiler_params=params(),
        name="settled",
    )(value)


def exchange(value, axis, groups=None):
    return lax.all_to_all(
        value, axis, split_axis=0, concat_axis=0, tiled=True, axis_index_groups=groups
    )


def partners(move):
    def index(x, y, core):
        return (x * 4 + y) * 2 + core

    return [
        (index(x, y, core), index(*move(x, y, core)))
        for x in range(4)
        for y in range(4)
        for core in range(2)
    ]


def around(at, size):
    return [min((i - at) % size, (at - i) % size) for i in range(size)]


def nearest_first(x, y):
    far_x, far_y = around(x, 4), around(y, 4)
    chips = [(i, j) for i in range(4) for j in range(4)]
    return sorted(chips, key=lambda chip: far_x[chip[0]] + far_y[chip[1]])


FIRST = (3, 2, 5)
SAME_CORE = [[(4 * x + y) * 2 + core for x, y in nearest_first(*FIRST[:2])] for core in range(2)]
CORE_FIRST = [SAME_CORE[0] + SAME_CORE[1]]
RING = [sorted(range(8), key=around(FIRST[2], 8).__getitem__)]
OTHER_CORE = partners(lambda x, y, c: (x, y, 1 - c))
ALONG_X = [partners(lambda x, y, c, k=k: (x ^ k, y, c)) for k in (1, 2, 3)]
ALONG_Y = [partners(lambda x, y, c, k=k: (x, y ^ k, c)) for k in (1, 3)]


def local(
    counts, batch_id, live_cells, knot_bin, depth_frac, cell_covariates,
    coefficients, batch_effect, factors, loadings,
):
    fact, load = factors.T, loadings.T
    tot = exchange(cell_totals(counts, 8), "gene", RING)
    rest, design, score, by_load, by_fact = prepare(
        live_cells, counts, knot_bin[None], depth_frac[None], batch_id[None],
        cell_covariates, coefficients.T, batch_effect.T, load, fact,
    )
    core = (lax.axis_index("cell") % 2)[None]
    pred, kept, given = gram_sums(
        live_cells, core, tot, rest, design, score
    )
    packed = kept + lax.ppermute(given, "cell", OTHER_CORE)
    steps = exchange(solve(exchange(packed, "cell", SAME_CORE)), "cell", CORE_FIRST)
    pieces, kept, given, beta = update(
        live_cells, core, steps.reshape(32, 384), pred, design, load, fact, by_load, by_fact
    )
    arrived = exchange(pieces, "gene", RING)

    value = kept + lax.ppermute(given, "cell", OTHER_CORE)
    near, across, beside = (lax.ppermute(value, "cell", pairs) for pairs in ALONG_X)
    value = (value + near) + (across + beside)
    near = lax.ppermute(value, "cell", ALONG_Y[0])
    shared = factor_share(arrived)
    gathered = settled(exchange(shared, "gene", RING))
    near, _ = lax.optimization_barrier((near, shared))
    value = value + near
    value = value + lax.ppermute(value, "cell", ALONG_Y[1])
    mine = value[:32] / jnp.sqrt(value[32:] + 1.0)
    other = lax.ppermute(mine, "cell", OTHER_CORE)
    score = joined_score(core, mine, other)
    factor_step = gathered.reshape(FACT, -1)
    return beta.T, factor_step.T, score.T


def solution(mesh):
    placed = (
        P("gene", "cell"),
        P("cell"),
        P("cell"),
        P("cell"),
        P("cell"),
        P(None, "cell"),
        P("gene", None),
        P("gene", None),
        P("cell", None),
        P("gene", None),
    )
    return jax.shard_map(
        local,
        mesh=mesh,
        in_specs=placed,
        out_specs=(P("gene", None), P("cell", None), P("gene", None)),
        check_vma=False,
    )
```

```python
import functools

import jax
import jax.numpy as jnp
from jax import lax
from jax.experimental import pallas as pl
from jax.experimental.pallas import tpu as pltpu
from jax.sharding import PartitionSpec as P

GENES = 3072
SPL = 16
COLS = 32
FACT = 64
CHUNK = 256
F32 = jnp.float32
BF16 = jnp.bfloat16
NN = (((1,), (0,)), ((), ()))
NT = (((1,), (1,)), ((), ()))
TN = (((0,), (0,)), ((), ()))
MIB = 1024 * 1024


def dot(a, b, dims):
    return lax.dot_general(a, b, dims, preferred_element_type=F32)


def split2(x):
    hi = x.astype(BF16)
    return hi, (x - hi.astype(F32)).astype(BF16)


def split3(x):
    hi = x.astype(BF16)
    rest = x - hi.astype(F32)
    mid = rest.astype(BF16)
    return hi, mid, (rest - mid.astype(F32)).astype(BF16)


def smem():
    return pl.BlockSpec(memory_space=pltpu.SMEM)


def vmem():
    return pl.BlockSpec(memory_space=pltpu.VMEM)


def hbm():
    return pl.BlockSpec(memory_space=pltpu.HBM)


def params(mib=16):
    return pltpu.CompilerParams(vmem_limit_bytes=mib * MIB)


def totals_kernel(counts_ref, out_ref, rows, stage, arrived, sent):
    blocks, size = rows.shape[0], rows.shape[1]

    def copy(b):
        return pltpu.make_async_copy(
            counts_ref.at[pl.ds(b * size, size), :], rows.at[b], arrived.at[b]
        )

    for b in range(blocks):
        copy(b).start()
    total = jnp.zeros((8, rows.shape[2]), F32)
    for b in range(blocks):
        copy(b).wait()
        part = rows[b, :8, :]
        for i in range(8, size, 8):
            part = part + rows[b, i : i + 8, :]
        total = total + part.astype(F32)
    total = jnp.sum(total, axis=0, keepdims=True)
    for i in range(8):
        stage[i : i + 1, :] = total[:, 128 * i : 128 * (i + 1)]
    sends = [
        pltpu.make_async_copy(stage, out_ref.at[z], sent.at[z]) for z in range(out_ref.shape[0])
    ]
    for send in sends:
        send.start()
    for send in sends:
        send.wait()


def cell_totals(counts, peers):
    genes, cells = counts.shape
    blocks = 12
    return pl.pallas_call(
        totals_kernel,
        in_specs=[hbm()],
        out_specs=hbm(),
        out_shape=pltpu.HBM((peers, 8, 128), F32),
        scratch_shapes=[
            pltpu.VMEM((blocks, genes // blocks, cells), jnp.int32),
            pltpu.VMEM((8, 128), F32),
            pltpu.SemaphoreType.DMA((blocks,)),
            pltpu.SemaphoreType.DMA((peers,)),
        ],
        compiler_params=params(),
        name="cell_totals",
    )(pltpu.with_memory_space_constraint(counts, pltpu.HBM))


def prepare_kernel(
    live_ref, counts_hbm, knot_hbm, frac_hbm, batch_hbm, cov_hbm, coef_hbm, shift_hbm,
    load_hbm, fact_hbm,
    rest_ref, design_ref, score_ref, by_load_ref, by_fact_ref,
    counts_all, knot_all, frac_all, batch_all, cov_all, coef, shift, load, fact_all, arrived,
):
    pairs = (
        (knot_hbm, knot_all), (frac_hbm, frac_all), (batch_hbm, batch_all), (cov_hbm, cov_all),
        (coef_hbm, coef), (shift_hbm, shift), (load_hbm, load), (fact_hbm, fact_all),
    )
    copies = [
        pltpu.make_async_copy(source, target, arrived.at[i])
        for i, (source, target) in enumerate(pairs)
    ]
    cells = rest_ref.shape[1]
    blocks = [
        pltpu.make_async_copy(
            counts_hbm.at[:, pl.ds(at, CHUNK)], counts_all.at[:, pl.ds(at, CHUNK)],
            arrived.at[len(pairs) + at // CHUNK],
        )
        for at in range(0, cells, CHUNK)
    ]
    for copy in copies + blocks:
        copy.start()
    for copy in copies:
        copy.wait()
    c1, c2, c3 = split3(coef[...])
    b1, b2, b3 = split3(shift[...])
    left = jnp.concatenate([c1, c1, c2, c2, c1, c3, b1, b2, b3, load[...]], axis=0)
    score, by_fact = 0.0, 0.0
    for at in range(0, cells, CHUNK):
        here = pl.ds(at, CHUNK)
        knot, frac = knot_all[:, here], frac_all[:, here]
        cov, fact = cov_all[:, here], fact_all[:, here]
        levels = lax.broadcasted_iota(jnp.int32, (SPL, CHUNK), 0)
        hat = jnp.where(levels == knot, 1.0 - frac, 0.0)
        hat = hat + jnp.where(levels == knot + 1, frac, 0.0)
        d1, d2, d3 = split3(jnp.concatenate([hat, cov], axis=0))
        terms = jnp.concatenate([d1, d2, d3], axis=0)
        design_ref[:, here] = terms
        batches = lax.broadcasted_iota(jnp.int32, (64, CHUNK), 0)
        onehot = (batches == batch_all[:, here]).astype(F32).astype(BF16)
        right = jnp.concatenate([d1, d2, d1, d2, d3, d1, onehot, onehot, onehot, fact], axis=0)
        rest_ref[:, here] = dot(left, right, TN)

        blocks[at // CHUNK].wait()
        slot = lax.broadcasted_iota(jnp.int32, (1, CHUNK), 1) + at
        mask = (slot < live_ref[0]).astype(F32)
        counts = (counts_all[:, here].astype(F32) * mask).astype(BF16)
        by_load_ref[:, here] = dot(load[...], counts, NN)
        by_fact = by_fact + dot(fact, counts, NT)
        score = score + dot(counts, terms, NT)
    by_fact_ref[...] = by_fact
    value = score[:, :32] + score[:, 32:64] + score[:, 64:96]
    blank = jnp.zeros((value.shape[0], 96), F32)
    score_ref[...] = jnp.concatenate([blank, value], axis=1)


def prepare(live, counts, knot, frac, batch, cov, coef, shift, load, fact):
    genes, cells = counts.shape
    arrays = [
        pltpu.with_memory_space_constraint(a, pltpu.HBM)
        for a in (counts, knot, frac, batch, cov, coef, shift, load, fact)
    ]
    return pl.pallas_call(
        prepare_kernel,
        in_specs=[smem()] + [hbm()] * len(arrays),
        out_specs=[vmem()] * 5,
        out_shape=[
            jax.ShapeDtypeStruct((genes, cells), F32),
            jax.ShapeDtypeStruct((96, cells), BF16),
            jax.ShapeDtypeStruct((genes, 128), F32),
            jax.ShapeDtypeStruct((FACT, cells), F32),
            jax.ShapeDtypeStruct((FACT, genes), F32),
        ],
        scratch_shapes=[pltpu.VMEM(a.shape, a.dtype) for a in arrays]
        + [pltpu.SemaphoreType.DMA((len(arrays) - 1 + cells // CHUNK,))],
        compiler_params=params(),
        name="prepare",
    )(live, *arrays)


def gram_kernel(
    live_ref, core_ref, tot_ref, rest_ref, design_ref, score_ref,
    pred_ref, kept_ref, given_ref, offset, acc, terms_hi, terms_lo,
):
    total = jnp.sum(tot_ref[...], axis=0)
    value = jnp.log((1.0 + total) / GENES)
    for i in range(8):
        offset[:, 128 * i : 128 * (i + 1)] = value[i : i + 1, :]

    for at in range(0, rest_ref.shape[1], CHUNK):
        here = pl.ds(at, CHUNK)
        hi_ref, lo_ref = terms_hi.at[:, here], terms_lo.at[:, here]

        def put(row, value):
            hi, lo = split2(value)
            hi_ref[row : row + value.shape[0], :] = hi
            lo_ref[row : row + value.shape[0], :] = lo

        d1, d2, d3 = (design_ref[32 * i : 32 * (i + 1), here] for i in range(3))
        design = (d1.astype(F32) + d2.astype(F32)) + d3.astype(F32)
        hat, cov = design[:SPL], design[SPL:]
        put(0, hat * hat)
        put(16, hat * pltpu.roll(hat, SPL - 1, axis=0))
        for p in range(SPL):
            put(32 + 16 * p, hat[p : p + 1, :] * cov)
        low, high = cov[:8], cov[8:]
        for i in range(0, 8, 2):
            for row, left, right in ((288, low, low), (352, low, high), (416, high, high)):
                both = [left[i : i + 1] * right, left[i + 1 : i + 2] * right]
                put(row + 8 * i, jnp.concatenate(both, axis=0))
        put(480, -design)

        pred = rest_ref[:, here] + offset[:, here]
        pred_ref[:, here] = pred
        slot = lax.broadcasted_iota(jnp.int32, (1, CHUNK), 1) + at
        mask = (slot < live_ref[0]).astype(F32)
        w1, w2 = split2(jnp.exp(pred) * mask)
        hi, lo = hi_ref[...], lo_ref[...]
        gram = dot(w1, hi, NT) + dot(w1, lo, NT) + dot(w2, hi, NT)
        for t in range(4):
            part = gram[:, 128 * t : 128 * (t + 1)]
            if at > 0:
                acc[t] += part
            else:
                acc[t] = part + score_ref[...] if t == 3 else part

    core = core_ref[0]
    for chip in range(16):
        for ref, j in ((kept_ref, 16 * core + chip), (given_ref, 16 * (1 - core) + chip)):
            for t in range(4):
                ref[chip, 12 * t : 12 * (t + 1), :] = acc[t, pl.ds(j, 12, stride=32), :]


def gram_sums(live, core, tot, rest, design, score):
    genes, cells = rest.shape
    return pl.pallas_call(
        gram_kernel,
        in_specs=[smem(), smem(), vmem(), vmem(), vmem(), vmem()],
        out_specs=[vmem(), vmem(), vmem()],
        out_shape=[
            jax.ShapeDtypeStruct((genes, cells), F32),
            jax.ShapeDtypeStruct((16, 48, 128), F32),
            jax.ShapeDtypeStruct((16, 48, 128), F32),
        ],
        scratch_shapes=[
            pltpu.VMEM((1, cells), F32), pltpu.VMEM((4, genes, 128), F32),
            pltpu.VMEM((512, cells), BF16), pltpu.VMEM((512, cells), BF16),
        ],
        compiler_params=params(),
        name="gram_sums",
    )(live, core, tot, rest, design, score)


def solve_kernel(parts_ref, out_ref, table):
    total = parts_ref[0]
    for j in range(1, parts_ref.shape[0]):
        total = total + parts_ref[j]
    turned = jnp.concatenate([total, jnp.zeros((80, 128), F32)], axis=0).T
    for t in range(4):
        moved = turned if t == 0 else pltpu.roll(turned, 128 - 12 * t, axis=1)
        table[128 * t : 128 * (t + 1), :] = moved
    row16 = lax.broadcasted_iota(jnp.int32, (SPL, 128), 0)
    row32 = lax.broadcasted_iota(jnp.int32, (COLS, 128), 0)
    diag, near = table[0:16, :] + 1.0, table[16:32, :]
    below = pltpu.roll(near, 1, axis=0)
    system = []
    for j in range(SPL):
        top = jnp.where(row16 == j, diag, 0.0)
        top = jnp.where(row16 == j - 1, near, top)
        top = jnp.where(row16 == j + 1, below, top)
        system.append(jnp.concatenate([top, table[32 + 16 * j : 48 + 16 * j, :]], axis=0))
    for q in range(SPL):
        top = table[pl.ds(32 + q, 16, stride=16), :]
        if q < 8:
            first = table[288 + 8 * q : 296 + 8 * q, :]
            second = table[352 + 8 * q : 360 + 8 * q, :]
        else:
            first = table[pl.ds(344 + q, 8, stride=8), :]
            second = table[352 + 8 * q : 360 + 8 * q, :]
        column = jnp.concatenate([top, first, second], axis=0)
        system.append(jnp.where(row32 == 16 + q, column + 1.0, column))
    rhs = table[480:512, :]
    scale = jnp.zeros((COLS, 128), F32)
    for k in range(COLS):
        column = system[k]
        inverse = 1.0 / column[k : k + 1, :]
        scale = jnp.where(row32 == k, inverse, scale)
        ratio = jnp.where(row32 == k, 0.0, column * inverse)
        touched = [j for j in range(k + 1, COLS) if j >= SPL or j == k + 1]
        for j in touched:
            system[j] = system[j] - ratio * column[j : j + 1, :]
        rhs = rhs - ratio * rhs[k : k + 1, :]
    answer = rhs * scale
    flat = jnp.concatenate([answer, jnp.zeros((96, 128), F32)], axis=0).T
    line = jnp.concatenate([flat[g : g + 1, :COLS] for g in range(12)], axis=1)
    out_ref[...] = jnp.broadcast_to(line[None], out_ref.shape)


def solve(parts):
    return pl.pallas_call(
        solve_kernel,
        in_specs=[vmem()],
        out_specs=vmem(),
        out_shape=jax.ShapeDtypeStruct((32, 1, 384), F32),
        scratch_shapes=[pltpu.VMEM((512, 128), F32)],
        compiler_params=params(),
        name="solve",
    )(parts)


def update_kernel(
    live_ref, core_ref, steps_ref, pred_ref, design_ref, load_ref, fact_ref,
    by_load_ref, by_fact_ref,
    out_hbm, kept_ref, given_ref, beta_hbm, left, loads, sums, out, beta_out, sent,
):
    steps = steps_ref[...]
    beta = jnp.concatenate([steps[:, COLS * g : COLS * (g + 1)] for g in range(12)], axis=0)
    b1, b2, b3 = split3(beta)
    left[...] = jnp.concatenate([b1, b1, b2, b2, b1, b3], axis=1)
    load = load_ref[...]
    wide = load.astype(F32)
    l1, l2 = split2(wide * wide)
    loads[...] = jnp.concatenate([load, l1, l2], axis=0)

    cells = pred_ref.shape[1]
    sends = []
    for at in range(0, cells, CHUNK):
        here = pl.ds(at, CHUNK)
        d1, d2, d3 = (design_ref[32 * i : 32 * (i + 1), here] for i in range(3))
        change = dot(left[...], jnp.concatenate([d1, d2, d1, d2, d3, d1], axis=0), NN)
        slot = lax.broadcasted_iota(jnp.int32, (1, CHUNK), 1) + at
        mask = (slot < live_ref[0]).astype(F32)
        w1, w2 = split2(jnp.exp(pred_ref[:, here] + change) * mask)
        first = dot(loads[...], w1, NN)
        second = dot(loads[: 2 * FACT], w2, NN)
        grad = by_load_ref[:, here] - (first[:FACT] + second[:FACT])
        curv = (first[FACT : 2 * FACT] + first[2 * FACT :]) + second[FACT:]
        for z in range(8):
            out[z, :8, here] = grad[8 * z : 8 * (z + 1), :]
            out[z, 8:, here] = curv[8 * z : 8 * (z + 1), :]
        send = pltpu.make_async_copy(
            out.at[:, :, here], out_hbm.at[:, :, here], sent.at[at // CHUNK]
        )
        send.start()
        sends.append(send)
        fact = fact_ref[:, here]
        wide = fact.astype(F32)
        f1, f2 = split2(wide * wide)
        first = dot(jnp.concatenate([fact, f1, f2], axis=0), w1, NT)
        second = dot(jnp.concatenate([fact, f1], axis=0), w2, NT)
        grad = first[:FACT] + second[:FACT]
        curv = (first[FACT : 2 * FACT] + first[2 * FACT :]) + second[FACT:]
        for h in range(2):
            rows = slice(32 * h, 32 * (h + 1))
            if at > 0:
                sums[h, :32, :] -= grad[rows]
                sums[h, 32:, :] += curv[rows]
            else:
                sums[h, :32, :] = by_fact_ref[rows, :] - grad[rows]
                sums[h, 32:, :] = curv[rows]

    beta_out[...] = beta.T
    send = pltpu.make_async_copy(beta_out, beta_hbm, sent.at[cells // CHUNK])
    send.start()
    sends.append(send)
    kept_ref[...] = sums[core_ref[0]]
    given_ref[...] = sums[1 - core_ref[0]]
    for send in sends:
        send.wait()


def update(live, core, steps, pred, design, load, fact, by_load, by_fact):
    genes, cells = pred.shape
    return pl.pallas_call(
        update_kernel,
        in_specs=[smem(), smem()] + [vmem()] * 7,
        out_specs=[hbm(), vmem(), vmem(), hbm()],
        out_shape=[
            pltpu.HBM((8, 16, cells), F32),
            jax.ShapeDtypeStruct((FACT, genes), F32),
            jax.ShapeDtypeStruct((FACT, genes), F32),
            pltpu.HBM((COLS, genes), F32),
        ],
        scratch_shapes=[
            pltpu.VMEM((genes, 6 * COLS), BF16), pltpu.VMEM((3 * FACT, genes), BF16),
            pltpu.VMEM((2, FACT, genes), F32), pltpu.VMEM((8, 16, cells), F32),
            pltpu.VMEM((COLS, genes), F32),
            pltpu.SemaphoreType.DMA((cells // CHUNK + 1,)),
        ],
        compiler_params=params(),
        name="update",
    )(live, core, steps, pred, design, load, fact, by_load, by_fact)


def score_kernel(core_ref, mine_ref, other_ref, out_hbm, sent):
    core = core_ref[0]
    sends = [
        pltpu.make_async_copy(
            ref, out_hbm.at[pl.ds(pl.multiple_of(32 * half, 32), 32), :], sent.at[i]
        )
        for i, (half, ref) in enumerate(((core, mine_ref), (1 - core, other_ref)))
    ]
    for send in sends:
        send.start()
    for send in sends:
        send.wait()


def joined_score(core, mine, other):
    return pl.pallas_call(
        score_kernel,
        in_specs=[smem(), vmem(), vmem()],
        out_specs=hbm(),
        out_shape=pltpu.HBM((FACT, mine.shape[1]), F32),
        scratch_shapes=[pltpu.SemaphoreType.DMA((2,))],
        compiler_params=params(),
        name="joined_score",
    )(core, mine, other)


def factor_kernel(parts_ref, out_hbm, stage, sent):
    total = parts_ref[0]
    for j in range(1, parts_ref.shape[0]):
        total = total + parts_ref[j]
    stage[...] = total[:8, :] / (total[8:, :] + 1.0)
    sends = [
        pltpu.make_async_copy(stage, out_hbm.at[z], sent.at[z]) for z in range(out_hbm.shape[0])
    ]
    for send in sends:
        send.start()
    for send in sends:
        send.wait()


def factor_share(parts):
    peers, _, cells = parts.shape
    return pl.pallas_call(
        factor_kernel,
        in_specs=[vmem()],
        out_specs=hbm(),
        out_shape=pltpu.HBM((peers, 8, cells), F32),
        scratch_shapes=[pltpu.VMEM((8, cells), F32), pltpu.SemaphoreType.DMA((peers,))],
        compiler_params=params(),
        name="factor_share",
    )(parts)


def settle_kernel(value_ref, out_hbm, sent):
    sends = [
        pltpu.make_async_copy(value_ref.at[z], out_hbm.at[z], sent.at[z])
        for z in range(value_ref.shape[0])
    ]
    for send in sends:
        send.start()
    for send in sends:
        send.wait()


def settled(value):
    return pl.pallas_call(
        settle_kernel,
        in_specs=[vmem()],
        out_specs=hbm(),
        out_shape=pltpu.HBM(value.shape, value.dtype),
        scratch_shapes=[pltpu.SemaphoreType.DMA((value.shape[0],))],
        compiler_params=params(),
        name="settled",
    )(value)


def exchange(value, axis, groups=None):
    return lax.all_to_all(
        value, axis, split_axis=0, concat_axis=0, tiled=True, axis_index_groups=groups
    )


def partners(move):
    def index(x, y, core):
        return (x * 4 + y) * 2 + core

    return [
        (index(x, y, core), index(*move(x, y, core)))
        for x in range(4)
        for y in range(4)
        for core in range(2)
    ]


def around(at, size):
    return [min((i - at) % size, (at - i) % size) for i in range(size)]


def nearest_first(x, y):
    far_x, far_y = around(x, 4), around(y, 4)
    chips = [(i, j) for i in range(4) for j in range(4)]
    return sorted(chips, key=lambda chip: far_x[chip[0]] + far_y[chip[1]])


FIRST = (3, 2, 5)
SAME_CORE = [[(4 * x + y) * 2 + core for x, y in nearest_first(*FIRST[:2])] for core in range(2)]
CORE_FIRST = [SAME_CORE[0] + SAME_CORE[1]]
RING = [sorted(range(8), key=around(FIRST[2], 8).__getitem__)]
OTHER_CORE = partners(lambda x, y, c: (x, y, 1 - c))
ALONG_X = [partners(lambda x, y, c, k=k: (x ^ k, y, c)) for k in (1, 2, 3)]
ALONG_Y = [partners(lambda x, y, c, k=k: (x, y ^ k, c)) for k in (1, 2, 3)]


def local(
    counts, batch_id, live_cells, knot_bin, depth_frac, cell_covariates,
    coefficients, batch_effect, factors, loadings,
):
    fact, load = factors.T, loadings.T
    tot = exchange(cell_totals(counts, 8), "gene", RING)
    rest, design, score, by_load, by_fact = prepare(
        live_cells, counts, knot_bin[None], depth_frac[None], batch_id[None],
        cell_covariates, coefficients.T, batch_effect.T, load, fact,
    )
    core = (lax.axis_index("cell") % 2)[None]
    pred, kept, given = gram_sums(
        live_cells, core, tot, rest, design, score
    )
    packed = kept + lax.ppermute(given, "cell", OTHER_CORE)
    steps = exchange(solve(exchange(packed, "cell", SAME_CORE)), "cell", CORE_FIRST)
    pieces, kept, given, beta = update(
        live_cells, core, steps.reshape(32, 384), pred, design, load, fact, by_load, by_fact
    )
    arrived = exchange(pieces, "gene", RING)

    value = kept + lax.ppermute(given, "cell", OTHER_CORE)
    for moves in (ALONG_X, ALONG_Y):
        near, across, beside = (lax.ppermute(value, "cell", pairs) for pairs in moves)
        value = (value + near) + (across + beside)
    gathered = settled(exchange(factor_share(arrived), "gene", RING))
    mine = value[:32] / jnp.sqrt(value[32:] + 1.0)
    other = lax.ppermute(mine, "cell", OTHER_CORE)
    score = joined_score(core, mine, other)
    factor_step = gathered.reshape(FACT, -1)
    return beta.T, factor_step.T, score.T


def solution(mesh):
    placed = (
        P("gene", "cell"),
        P("cell"),
        P("cell"),
        P("cell"),
        P("cell"),
        P(None, "cell"),
        P("gene", None),
        P("gene", None),
        P("cell", None),
        P("gene", None),
    )
    return jax.shard_map(
        local,
        mesh=mesh,
        in_specs=placed,
        out_specs=(P("gene", None), P("cell", None), P("gene", None)),
        check_vma=False,
    )
```

```python
import functools

import jax
import jax.numpy as jnp
from jax import lax
from jax.experimental import pallas as pl
from jax.experimental.pallas import tpu as pltpu
from jax.sharding import PartitionSpec as P

GENES = 3072
SPL = 16
COLS = 32
FACT = 64
CHUNK = 256
F32 = jnp.float32
BF16 = jnp.bfloat16
NN = (((1,), (0,)), ((), ()))
NT = (((1,), (1,)), ((), ()))
TN = (((0,), (0,)), ((), ()))
MIB = 1024 * 1024


def dot(a, b, dims):
    return lax.dot_general(a, b, dims, preferred_element_type=F32)


def split2(x):
    hi = x.astype(BF16)
    return hi, (x - hi.astype(F32)).astype(BF16)


def split3(x):
    hi = x.astype(BF16)
    rest = x - hi.astype(F32)
    mid = rest.astype(BF16)
    return hi, mid, (rest - mid.astype(F32)).astype(BF16)


def smem():
    return pl.BlockSpec(memory_space=pltpu.SMEM)


def vmem():
    return pl.BlockSpec(memory_space=pltpu.VMEM)


def hbm():
    return pl.BlockSpec(memory_space=pltpu.HBM)


def params(mib=16):
    return pltpu.CompilerParams(vmem_limit_bytes=mib * MIB)


def totals_kernel(counts_ref, out_ref, rows, stage, arrived, sent):
    blocks, size = rows.shape[0], rows.shape[1]

    def copy(b):
        return pltpu.make_async_copy(
            counts_ref.at[pl.ds(b * size, size), :], rows.at[b], arrived.at[b]
        )

    for b in range(blocks):
        copy(b).start()
    total = jnp.zeros((8, rows.shape[2]), F32)
    for b in range(blocks):
        copy(b).wait()
        part = rows[b, :8, :]
        for i in range(8, size, 8):
            part = part + rows[b, i : i + 8, :]
        total = total + part.astype(F32)
    total = jnp.sum(total, axis=0, keepdims=True)
    for i in range(8):
        stage[i : i + 1, :] = total[:, 128 * i : 128 * (i + 1)]
    sends = [
        pltpu.make_async_copy(stage, out_ref.at[z], sent.at[z]) for z in range(out_ref.shape[0])
    ]
    for send in sends:
        send.start()
    for send in sends:
        send.wait()


def cell_totals(counts, peers):
    genes, cells = counts.shape
    blocks = 12
    return pl.pallas_call(
        totals_kernel,
        in_specs=[hbm()],
        out_specs=hbm(),
        out_shape=pltpu.HBM((peers, 8, 128), F32),
        scratch_shapes=[
            pltpu.VMEM((blocks, genes // blocks, cells), jnp.int32),
            pltpu.VMEM((8, 128), F32),
            pltpu.SemaphoreType.DMA((blocks,)),
            pltpu.SemaphoreType.DMA((peers,)),
        ],
        compiler_params=params(),
        name="cell_totals",
    )(pltpu.with_memory_space_constraint(counts, pltpu.HBM))


def prepare_kernel(
    live_ref, counts_hbm, knot_hbm, frac_hbm, batch_hbm, cov_hbm, coef_hbm, shift_hbm,
    load_hbm, fact_hbm,
    rest_ref, design_ref, score_ref, by_load_ref, by_fact_ref,
    counts_all, knot_all, frac_all, batch_all, cov_all, coef, shift, load, fact_all, arrived,
):
    pairs = (
        (knot_hbm, knot_all), (frac_hbm, frac_all), (batch_hbm, batch_all), (cov_hbm, cov_all),
        (coef_hbm, coef), (shift_hbm, shift), (load_hbm, load), (fact_hbm, fact_all),
    )
    copies = [
        pltpu.make_async_copy(source, target, arrived.at[i])
        for i, (source, target) in enumerate(pairs)
    ]
    cells = rest_ref.shape[1]
    blocks = [
        pltpu.make_async_copy(
            counts_hbm.at[:, pl.ds(at, CHUNK)], counts_all.at[:, pl.ds(at, CHUNK)],
            arrived.at[len(pairs) + at // CHUNK],
        )
        for at in range(0, cells, CHUNK)
    ]
    for copy in copies + blocks:
        copy.start()
    for copy in copies:
        copy.wait()
    c1, c2, c3 = split3(coef[...])
    b1, b2, b3 = split3(shift[...])
    left = jnp.concatenate([c1, c1, c2, c2, c1, c3, b1, b2, b3, load[...]], axis=0)
    score, by_fact = 0.0, 0.0
    for at in range(0, cells, CHUNK):
        here = pl.ds(at, CHUNK)
        knot, frac = knot_all[:, here], frac_all[:, here]
        cov, fact = cov_all[:, here], fact_all[:, here]
        levels = lax.broadcasted_iota(jnp.int32, (SPL, CHUNK), 0)
        hat = jnp.where(levels == knot, 1.0 - frac, 0.0)
        hat = hat + jnp.where(levels == knot + 1, frac, 0.0)
        d1, d2, d3 = split3(jnp.concatenate([hat, cov], axis=0))
        terms = jnp.concatenate([d1, d2, d3], axis=0)
        design_ref[:, here] = terms
        batches = lax.broadcasted_iota(jnp.int32, (64, CHUNK), 0)
        onehot = (batches == batch_all[:, here]).astype(F32).astype(BF16)
        right = jnp.concatenate([d1, d2, d1, d2, d3, d1, onehot, onehot, onehot, fact], axis=0)
        rest_ref[:, here] = dot(left, right, TN)

        blocks[at // CHUNK].wait()
        slot = lax.broadcasted_iota(jnp.int32, (1, CHUNK), 1) + at
        mask = (slot < live_ref[0]).astype(F32)
        counts = (counts_all[:, here].astype(F32) * mask).astype(BF16)
        by_load_ref[:, here] = dot(load[...], counts, NN)
        by_fact = by_fact + dot(fact, counts, NT)
        score = score + dot(counts, terms, NT)
    by_fact_ref[...] = by_fact
    value = score[:, :32] + score[:, 32:64] + score[:, 64:96]
    blank = jnp.zeros((value.shape[0], 96), F32)
    score_ref[...] = jnp.concatenate([blank, value], axis=1)


def prepare(live, counts, knot, frac, batch, cov, coef, shift, load, fact):
    genes, cells = counts.shape
    arrays = [
        pltpu.with_memory_space_constraint(a, pltpu.HBM)
        for a in (counts, knot, frac, batch, cov, coef, shift, load, fact)
    ]
    return pl.pallas_call(
        prepare_kernel,
        in_specs=[smem()] + [hbm()] * len(arrays),
        out_specs=[vmem()] * 5,
        out_shape=[
            jax.ShapeDtypeStruct((genes, cells), F32),
            jax.ShapeDtypeStruct((96, cells), BF16),
            jax.ShapeDtypeStruct((genes, 128), F32),
            jax.ShapeDtypeStruct((FACT, cells), F32),
            jax.ShapeDtypeStruct((FACT, genes), F32),
        ],
        scratch_shapes=[pltpu.VMEM(a.shape, a.dtype) for a in arrays]
        + [pltpu.SemaphoreType.DMA((len(arrays) - 1 + cells // CHUNK,))],
        compiler_params=params(),
        name="prepare",
    )(live, *arrays)


def gram_kernel(
    live_ref, core_ref, tot_ref, rest_ref, design_ref, score_ref,
    pred_ref, kept_ref, given_ref, offset, acc, terms_hi, terms_lo,
):
    total = jnp.sum(tot_ref[...], axis=0)
    value = jnp.log((1.0 + total) / GENES)
    for i in range(8):
        offset[:, 128 * i : 128 * (i + 1)] = value[i : i + 1, :]

    for at in range(0, rest_ref.shape[1], CHUNK):
        here = pl.ds(at, CHUNK)
        hi_ref, lo_ref = terms_hi.at[:, here], terms_lo.at[:, here]

        def put(row, value):
            hi, lo = split2(value)
            hi_ref[row : row + value.shape[0], :] = hi
            lo_ref[row : row + value.shape[0], :] = lo

        d1, d2, d3 = (design_ref[32 * i : 32 * (i + 1), here] for i in range(3))
        design = (d1.astype(F32) + d2.astype(F32)) + d3.astype(F32)
        hat, cov = design[:SPL], design[SPL:]
        put(0, hat * hat)
        put(16, hat * pltpu.roll(hat, SPL - 1, axis=0))
        for p in range(SPL):
            put(32 + 16 * p, hat[p : p + 1, :] * cov)
        low, high = cov[:8], cov[8:]
        for i in range(0, 8, 2):
            for row, left, right in ((288, low, low), (352, low, high), (416, high, high)):
                both = [left[i : i + 1] * right, left[i + 1 : i + 2] * right]
                put(row + 8 * i, jnp.concatenate(both, axis=0))
        put(480, -design)

        pred = rest_ref[:, here] + offset[:, here]
        pred_ref[:, here] = pred
        slot = lax.broadcasted_iota(jnp.int32, (1, CHUNK), 1) + at
        mask = (slot < live_ref[0]).astype(F32)
        w1, w2 = split2(jnp.exp(pred) * mask)
        hi, lo = hi_ref[...], lo_ref[...]
        gram = dot(w1, hi, NT) + dot(w1, lo, NT) + dot(w2, hi, NT)
        for t in range(4):
            part = gram[:, 128 * t : 128 * (t + 1)]
            if at > 0:
                acc[t] += part
            else:
                acc[t] = part + score_ref[...] if t == 3 else part

    core = core_ref[0]
    for chip in range(16):
        for ref, j in ((kept_ref, 16 * core + chip), (given_ref, 16 * (1 - core) + chip)):
            for t in range(4):
                ref[chip, 12 * t : 12 * (t + 1), :] = acc[t, pl.ds(j, 12, stride=32), :]


def gram_sums(live, core, tot, rest, design, score):
    genes, cells = rest.shape
    return pl.pallas_call(
        gram_kernel,
        in_specs=[smem(), smem(), vmem(), vmem(), vmem(), vmem()],
        out_specs=[vmem(), vmem(), vmem()],
        out_shape=[
            jax.ShapeDtypeStruct((genes, cells), F32),
            jax.ShapeDtypeStruct((16, 48, 128), F32),
            jax.ShapeDtypeStruct((16, 48, 128), F32),
        ],
        scratch_shapes=[
            pltpu.VMEM((1, cells), F32), pltpu.VMEM((4, genes, 128), F32),
            pltpu.VMEM((512, cells), BF16), pltpu.VMEM((512, cells), BF16),
        ],
        compiler_params=params(),
        name="gram_sums",
    )(live, core, tot, rest, design, score)


def solve_kernel(parts_ref, out_ref, table):
    total = parts_ref[0]
    for j in range(1, parts_ref.shape[0]):
        total = total + parts_ref[j]
    turned = jnp.concatenate([total, jnp.zeros((80, 128), F32)], axis=0).T
    for t in range(4):
        moved = turned if t == 0 else pltpu.roll(turned, 128 - 12 * t, axis=1)
        table[128 * t : 128 * (t + 1), :] = moved
    row16 = lax.broadcasted_iota(jnp.int32, (SPL, 128), 0)
    row32 = lax.broadcasted_iota(jnp.int32, (COLS, 128), 0)
    diag, near = table[0:16, :] + 1.0, table[16:32, :]
    below = pltpu.roll(near, 1, axis=0)
    system = []
    for j in range(SPL):
        top = jnp.where(row16 == j, diag, 0.0)
        top = jnp.where(row16 == j - 1, near, top)
        top = jnp.where(row16 == j + 1, below, top)
        system.append(jnp.concatenate([top, table[32 + 16 * j : 48 + 16 * j, :]], axis=0))
    for q in range(SPL):
        top = table[pl.ds(32 + q, 16, stride=16), :]
        if q < 8:
            first = table[288 + 8 * q : 296 + 8 * q, :]
            second = table[352 + 8 * q : 360 + 8 * q, :]
        else:
            first = table[pl.ds(344 + q, 8, stride=8), :]
            second = table[352 + 8 * q : 360 + 8 * q, :]
        column = jnp.concatenate([top, first, second], axis=0)
        system.append(jnp.where(row32 == 16 + q, column + 1.0, column))
    rhs = table[480:512, :]
    scale = jnp.zeros((COLS, 128), F32)
    for k in range(COLS):
        column = system[k]
        inverse = 1.0 / column[k : k + 1, :]
        scale = jnp.where(row32 == k, inverse, scale)
        ratio = jnp.where(row32 == k, 0.0, column * inverse)
        touched = [j for j in range(k + 1, COLS) if j >= SPL or j == k + 1]
        for j in touched:
            system[j] = system[j] - ratio * column[j : j + 1, :]
        rhs = rhs - ratio * rhs[k : k + 1, :]
    answer = rhs * scale
    flat = jnp.concatenate([answer, jnp.zeros((96, 128), F32)], axis=0).T
    line = jnp.concatenate([flat[g : g + 1, :COLS] for g in range(12)], axis=1)
    out_ref[...] = jnp.broadcast_to(line[None], out_ref.shape)


def solve(parts):
    return pl.pallas_call(
        solve_kernel,
        in_specs=[vmem()],
        out_specs=vmem(),
        out_shape=jax.ShapeDtypeStruct((32, 1, 384), F32),
        scratch_shapes=[pltpu.VMEM((512, 128), F32)],
        compiler_params=params(),
        name="solve",
    )(parts)


def update_kernel(
    live_ref, core_ref, steps_ref, pred_ref, design_ref, load_ref, fact_ref,
    by_load_ref, by_fact_ref,
    out_hbm, kept_ref, given_ref, beta_hbm, left, loads, sums, out, beta_out, sent,
):
    steps = steps_ref[...]
    beta = jnp.concatenate([steps[:, COLS * g : COLS * (g + 1)] for g in range(12)], axis=0)
    b1, b2, b3 = split3(beta)
    left[...] = jnp.concatenate([b1, b1, b2, b2, b1, b3], axis=1)
    load = load_ref[...]
    wide = load.astype(F32)
    l1, l2 = split2(wide * wide)
    loads[...] = jnp.concatenate([load, l1, l2], axis=0)

    cells = pred_ref.shape[1]
    sends = []
    for at in range(0, cells, CHUNK):
        here = pl.ds(at, CHUNK)
        d1, d2, d3 = (design_ref[32 * i : 32 * (i + 1), here] for i in range(3))
        change = dot(left[...], jnp.concatenate([d1, d2, d1, d2, d3, d1], axis=0), NN)
        slot = lax.broadcasted_iota(jnp.int32, (1, CHUNK), 1) + at
        mask = (slot < live_ref[0]).astype(F32)
        w1, w2 = split2(jnp.exp(pred_ref[:, here] + change) * mask)
        first = dot(loads[...], w1, NN)
        second = dot(loads[: 2 * FACT], w2, NN)
        grad = by_load_ref[:, here] - (first[:FACT] + second[:FACT])
        curv = (first[FACT : 2 * FACT] + first[2 * FACT :]) + second[FACT:]
        for z in range(8):
            out[z, :8, here] = grad[8 * z : 8 * (z + 1), :]
            out[z, 8:, here] = curv[8 * z : 8 * (z + 1), :]
        send = pltpu.make_async_copy(
            out.at[:, :, here], out_hbm.at[:, :, here], sent.at[at // CHUNK]
        )
        send.start()
        sends.append(send)
        fact = fact_ref[:, here]
        wide = fact.astype(F32)
        f1, f2 = split2(wide * wide)
        first = dot(jnp.concatenate([fact, f1, f2], axis=0), w1, NT)
        second = dot(jnp.concatenate([fact, f1], axis=0), w2, NT)
        grad = first[:FACT] + second[:FACT]
        curv = (first[FACT : 2 * FACT] + first[2 * FACT :]) + second[FACT:]
        for h in range(2):
            rows = slice(32 * h, 32 * (h + 1))
            if at > 0:
                sums[h, :32, :] -= grad[rows]
                sums[h, 32:, :] += curv[rows]
            else:
                sums[h, :32, :] = by_fact_ref[rows, :] - grad[rows]
                sums[h, 32:, :] = curv[rows]

    beta_out[...] = beta.T
    send = pltpu.make_async_copy(beta_out, beta_hbm, sent.at[cells // CHUNK])
    send.start()
    sends.append(send)
    kept_ref[...] = sums[core_ref[0]]
    given_ref[...] = sums[1 - core_ref[0]]
    for send in sends:
        send.wait()


def update(live, core, steps, pred, design, load, fact, by_load, by_fact):
    genes, cells = pred.shape
    return pl.pallas_call(
        update_kernel,
        in_specs=[smem(), smem()] + [vmem()] * 7,
        out_specs=[hbm(), vmem(), vmem(), hbm()],
        out_shape=[
            pltpu.HBM((8, 16, cells), F32),
            jax.ShapeDtypeStruct((FACT, genes), F32),
            jax.ShapeDtypeStruct((FACT, genes), F32),
            pltpu.HBM((COLS, genes), F32),
        ],
        scratch_shapes=[
            pltpu.VMEM((genes, 6 * COLS), BF16), pltpu.VMEM((3 * FACT, genes), BF16),
            pltpu.VMEM((2, FACT, genes), F32), pltpu.VMEM((8, 16, cells), F32),
            pltpu.VMEM((COLS, genes), F32),
            pltpu.SemaphoreType.DMA((cells // CHUNK + 1,)),
        ],
        compiler_params=params(),
        name="update",
    )(live, core, steps, pred, design, load, fact, by_load, by_fact)


def score_kernel(core_ref, mine_ref, other_ref, out_hbm, sent):
    core = core_ref[0]
    sends = [
        pltpu.make_async_copy(
            ref, out_hbm.at[pl.ds(pl.multiple_of(32 * half, 32), 32), :], sent.at[i]
        )
        for i, (half, ref) in enumerate(((core, mine_ref), (1 - core, other_ref)))
    ]
    for send in sends:
        send.start()
    for send in sends:
        send.wait()


def joined_score(core, mine, other):
    return pl.pallas_call(
        score_kernel,
        in_specs=[smem(), vmem(), vmem()],
        out_specs=hbm(),
        out_shape=pltpu.HBM((FACT, mine.shape[1]), F32),
        scratch_shapes=[pltpu.SemaphoreType.DMA((2,))],
        compiler_params=params(),
        name="joined_score",
    )(core, mine, other)


def factor_kernel(parts_ref, out_hbm, stage, sent):
    total = parts_ref[0]
    for j in range(1, parts_ref.shape[0]):
        total = total + parts_ref[j]
    stage[...] = total[:8, :] / (total[8:, :] + 1.0)
    sends = [
        pltpu.make_async_copy(stage, out_hbm.at[z], sent.at[z]) for z in range(out_hbm.shape[0])
    ]
    for send in sends:
        send.start()
    for send in sends:
        send.wait()


def factor_share(parts):
    peers, _, cells = parts.shape
    return pl.pallas_call(
        factor_kernel,
        in_specs=[vmem()],
        out_specs=hbm(),
        out_shape=pltpu.HBM((peers, 8, cells), F32),
        scratch_shapes=[pltpu.VMEM((8, cells), F32), pltpu.SemaphoreType.DMA((peers,))],
        compiler_params=params(),
        name="factor_share",
    )(parts)


def settle_kernel(value_ref, out_hbm, sent):
    sends = [
        pltpu.make_async_copy(value_ref.at[z], out_hbm.at[z], sent.at[z])
        for z in range(value_ref.shape[0])
    ]
    for send in sends:
        send.start()
    for send in sends:
        send.wait()


def settled(value):
    return pl.pallas_call(
        settle_kernel,
        in_specs=[vmem()],
        out_specs=hbm(),
        out_shape=pltpu.HBM(value.shape, value.dtype),
        scratch_shapes=[pltpu.SemaphoreType.DMA((value.shape[0],))],
        compiler_params=params(),
        name="settled",
    )(value)


def exchange(value, axis, groups=None):
    return lax.all_to_all(
        value, axis, split_axis=0, concat_axis=0, tiled=True, axis_index_groups=groups
    )


def partners(move):
    def index(x, y, core):
        return (x * 4 + y) * 2 + core

    return [
        (index(x, y, core), index(*move(x, y, core)))
        for x in range(4)
        for y in range(4)
        for core in range(2)
    ]


def around(at, size):
    return [min((i - at) % size, (at - i) % size) for i in range(size)]


def nearest_first(x, y):
    far_x, far_y = around(x, 4), around(y, 4)
    chips = [(i, j) for i in range(4) for j in range(4)]
    return sorted(chips, key=lambda chip: far_x[chip[0]] + far_y[chip[1]])


FIRST = (3, 2, 5)
SAME_CORE = [[(4 * x + y) * 2 + core for x, y in nearest_first(*FIRST[:2])] for core in range(2)]
CORE_FIRST = [SAME_CORE[0] + SAME_CORE[1]]
RING = [[(FIRST[2] + step) % 8 for step in (0, 1, -1, 2, -2, 3, -3, 4)]]
OTHER_CORE = partners(lambda x, y, c: (x, y, 1 - c))
ALONG_X = [partners(lambda x, y, c, k=k: (x ^ k, y, c)) for k in (1, 2, 3)]
ALONG_Y = [partners(lambda x, y, c, k=k: (x, y ^ k, c)) for k in (1, 2, 3)]


def local(
    counts, batch_id, live_cells, knot_bin, depth_frac, cell_covariates,
    coefficients, batch_effect, factors, loadings,
):
    fact, load = factors.T, loadings.T
    tot = exchange(cell_totals(counts, 8), "gene", RING)
    rest, design, score, by_load, by_fact = prepare(
        live_cells, counts, knot_bin[None], depth_frac[None], batch_id[None],
        cell_covariates, coefficients.T, batch_effect.T, load, fact,
    )
    core = (lax.axis_index("cell") % 2)[None]
    pred, kept, given = gram_sums(
        live_cells, core, tot, rest, design, score
    )
    packed = kept + lax.ppermute(given, "cell", OTHER_CORE)
    steps = exchange(solve(exchange(packed, "cell", SAME_CORE)), "cell", CORE_FIRST)
    pieces, kept, given, beta = update(
        live_cells, core, steps.reshape(32, 384), pred, design, load, fact, by_load, by_fact
    )
    arrived = exchange(pieces, "gene", RING)

    value = kept + lax.ppermute(given, "cell", OTHER_CORE)
    for moves in (ALONG_X, ALONG_Y):
        near, across, beside = (lax.ppermute(value, "cell", pairs) for pairs in moves)
        value = (value + near) + (across + beside)
    gathered = settled(exchange(factor_share(arrived), "gene", RING))
    mine = value[:32] / jnp.sqrt(value[32:] + 1.0)
    other = lax.ppermute(mine, "cell", OTHER_CORE)
    score = joined_score(core, mine, other)
    factor_step = gathered.reshape(FACT, -1)
    return beta.T, factor_step.T, score.T


def solution(mesh):
    placed = (
        P("gene", "cell"),
        P("cell"),
        P("cell"),
        P("cell"),
        P("cell"),
        P(None, "cell"),
        P("gene", None),
        P("gene", None),
        P("cell", None),
        P("gene", None),
    )
    return jax.shard_map(
        local,
        mesh=mesh,
        in_specs=placed,
        out_specs=(P("gene", None), P("cell", None), P("gene", None)),
        check_vma=False,
    )
```

```python
import functools

import jax
import jax.numpy as jnp
from jax import lax
from jax.experimental import pallas as pl
from jax.experimental.pallas import tpu as pltpu
from jax.sharding import PartitionSpec as P

GENES = 3072
SPL = 16
COLS = 32
FACT = 64
CHUNK = 256
F32 = jnp.float32
BF16 = jnp.bfloat16
NN = (((1,), (0,)), ((), ()))
NT = (((1,), (1,)), ((), ()))
TN = (((0,), (0,)), ((), ()))
MIB = 1024 * 1024


def dot(a, b, dims):
    return lax.dot_general(a, b, dims, preferred_element_type=F32)


def split2(x):
    hi = x.astype(BF16)
    return hi, (x - hi.astype(F32)).astype(BF16)


def split3(x):
    hi = x.astype(BF16)
    rest = x - hi.astype(F32)
    mid = rest.astype(BF16)
    return hi, mid, (rest - mid.astype(F32)).astype(BF16)


def smem():
    return pl.BlockSpec(memory_space=pltpu.SMEM)


def vmem():
    return pl.BlockSpec(memory_space=pltpu.VMEM)


def hbm():
    return pl.BlockSpec(memory_space=pltpu.HBM)


def params(mib=16):
    return pltpu.CompilerParams(vmem_limit_bytes=mib * MIB)


def totals_kernel(counts_ref, out_ref, rows, stage, arrived, sent):
    blocks, size = rows.shape[0], rows.shape[1]

    def copy(b):
        return pltpu.make_async_copy(
            counts_ref.at[pl.ds(b * size, size), :], rows.at[b], arrived.at[b]
        )

    for b in range(blocks):
        copy(b).start()
    total = jnp.zeros((8, rows.shape[2]), F32)
    for b in range(blocks):
        copy(b).wait()
        part = rows[b, :8, :]
        for i in range(8, size, 8):
            part = part + rows[b, i : i + 8, :]
        total = total + part.astype(F32)
    total = jnp.sum(total, axis=0, keepdims=True)
    for i in range(8):
        stage[i : i + 1, :] = total[:, 128 * i : 128 * (i + 1)]
    sends = [
        pltpu.make_async_copy(stage, out_ref.at[z], sent.at[z]) for z in range(out_ref.shape[0])
    ]
    for send in sends:
        send.start()
    for send in sends:
        send.wait()


def cell_totals(counts, peers):
    genes, cells = counts.shape
    blocks = 12
    return pl.pallas_call(
        totals_kernel,
        in_specs=[hbm()],
        out_specs=hbm(),
        out_shape=pltpu.HBM((peers, 8, 128), F32),
        scratch_shapes=[
            pltpu.VMEM((blocks, genes // blocks, cells), jnp.int32),
            pltpu.VMEM((8, 128), F32),
            pltpu.SemaphoreType.DMA((blocks,)),
            pltpu.SemaphoreType.DMA((peers,)),
        ],
        compiler_params=params(),
        name="cell_totals",
    )(pltpu.with_memory_space_constraint(counts, pltpu.HBM))


def prepare_kernel(
    live_ref, counts_hbm, knot_hbm, frac_hbm, batch_hbm, cov_hbm, coef_hbm, shift_hbm,
    load_hbm, fact_hbm,
    rest_ref, design_ref, score_ref, by_load_ref, by_fact_ref,
    counts_all, knot_all, frac_all, batch_all, cov_all, coef, shift, load, fact_all, arrived,
):
    pairs = (
        (knot_hbm, knot_all), (frac_hbm, frac_all), (batch_hbm, batch_all), (cov_hbm, cov_all),
        (coef_hbm, coef), (shift_hbm, shift), (load_hbm, load), (fact_hbm, fact_all),
    )
    copies = [
        pltpu.make_async_copy(source, target, arrived.at[i])
        for i, (source, target) in enumerate(pairs)
    ]
    cells = rest_ref.shape[1]
    blocks = [
        pltpu.make_async_copy(
            counts_hbm.at[:, pl.ds(at, CHUNK)], counts_all.at[:, pl.ds(at, CHUNK)],
            arrived.at[len(pairs) + at // CHUNK],
        )
        for at in range(0, cells, CHUNK)
    ]
    for copy in copies + blocks:
        copy.start()
    for copy in copies:
        copy.wait()
    c1, c2, c3 = split3(coef[...])
    b1, b2, b3 = split3(shift[...])
    left = jnp.concatenate([c1, c1, c2, c2, c1, c3, b1, b2, b3, load[...]], axis=0)
    score, by_fact = 0.0, 0.0
    for at in range(0, cells, CHUNK):
        here = pl.ds(at, CHUNK)
        knot, frac = knot_all[:, here], frac_all[:, here]
        cov, fact = cov_all[:, here], fact_all[:, here]
        levels = lax.broadcasted_iota(jnp.int32, (SPL, CHUNK), 0)
        hat = jnp.where(levels == knot, 1.0 - frac, 0.0)
        hat = hat + jnp.where(levels == knot + 1, frac, 0.0)
        d1, d2, d3 = split3(jnp.concatenate([hat, cov], axis=0))
        terms = jnp.concatenate([d1, d2, d3], axis=0)
        design_ref[:, here] = terms
        batches = lax.broadcasted_iota(jnp.int32, (64, CHUNK), 0)
        onehot = (batches == batch_all[:, here]).astype(F32).astype(BF16)
        right = jnp.concatenate([d1, d2, d1, d2, d3, d1, onehot, onehot, onehot, fact], axis=0)
        rest_ref[:, here] = dot(left, right, TN)

        blocks[at // CHUNK].wait()
        slot = lax.broadcasted_iota(jnp.int32, (1, CHUNK), 1) + at
        mask = (slot < live_ref[0]).astype(F32)
        counts = (counts_all[:, here].astype(F32) * mask).astype(BF16)
        by_load_ref[:, here] = dot(load[...], counts, NN)
        by_fact = by_fact + dot(fact, counts, NT)
        score = score + dot(counts, terms, NT)
    by_fact_ref[...] = by_fact
    value = score[:, :32] + score[:, 32:64] + score[:, 64:96]
    blank = jnp.zeros((value.shape[0], 96), F32)
    score_ref[...] = jnp.concatenate([blank, value], axis=1)


def prepare(live, counts, knot, frac, batch, cov, coef, shift, load, fact):
    genes, cells = counts.shape
    arrays = [
        pltpu.with_memory_space_constraint(a, pltpu.HBM)
        for a in (counts, knot, frac, batch, cov, coef, shift, load, fact)
    ]
    return pl.pallas_call(
        prepare_kernel,
        in_specs=[smem()] + [hbm()] * len(arrays),
        out_specs=[vmem()] * 5,
        out_shape=[
            jax.ShapeDtypeStruct((genes, cells), F32),
            jax.ShapeDtypeStruct((96, cells), BF16),
            jax.ShapeDtypeStruct((genes, 128), F32),
            jax.ShapeDtypeStruct((FACT, cells), F32),
            jax.ShapeDtypeStruct((FACT, genes), F32),
        ],
        scratch_shapes=[pltpu.VMEM(a.shape, a.dtype) for a in arrays]
        + [pltpu.SemaphoreType.DMA((len(arrays) - 1 + cells // CHUNK,))],
        compiler_params=params(),
        name="prepare",
    )(live, *arrays)


def half_rows(ref, half, here):
    rows = [
        ref[pl.ds(pl.multiple_of(32 * g + 16 * half, 16), 16), here] for g in range(12)
    ]
    return jnp.concatenate(rows, axis=0)


def half_sums(live_ref, half, pred_ref, score_ref, hi_ref, lo_ref, out_ref, acc, at):
    here = pl.ds(at, CHUNK)
    slot = lax.broadcasted_iota(jnp.int32, (1, CHUNK), 1) + at
    mask = (slot < live_ref[0]).astype(F32)
    w1, w2 = split2(jnp.exp(half_rows(pred_ref, half, here)) * mask)
    hi, lo = hi_ref[:, here], lo_ref[:, here]
    gram = dot(w1, hi, NT) + dot(w1, lo, NT) + dot(w2, hi, NT)
    for t in range(4):
        part = gram[:, 128 * t : 128 * (t + 1)]
        if at > 0:
            acc[t] += part
        else:
            acc[t] = part + half_rows(score_ref, half, slice(None)) if t == 3 else part
    if at + CHUNK == pred_ref.shape[1]:
        for chip in range(16):
            for t in range(4):
                out_ref[chip, 12 * t : 12 * (t + 1), :] = acc[t, pl.ds(chip, 12, stride=16), :]


def given_kernel(
    live_ref, half_ref, tot_ref, rest_ref, design_ref, score_ref,
    pred_ref, hi_ref, lo_ref, out_ref, offset, acc,
):
    total = jnp.sum(tot_ref[...], axis=0)
    value = jnp.log((1.0 + total) / GENES)
    for i in range(8):
        offset[:, 128 * i : 128 * (i + 1)] = value[i : i + 1, :]

    for at in range(0, rest_ref.shape[1], CHUNK):
        here = pl.ds(at, CHUNK)

        def put(row, value):
            hi, lo = split2(value)
            hi_ref[row : row + value.shape[0], here] = hi
            lo_ref[row : row + value.shape[0], here] = lo

        d1, d2, d3 = (design_ref[32 * i : 32 * (i + 1), here] for i in range(3))
        design = (d1.astype(F32) + d2.astype(F32)) + d3.astype(F32)
        hat, cov = design[:SPL], design[SPL:]
        put(0, hat * hat)
        put(16, hat * pltpu.roll(hat, SPL - 1, axis=0))
        for p in range(SPL):
            put(32 + 16 * p, hat[p : p + 1, :] * cov)
        low, high = cov[:8], cov[8:]
        for i in range(0, 8, 2):
            for row, left, right in ((288, low, low), (352, low, high), (416, high, high)):
                both = [left[i : i + 1] * right, left[i + 1 : i + 2] * right]
                put(row + 8 * i, jnp.concatenate(both, axis=0))
        put(480, -design)
        pred_ref[:, here] = rest_ref[:, here] + offset[:, here]
        half_sums(live_ref, half_ref[0], pred_ref, score_ref, hi_ref, lo_ref, out_ref, acc, at)


def kept_kernel(live_ref, half_ref, pred_ref, score_ref, hi_ref, lo_ref, out_ref, acc):
    for at in range(0, pred_ref.shape[1], CHUNK):
        half_sums(live_ref, half_ref[0], pred_ref, score_ref, hi_ref, lo_ref, out_ref, acc, at)


def gram_sums(live, core, tot, rest, design, score):
    genes, cells = rest.shape
    packed = jax.ShapeDtypeStruct((16, 48, 128), F32)
    acc = pltpu.VMEM((4, genes // 2, 128), F32)
    pred, hi, lo, given = pl.pallas_call(
        given_kernel,
        in_specs=[smem(), smem(), vmem(), vmem(), vmem(), vmem()],
        out_specs=[vmem()] * 4,
        out_shape=[
            jax.ShapeDtypeStruct((genes, cells), F32),
            jax.ShapeDtypeStruct((512, cells), BF16),
            jax.ShapeDtypeStruct((512, cells), BF16),
            packed,
        ],
        scratch_shapes=[pltpu.VMEM((1, cells), F32), acc],
        compiler_params=params(),
        name="gram_given",
    )(live, 1 - core, tot, rest, design, score)
    arrived = lax.ppermute(given, "cell", OTHER_CORE)
    kept = pl.pallas_call(
        kept_kernel,
        in_specs=[smem(), smem(), vmem(), vmem(), vmem(), vmem()],
        out_specs=vmem(),
        out_shape=packed,
        scratch_shapes=[acc],
        compiler_params=params(),
        name="gram_kept",
    )(live, core, pred, score, hi, lo)
    return pred, kept + arrived


def solve_kernel(parts_ref, out_ref, table):
    total = parts_ref[0]
    for j in range(1, parts_ref.shape[0]):
        total = total + parts_ref[j]
    turned = jnp.concatenate([total, jnp.zeros((80, 128), F32)], axis=0).T
    for t in range(4):
        moved = turned if t == 0 else pltpu.roll(turned, 128 - 12 * t, axis=1)
        table[128 * t : 128 * (t + 1), :] = moved
    row16 = lax.broadcasted_iota(jnp.int32, (SPL, 128), 0)
    row32 = lax.broadcasted_iota(jnp.int32, (COLS, 128), 0)
    diag, near = table[0:16, :] + 1.0, table[16:32, :]
    below = pltpu.roll(near, 1, axis=0)
    system = []
    for j in range(SPL):
        top = jnp.where(row16 == j, diag, 0.0)
        top = jnp.where(row16 == j - 1, near, top)
        top = jnp.where(row16 == j + 1, below, top)
        system.append(jnp.concatenate([top, table[32 + 16 * j : 48 + 16 * j, :]], axis=0))
    for q in range(SPL):
        top = table[pl.ds(32 + q, 16, stride=16), :]
        if q < 8:
            first = table[288 + 8 * q : 296 + 8 * q, :]
            second = table[352 + 8 * q : 360 + 8 * q, :]
        else:
            first = table[pl.ds(344 + q, 8, stride=8), :]
            second = table[352 + 8 * q : 360 + 8 * q, :]
        column = jnp.concatenate([top, first, second], axis=0)
        system.append(jnp.where(row32 == 16 + q, column + 1.0, column))
    rhs = table[480:512, :]
    scale = jnp.zeros((COLS, 128), F32)
    for k in range(COLS):
        column = system[k]
        inverse = 1.0 / column[k : k + 1, :]
        scale = jnp.where(row32 == k, inverse, scale)
        ratio = jnp.where(row32 == k, 0.0, column * inverse)
        touched = [j for j in range(k + 1, COLS) if j >= SPL or j == k + 1]
        for j in touched:
            system[j] = system[j] - ratio * column[j : j + 1, :]
        rhs = rhs - ratio * rhs[k : k + 1, :]
    answer = rhs * scale
    flat = jnp.concatenate([answer, jnp.zeros((96, 128), F32)], axis=0).T
    line = jnp.concatenate([flat[g : g + 1, :COLS] for g in range(12)], axis=1)
    out_ref[...] = jnp.broadcast_to(line[None], out_ref.shape)


def solve(parts):
    return pl.pallas_call(
        solve_kernel,
        in_specs=[vmem()],
        out_specs=vmem(),
        out_shape=jax.ShapeDtypeStruct((32, 1, 384), F32),
        scratch_shapes=[pltpu.VMEM((512, 128), F32)],
        compiler_params=params(),
        name="solve",
    )(parts)


def update_kernel(
    live_ref, core_ref, steps_ref, pred_ref, design_ref, load_ref, fact_ref,
    by_load_ref, by_fact_ref,
    out_hbm, kept_ref, given_ref, beta_hbm, left, loads, sums, out, beta_out, sent,
):
    steps = steps_ref[...]
    beta = jnp.concatenate([steps[:, COLS * g : COLS * (g + 1)] for g in range(12)], axis=0)
    b1, b2, b3 = split3(beta)
    left[...] = jnp.concatenate([b1, b1, b2, b2, b1, b3], axis=1)
    load = load_ref[...]
    wide = load.astype(F32)
    l1, l2 = split2(wide * wide)
    loads[...] = jnp.concatenate([load, l1, l2], axis=0)

    cells = pred_ref.shape[1]
    sends = []
    for at in range(0, cells, CHUNK):
        here = pl.ds(at, CHUNK)
        d1, d2, d3 = (design_ref[32 * i : 32 * (i + 1), here] for i in range(3))
        change = dot(left[...], jnp.concatenate([d1, d2, d1, d2, d3, d1], axis=0), NN)
        slot = lax.broadcasted_iota(jnp.int32, (1, CHUNK), 1) + at
        mask = (slot < live_ref[0]).astype(F32)
        w1, w2 = split2(jnp.exp(pred_ref[:, here] + change) * mask)
        first = dot(loads[...], w1, NN)
        second = dot(loads[: 2 * FACT], w2, NN)
        grad = by_load_ref[:, here] - (first[:FACT] + second[:FACT])
        curv = (first[FACT : 2 * FACT] + first[2 * FACT :]) + second[FACT:]
        for z in range(8):
            out[z, :8, here] = grad[8 * z : 8 * (z + 1), :]
            out[z, 8:, here] = curv[8 * z : 8 * (z + 1), :]
        send = pltpu.make_async_copy(
            out.at[:, :, here], out_hbm.at[:, :, here], sent.at[at // CHUNK]
        )
        send.start()
        sends.append(send)
        fact = fact_ref[:, here]
        wide = fact.astype(F32)
        f1, f2 = split2(wide * wide)
        first = dot(jnp.concatenate([fact, f1, f2], axis=0), w1, NT)
        second = dot(jnp.concatenate([fact, f1], axis=0), w2, NT)
        grad = first[:FACT] + second[:FACT]
        curv = (first[FACT : 2 * FACT] + first[2 * FACT :]) + second[FACT:]
        for h in range(2):
            rows = slice(32 * h, 32 * (h + 1))
            if at > 0:
                sums[h, :32, :] -= grad[rows]
                sums[h, 32:, :] += curv[rows]
            else:
                sums[h, :32, :] = by_fact_ref[rows, :] - grad[rows]
                sums[h, 32:, :] = curv[rows]

    beta_out[...] = beta.T
    send = pltpu.make_async_copy(beta_out, beta_hbm, sent.at[cells // CHUNK])
    send.start()
    sends.append(send)
    kept_ref[...] = sums[core_ref[0]]
    given_ref[...] = sums[1 - core_ref[0]]
    for send in sends:
        send.wait()


def update(live, core, steps, pred, design, load, fact, by_load, by_fact):
    genes, cells = pred.shape
    return pl.pallas_call(
        update_kernel,
        in_specs=[smem(), smem()] + [vmem()] * 7,
        out_specs=[hbm(), vmem(), vmem(), hbm()],
        out_shape=[
            pltpu.HBM((8, 16, cells), F32),
            jax.ShapeDtypeStruct((FACT, genes), F32),
            jax.ShapeDtypeStruct((FACT, genes), F32),
            pltpu.HBM((COLS, genes), F32),
        ],
        scratch_shapes=[
            pltpu.VMEM((genes, 6 * COLS), BF16), pltpu.VMEM((3 * FACT, genes), BF16),
            pltpu.VMEM((2, FACT, genes), F32), pltpu.VMEM((8, 16, cells), F32),
            pltpu.VMEM((COLS, genes), F32),
            pltpu.SemaphoreType.DMA((cells // CHUNK + 1,)),
        ],
        compiler_params=params(),
        name="update",
    )(live, core, steps, pred, design, load, fact, by_load, by_fact)


def score_kernel(core_ref, mine_ref, other_ref, out_hbm, sent):
    core = core_ref[0]
    sends = [
        pltpu.make_async_copy(
            ref, out_hbm.at[pl.ds(pl.multiple_of(32 * half, 32), 32), :], sent.at[i]
        )
        for i, (half, ref) in enumerate(((core, mine_ref), (1 - core, other_ref)))
    ]
    for send in sends:
        send.start()
    for send in sends:
        send.wait()


def joined_score(core, mine, other):
    return pl.pallas_call(
        score_kernel,
        in_specs=[smem(), vmem(), vmem()],
        out_specs=hbm(),
        out_shape=pltpu.HBM((FACT, mine.shape[1]), F32),
        scratch_shapes=[pltpu.SemaphoreType.DMA((2,))],
        compiler_params=params(),
        name="joined_score",
    )(core, mine, other)


def factor_kernel(parts_ref, out_hbm, stage, sent):
    total = parts_ref[0]
    for j in range(1, parts_ref.shape[0]):
        total = total + parts_ref[j]
    stage[...] = total[:8, :] / (total[8:, :] + 1.0)
    sends = [
        pltpu.make_async_copy(stage, out_hbm.at[z], sent.at[z]) for z in range(out_hbm.shape[0])
    ]
    for send in sends:
        send.start()
    for send in sends:
        send.wait()


def factor_share(parts):
    peers, _, cells = parts.shape
    return pl.pallas_call(
        factor_kernel,
        in_specs=[vmem()],
        out_specs=hbm(),
        out_shape=pltpu.HBM((peers, 8, cells), F32),
        scratch_shapes=[pltpu.VMEM((8, cells), F32), pltpu.SemaphoreType.DMA((peers,))],
        compiler_params=params(),
        name="factor_share",
    )(parts)


def settle_kernel(value_ref, out_hbm, sent):
    sends = [
        pltpu.make_async_copy(value_ref.at[z], out_hbm.at[z], sent.at[z])
        for z in range(value_ref.shape[0])
    ]
    for send in sends:
        send.start()
    for send in sends:
        send.wait()


def settled(value):
    return pl.pallas_call(
        settle_kernel,
        in_specs=[vmem()],
        out_specs=hbm(),
        out_shape=pltpu.HBM(value.shape, value.dtype),
        scratch_shapes=[pltpu.SemaphoreType.DMA((value.shape[0],))],
        compiler_params=params(),
        name="settled",
    )(value)


def exchange(value, axis, groups=None):
    return lax.all_to_all(
        value, axis, split_axis=0, concat_axis=0, tiled=True, axis_index_groups=groups
    )


def partners(move):
    def index(x, y, core):
        return (x * 4 + y) * 2 + core

    return [
        (index(x, y, core), index(*move(x, y, core)))
        for x in range(4)
        for y in range(4)
        for core in range(2)
    ]


def around(at, size):
    return [min((i - at) % size, (at - i) % size) for i in range(size)]


def nearest_first(x, y):
    far_x, far_y = around(x, 4), around(y, 4)
    chips = [(i, j) for i in range(4) for j in range(4)]
    return sorted(chips, key=lambda chip: far_x[chip[0]] + far_y[chip[1]])


FIRST = (3, 2, 5)
SAME_CORE = [[(4 * x + y) * 2 + core for x, y in nearest_first(*FIRST[:2])] for core in range(2)]
CORE_FIRST = [SAME_CORE[0] + SAME_CORE[1]]
RING = [[(FIRST[2] + step) % 8 for step in (0, 1, -1, 2, -2, 3, -3, 4)]]
OTHER_CORE = partners(lambda x, y, c: (x, y, 1 - c))
ALONG_X = [partners(lambda x, y, c, k=k: (x ^ k, y, c)) for k in (1, 2, 3)]
ALONG_Y = [partners(lambda x, y, c, k=k: (x, y ^ k, c)) for k in (1, 2, 3)]


def local(
    counts, batch_id, live_cells, knot_bin, depth_frac, cell_covariates,
    coefficients, batch_effect, factors, loadings,
):
    fact, load = factors.T, loadings.T
    tot = exchange(cell_totals(counts, 8), "gene", RING)
    rest, design, score, by_load, by_fact = prepare(
        live_cells, counts, knot_bin[None], depth_frac[None], batch_id[None],
        cell_covariates, coefficients.T, batch_effect.T, load, fact,
    )
    core = (lax.axis_index("cell") % 2)[None]
    pred, packed = gram_sums(live_cells, core, tot, rest, design, score)
    steps = exchange(solve(exchange(packed, "cell", SAME_CORE)), "cell", CORE_FIRST)
    pieces, kept, given, beta = update(
        live_cells, core, steps.reshape(32, 384), pred, design, load, fact, by_load, by_fact
    )
    arrived = exchange(pieces, "gene", RING)

    value = kept + lax.ppermute(given, "cell", OTHER_CORE)
    for moves in (ALONG_X, ALONG_Y):
        near, across, beside = (lax.ppermute(value, "cell", pairs) for pairs in moves)
        value = (value + near) + (across + beside)
    gathered = settled(exchange(factor_share(arrived), "gene", RING))
    mine = value[:32] / jnp.sqrt(value[32:] + 1.0)
    other = lax.ppermute(mine, "cell", OTHER_CORE)
    score = joined_score(core, mine, other)
    factor_step = gathered.reshape(FACT, -1)
    return beta.T, factor_step.T, score.T


def solution(mesh):
    placed = (
        P("gene", "cell"),
        P("cell"),
        P("cell"),
        P("cell"),
        P("cell"),
        P(None, "cell"),
        P("gene", None),
        P("gene", None),
        P("cell", None),
        P("gene", None),
    )
    return jax.shard_map(
        local,
        mesh=mesh,
        in_specs=placed,
        out_specs=(P("gene", None), P("cell", None), P("gene", None)),
        check_vma=False,
    )
```

```python
import functools

import jax
import jax.numpy as jnp
from jax import lax
from jax.experimental import pallas as pl
from jax.experimental.pallas import tpu as pltpu
from jax.sharding import PartitionSpec as P

GENES = 3072
SPL = 16
COLS = 32
FACT = 64
CHUNK = 256
F32 = jnp.float32
BF16 = jnp.bfloat16
NN = (((1,), (0,)), ((), ()))
NT = (((1,), (1,)), ((), ()))
TN = (((0,), (0,)), ((), ()))
MIB = 1024 * 1024


def dot(a, b, dims):
    return lax.dot_general(a, b, dims, preferred_element_type=F32)


def split2(x):
    hi = x.astype(BF16)
    return hi, (x - hi.astype(F32)).astype(BF16)


def split3(x):
    hi = x.astype(BF16)
    rest = x - hi.astype(F32)
    mid = rest.astype(BF16)
    return hi, mid, (rest - mid.astype(F32)).astype(BF16)


def smem():
    return pl.BlockSpec(memory_space=pltpu.SMEM)


def vmem():
    return pl.BlockSpec(memory_space=pltpu.VMEM)


def hbm():
    return pl.BlockSpec(memory_space=pltpu.HBM)


def params(mib=16):
    return pltpu.CompilerParams(vmem_limit_bytes=mib * MIB)


def totals_kernel(counts_ref, out_ref, rows, stage, arrived, sent):
    blocks, size = rows.shape[0], rows.shape[1]

    def copy(b):
        return pltpu.make_async_copy(
            counts_ref.at[pl.ds(b * size, size), :], rows.at[b], arrived.at[b]
        )

    for b in range(blocks):
        copy(b).start()
    total = jnp.zeros((8, rows.shape[2]), F32)
    for b in range(blocks):
        copy(b).wait()
        part = rows[b, :8, :]
        for i in range(8, size, 8):
            part = part + rows[b, i : i + 8, :]
        total = total + part.astype(F32)
    total = jnp.sum(total, axis=0, keepdims=True)
    for i in range(8):
        stage[i : i + 1, :] = total[:, 128 * i : 128 * (i + 1)]
    sends = [
        pltpu.make_async_copy(stage, out_ref.at[z], sent.at[z]) for z in range(out_ref.shape[0])
    ]
    for send in sends:
        send.start()
    for send in sends:
        send.wait()


def cell_totals(counts, peers):
    genes, cells = counts.shape
    blocks = 12
    return pl.pallas_call(
        totals_kernel,
        in_specs=[hbm()],
        out_specs=hbm(),
        out_shape=pltpu.HBM((peers, 8, 128), F32),
        scratch_shapes=[
            pltpu.VMEM((blocks, genes // blocks, cells), jnp.int32),
            pltpu.VMEM((8, 128), F32),
            pltpu.SemaphoreType.DMA((blocks,)),
            pltpu.SemaphoreType.DMA((peers,)),
        ],
        compiler_params=params(),
        name="cell_totals",
    )(pltpu.with_memory_space_constraint(counts, pltpu.HBM))


def prepare_kernel(
    live_ref, counts_hbm, knot_hbm, frac_hbm, batch_hbm, cov_hbm, coef_hbm, shift_hbm,
    load_hbm, fact_hbm,
    rest_ref, design_ref, score_ref, by_load_ref, by_fact_ref,
    counts_all, knot_all, frac_all, batch_all, cov_all, coef, shift, load, fact_all, arrived,
):
    pairs = (
        (knot_hbm, knot_all), (frac_hbm, frac_all), (batch_hbm, batch_all), (cov_hbm, cov_all),
        (coef_hbm, coef), (shift_hbm, shift), (load_hbm, load), (fact_hbm, fact_all),
    )
    copies = [
        pltpu.make_async_copy(source, target, arrived.at[i])
        for i, (source, target) in enumerate(pairs)
    ]
    cells = rest_ref.shape[1]
    blocks = [
        pltpu.make_async_copy(
            counts_hbm.at[:, pl.ds(at, CHUNK)], counts_all.at[:, pl.ds(at, CHUNK)],
            arrived.at[len(pairs) + at // CHUNK],
        )
        for at in range(0, cells, CHUNK)
    ]
    for copy in copies + blocks:
        copy.start()
    for copy in copies:
        copy.wait()
    c1, c2, c3 = split3(coef[...])
    b1, b2, b3 = split3(shift[...])
    left = jnp.concatenate([c1, c1, c2, c2, c1, c3, b1, b2, b3, load[...]], axis=0)
    score, by_fact = 0.0, 0.0
    for at in range(0, cells, CHUNK):
        here = pl.ds(at, CHUNK)
        knot, frac = knot_all[:, here], frac_all[:, here]
        cov, fact = cov_all[:, here], fact_all[:, here]
        levels = lax.broadcasted_iota(jnp.int32, (SPL, CHUNK), 0)
        hat = jnp.where(levels == knot, 1.0 - frac, 0.0)
        hat = hat + jnp.where(levels == knot + 1, frac, 0.0)
        d1, d2, d3 = split3(jnp.concatenate([hat, cov], axis=0))
        terms = jnp.concatenate([d1, d2, d3], axis=0)
        design_ref[:, here] = terms
        batches = lax.broadcasted_iota(jnp.int32, (64, CHUNK), 0)
        onehot = (batches == batch_all[:, here]).astype(F32).astype(BF16)
        right = jnp.concatenate([d1, d2, d1, d2, d3, d1, onehot, onehot, onehot, fact], axis=0)
        rest_ref[:, here] = dot(left, right, TN)

        blocks[at // CHUNK].wait()
        slot = lax.broadcasted_iota(jnp.int32, (1, CHUNK), 1) + at
        mask = (slot < live_ref[0]).astype(F32)
        counts = (counts_all[:, here].astype(F32) * mask).astype(BF16)
        by_load_ref[:, here] = dot(load[...], counts, NN)
        by_fact = by_fact + dot(fact, counts, NT)
        score = score + dot(counts, terms, NT)
    by_fact_ref[...] = by_fact
    value = score[:, :32] + score[:, 32:64] + score[:, 64:96]
    blank = jnp.zeros((value.shape[0], 96), F32)
    score_ref[...] = jnp.concatenate([blank, value], axis=1)


def prepare(live, counts, knot, frac, batch, cov, coef, shift, load, fact):
    genes, cells = counts.shape
    arrays = [
        pltpu.with_memory_space_constraint(a, pltpu.HBM)
        for a in (counts, knot, frac, batch, cov, coef, shift, load, fact)
    ]
    return pl.pallas_call(
        prepare_kernel,
        in_specs=[smem()] + [hbm()] * len(arrays),
        out_specs=[vmem()] * 5,
        out_shape=[
            jax.ShapeDtypeStruct((genes, cells), F32),
            jax.ShapeDtypeStruct((96, cells), BF16),
            jax.ShapeDtypeStruct((genes, 128), F32),
            jax.ShapeDtypeStruct((FACT, cells), F32),
            jax.ShapeDtypeStruct((FACT, genes), F32),
        ],
        scratch_shapes=[pltpu.VMEM(a.shape, a.dtype) for a in arrays]
        + [pltpu.SemaphoreType.DMA((len(arrays) - 1 + cells // CHUNK,))],
        compiler_params=params(),
        name="prepare",
    )(live, *arrays)


def half_rows(ref, half, here):
    rows = [
        ref[pl.ds(pl.multiple_of(32 * g + 16 * half, 16), 16), here] for g in range(12)
    ]
    return jnp.concatenate(rows, axis=0)


def half_sums(live_ref, half, pred_ref, score_ref, hi_ref, lo_ref, out_ref, acc, at):
    here = pl.ds(at, CHUNK)
    slot = lax.broadcasted_iota(jnp.int32, (1, CHUNK), 1) + at
    mask = (slot < live_ref[0]).astype(F32)
    w1, w2 = split2(jnp.exp(half_rows(pred_ref, half, here)) * mask)
    hi, lo = hi_ref[:, here], lo_ref[:, here]
    gram = dot(w1, hi, NT) + dot(w1, lo, NT) + dot(w2, hi, NT)
    for t in range(4):
        part = gram[:, 128 * t : 128 * (t + 1)]
        if at > 0:
            acc[t] += part
        else:
            acc[t] = part + half_rows(score_ref, half, slice(None)) if t == 3 else part
    if at + CHUNK == pred_ref.shape[1]:
        for chip in range(16):
            for t in range(4):
                out_ref[chip, 12 * t : 12 * (t + 1), :] = acc[t, pl.ds(chip, 12, stride=16), :]


def given_kernel(
    live_ref, half_ref, tot_ref, rest_ref, design_ref, score_ref,
    pred_ref, hi_ref, lo_ref, out_ref, offset, acc,
):
    total = jnp.sum(tot_ref[...], axis=0)
    value = jnp.log((1.0 + total) / GENES)
    for i in range(8):
        offset[:, 128 * i : 128 * (i + 1)] = value[i : i + 1, :]

    for at in range(0, rest_ref.shape[1], CHUNK):
        here = pl.ds(at, CHUNK)

        def put(row, value):
            hi, lo = split2(value)
            hi_ref[row : row + value.shape[0], here] = hi
            lo_ref[row : row + value.shape[0], here] = lo

        d1, d2, d3 = (design_ref[32 * i : 32 * (i + 1), here] for i in range(3))
        design = (d1.astype(F32) + d2.astype(F32)) + d3.astype(F32)
        hat, cov = design[:SPL], design[SPL:]
        put(0, hat * hat)
        put(16, hat * pltpu.roll(hat, SPL - 1, axis=0))
        for p in range(SPL):
            put(32 + 16 * p, hat[p : p + 1, :] * cov)
        low, high = cov[:8], cov[8:]
        for i in range(0, 8, 2):
            for row, left, right in ((288, low, low), (352, low, high), (416, high, high)):
                both = [left[i : i + 1] * right, left[i + 1 : i + 2] * right]
                put(row + 8 * i, jnp.concatenate(both, axis=0))
        put(480, -design)
        pred_ref[:, here] = rest_ref[:, here] + offset[:, here]
        half_sums(live_ref, half_ref[0], pred_ref, score_ref, hi_ref, lo_ref, out_ref, acc, at)


def kept_kernel(live_ref, half_ref, pred_ref, score_ref, hi_ref, lo_ref, out_ref, acc):
    for at in range(0, pred_ref.shape[1], CHUNK):
        half_sums(live_ref, half_ref[0], pred_ref, score_ref, hi_ref, lo_ref, out_ref, acc, at)


def gram_sums(live, core, tot, rest, design, score):
    genes, cells = rest.shape
    packed = jax.ShapeDtypeStruct((16, 48, 128), F32)
    acc = pltpu.VMEM((4, genes // 2, 128), F32)
    pred, hi, lo, given = pl.pallas_call(
        given_kernel,
        in_specs=[smem(), smem(), vmem(), vmem(), vmem(), vmem()],
        out_specs=[vmem()] * 4,
        out_shape=[
            jax.ShapeDtypeStruct((genes, cells), F32),
            jax.ShapeDtypeStruct((512, cells), BF16),
            jax.ShapeDtypeStruct((512, cells), BF16),
            packed,
        ],
        scratch_shapes=[pltpu.VMEM((1, cells), F32), acc],
        compiler_params=params(),
        name="gram_given",
    )(live, 1 - core, tot, rest, design, score)
    arrived = lax.ppermute(given, "cell", OTHER_CORE)
    kept = pl.pallas_call(
        kept_kernel,
        in_specs=[smem(), smem(), vmem(), vmem(), vmem(), vmem()],
        out_specs=vmem(),
        out_shape=packed,
        scratch_shapes=[acc],
        compiler_params=params(),
        name="gram_kept",
    )(live, core, pred, score, hi, lo)
    return pred, kept + arrived


def solve_kernel(parts_ref, out_ref, table):
    total = parts_ref[0]
    for j in range(1, parts_ref.shape[0]):
        total = total + parts_ref[j]
    turned = jnp.concatenate([total, jnp.zeros((80, 128), F32)], axis=0).T
    for t in range(4):
        moved = turned if t == 0 else pltpu.roll(turned, 128 - 12 * t, axis=1)
        table[128 * t : 128 * (t + 1), :] = moved
    row16 = lax.broadcasted_iota(jnp.int32, (SPL, 128), 0)
    row32 = lax.broadcasted_iota(jnp.int32, (COLS, 128), 0)
    diag, near = table[0:16, :] + 1.0, table[16:32, :]
    below = pltpu.roll(near, 1, axis=0)
    system = []
    for j in range(SPL):
        top = jnp.where(row16 == j, diag, 0.0)
        top = jnp.where(row16 == j - 1, near, top)
        top = jnp.where(row16 == j + 1, below, top)
        system.append(jnp.concatenate([top, table[32 + 16 * j : 48 + 16 * j, :]], axis=0))
    for q in range(SPL):
        top = table[pl.ds(32 + q, 16, stride=16), :]
        if q < 8:
            first = table[288 + 8 * q : 296 + 8 * q, :]
            second = table[352 + 8 * q : 360 + 8 * q, :]
        else:
            first = table[pl.ds(344 + q, 8, stride=8), :]
            second = table[352 + 8 * q : 360 + 8 * q, :]
        column = jnp.concatenate([top, first, second], axis=0)
        system.append(jnp.where(row32 == 16 + q, column + 1.0, column))
    rhs = table[480:512, :]
    scale = jnp.zeros((COLS, 128), F32)
    for k in range(COLS):
        column = system[k]
        inverse = 1.0 / column[k : k + 1, :]
        scale = jnp.where(row32 == k, inverse, scale)
        ratio = jnp.where(row32 == k, 0.0, column * inverse)
        touched = [j for j in range(k + 1, COLS) if j >= SPL or j == k + 1]
        for j in touched:
            system[j] = system[j] - ratio * column[j : j + 1, :]
        rhs = rhs - ratio * rhs[k : k + 1, :]
    answer = rhs * scale
    flat = jnp.concatenate([answer, jnp.zeros((96, 128), F32)], axis=0).T
    line = jnp.concatenate([flat[g : g + 1, :COLS] for g in range(12)], axis=1)
    out_ref[...] = jnp.broadcast_to(line[None], out_ref.shape)


def solve(parts):
    return pl.pallas_call(
        solve_kernel,
        in_specs=[vmem()],
        out_specs=vmem(),
        out_shape=jax.ShapeDtypeStruct((32, 1, 384), F32),
        scratch_shapes=[pltpu.VMEM((512, 128), F32)],
        compiler_params=params(),
        name="solve",
    )(parts)


def update_kernel(
    live_ref, core_ref, steps_ref, pred_ref, design_ref, load_ref, fact_ref,
    by_load_ref, by_fact_ref,
    out_hbm, kept_ref, given_ref, beta_hbm, left, loads, sums, out, beta_out, sent,
):
    steps = steps_ref[...]
    beta = jnp.concatenate([steps[:, COLS * g : COLS * (g + 1)] for g in range(12)], axis=0)
    b1, b2, b3 = split3(beta)
    left[...] = jnp.concatenate([b1, b1, b2, b2, b1, b3], axis=1)
    load = load_ref[...]
    wide = load.astype(F32)
    l1, l2 = split2(wide * wide)
    loads[...] = jnp.concatenate([load, l1, l2], axis=0)

    cells = pred_ref.shape[1]
    sends = []
    for at in range(0, cells, CHUNK):
        here = pl.ds(at, CHUNK)
        d1, d2, d3 = (design_ref[32 * i : 32 * (i + 1), here] for i in range(3))
        change = dot(left[...], jnp.concatenate([d1, d2, d1, d2, d3, d1], axis=0), NN)
        slot = lax.broadcasted_iota(jnp.int32, (1, CHUNK), 1) + at
        mask = (slot < live_ref[0]).astype(F32)
        w1, w2 = split2(jnp.exp(pred_ref[:, here] + change) * mask)
        first = dot(loads[...], w1, NN)
        second = dot(loads[: 2 * FACT], w2, NN)
        grad = by_load_ref[:, here] - (first[:FACT] + second[:FACT])
        curv = (first[FACT : 2 * FACT] + first[2 * FACT :]) + second[FACT:]
        for z in range(8):
            out[z, :8, here] = grad[8 * z : 8 * (z + 1), :]
            out[z, 8:, here] = curv[8 * z : 8 * (z + 1), :]
        send = pltpu.make_async_copy(
            out.at[:, :, here], out_hbm.at[:, :, here], sent.at[at // CHUNK]
        )
        send.start()
        sends.append(send)
        fact = fact_ref[:, here]
        wide = fact.astype(F32)
        f1, f2 = split2(wide * wide)
        first = dot(jnp.concatenate([fact, f1, f2], axis=0), w1, NT)
        second = dot(jnp.concatenate([fact, f1], axis=0), w2, NT)
        grad = first[:FACT] + second[:FACT]
        curv = (first[FACT : 2 * FACT] + first[2 * FACT :]) + second[FACT:]
        for h in range(2):
            rows = slice(32 * h, 32 * (h + 1))
            if at > 0:
                sums[h, :32, :] -= grad[rows]
                sums[h, 32:, :] += curv[rows]
            else:
                sums[h, :32, :] = by_fact_ref[rows, :] - grad[rows]
                sums[h, 32:, :] = curv[rows]

    beta_out[...] = beta.T
    send = pltpu.make_async_copy(beta_out, beta_hbm, sent.at[cells // CHUNK])
    send.start()
    sends.append(send)
    kept_ref[...] = sums[core_ref[0]]
    given_ref[...] = sums[1 - core_ref[0]]
    for send in sends:
        send.wait()


def update(live, core, steps, pred, design, load, fact, by_load, by_fact):
    genes, cells = pred.shape
    return pl.pallas_call(
        update_kernel,
        in_specs=[smem(), smem()] + [vmem()] * 7,
        out_specs=[hbm(), vmem(), vmem(), hbm()],
        out_shape=[
            pltpu.HBM((8, 16, cells), F32),
            jax.ShapeDtypeStruct((FACT, genes), F32),
            jax.ShapeDtypeStruct((FACT, genes), F32),
            pltpu.HBM((COLS, genes), F32),
        ],
        scratch_shapes=[
            pltpu.VMEM((genes, 6 * COLS), BF16), pltpu.VMEM((3 * FACT, genes), BF16),
            pltpu.VMEM((2, FACT, genes), F32), pltpu.VMEM((8, 16, cells), F32),
            pltpu.VMEM((COLS, genes), F32),
            pltpu.SemaphoreType.DMA((cells // CHUNK + 1,)),
        ],
        compiler_params=params(),
        name="update",
    )(live, core, steps, pred, design, load, fact, by_load, by_fact)


def score_kernel(core_ref, mine_ref, other_ref, out_hbm, sent):
    core = core_ref[0]
    sends = [
        pltpu.make_async_copy(
            ref, out_hbm.at[pl.ds(pl.multiple_of(32 * half, 32), 32), :], sent.at[i]
        )
        for i, (half, ref) in enumerate(((core, mine_ref), (1 - core, other_ref)))
    ]
    for send in sends:
        send.start()
    for send in sends:
        send.wait()


def joined_score(core, mine, other):
    return pl.pallas_call(
        score_kernel,
        in_specs=[smem(), vmem(), vmem()],
        out_specs=hbm(),
        out_shape=pltpu.HBM((FACT, mine.shape[1]), F32),
        scratch_shapes=[pltpu.SemaphoreType.DMA((2,))],
        compiler_params=params(),
        name="joined_score",
    )(core, mine, other)


def factor_kernel(parts_ref, out_hbm, stage, sent):
    total = parts_ref[0]
    for j in range(1, parts_ref.shape[0]):
        total = total + parts_ref[j]
    stage[...] = total[:8, :] / (total[8:, :] + 1.0)
    sends = [
        pltpu.make_async_copy(stage, out_hbm.at[z], sent.at[z]) for z in range(out_hbm.shape[0])
    ]
    for send in sends:
        send.start()
    for send in sends:
        send.wait()


def factor_share(parts):
    peers, _, cells = parts.shape
    return pl.pallas_call(
        factor_kernel,
        in_specs=[vmem()],
        out_specs=hbm(),
        out_shape=pltpu.HBM((peers, 8, cells), F32),
        scratch_shapes=[pltpu.VMEM((8, cells), F32), pltpu.SemaphoreType.DMA((peers,))],
        compiler_params=params(),
        name="factor_share",
    )(parts)


def settle_kernel(value_ref, out_hbm, sent):
    sends = [
        pltpu.make_async_copy(value_ref.at[z], out_hbm.at[z], sent.at[z])
        for z in range(value_ref.shape[0])
    ]
    for send in sends:
        send.start()
    for send in sends:
        send.wait()


def settled(value):
    return pl.pallas_call(
        settle_kernel,
        in_specs=[vmem()],
        out_specs=hbm(),
        out_shape=pltpu.HBM(value.shape, value.dtype),
        scratch_shapes=[pltpu.SemaphoreType.DMA((value.shape[0],))],
        compiler_params=params(),
        name="settled",
    )(value)


def exchange(value, axis, groups=None):
    return lax.all_to_all(
        value, axis, split_axis=0, concat_axis=0, tiled=True, axis_index_groups=groups
    )


def partners(move):
    def index(x, y, core):
        return (x * 4 + y) * 2 + core

    return [
        (index(x, y, core), index(*move(x, y, core)))
        for x in range(4)
        for y in range(4)
        for core in range(2)
    ]


def around(at, size):
    return [min((i - at) % size, (at - i) % size) for i in range(size)]


def nearest_first(x, y):
    far_x, far_y = around(x, 4), around(y, 4)
    chips = [(i, j) for i in range(4) for j in range(4)]
    return sorted(chips, key=lambda chip: far_x[chip[0]] + far_y[chip[1]])


FIRST = (3, 2, 5)
SAME_CORE = [[(4 * x + y) * 2 + core for x, y in nearest_first(*FIRST[:2])] for core in range(2)]
CORE_FIRST = [SAME_CORE[0] + SAME_CORE[1]]
RING = [[(FIRST[2] + step) % 8 for step in (0, 1, -1, 2, -2, 3, -3, 4)]]
OTHER_CORE = partners(lambda x, y, c: (x, y, 1 - c))
STAGES = [
    [
        partners(lambda x, y, c, k=k: (x ^ k, y, c) if c == swap else (x, y ^ k, c))
        for k in (1, 2, 3)
    ]
    for swap in (0, 1)
]


def local(
    counts, batch_id, live_cells, knot_bin, depth_frac, cell_covariates,
    coefficients, batch_effect, factors, loadings,
):
    fact, load = factors.T, loadings.T
    tot = exchange(cell_totals(counts, 8), "gene", RING)
    rest, design, score, by_load, by_fact = prepare(
        live_cells, counts, knot_bin[None], depth_frac[None], batch_id[None],
        cell_covariates, coefficients.T, batch_effect.T, load, fact,
    )
    core = (lax.axis_index("cell") % 2)[None]
    pred, packed = gram_sums(live_cells, core, tot, rest, design, score)
    steps = exchange(solve(exchange(packed, "cell", SAME_CORE)), "cell", CORE_FIRST)
    pieces, kept, given, beta = update(
        live_cells, core, steps.reshape(32, 384), pred, design, load, fact, by_load, by_fact
    )
    arrived = exchange(pieces, "gene", RING)

    value = kept + lax.ppermute(given, "cell", OTHER_CORE)
    for moves in STAGES:
        near, across, beside = (lax.ppermute(value, "cell", pairs) for pairs in moves)
        value = (value + near) + (across + beside)
    gathered = settled(exchange(factor_share(arrived), "gene", RING))
    mine = value[:32] / jnp.sqrt(value[32:] + 1.0)
    other = lax.ppermute(mine, "cell", OTHER_CORE)
    score = joined_score(core, mine, other)
    factor_step = gathered.reshape(FACT, -1)
    return beta.T, factor_step.T, score.T


def solution(mesh):
    placed = (
        P("gene", "cell"),
        P("cell"),
        P("cell"),
        P("cell"),
        P("cell"),
        P(None, "cell"),
        P("gene", None),
        P("gene", None),
        P("cell", None),
        P("gene", None),
    )
    return jax.shard_map(
        local,
        mesh=mesh,
        in_specs=placed,
        out_specs=(P("gene", None), P("cell", None), P("gene", None)),
        check_vma=False,
    )
```

```python
import functools

import jax
import jax.numpy as jnp
from jax import lax
from jax.experimental import pallas as pl
from jax.experimental.pallas import tpu as pltpu
from jax.sharding import PartitionSpec as P

GENES = 3072
SPL = 16
COLS = 32
FACT = 64
CHUNK = 256
F32 = jnp.float32
BF16 = jnp.bfloat16
NN = (((1,), (0,)), ((), ()))
NT = (((1,), (1,)), ((), ()))
TN = (((0,), (0,)), ((), ()))
MIB = 1024 * 1024


def dot(a, b, dims):
    return lax.dot_general(a, b, dims, preferred_element_type=F32)


def split2(x):
    hi = x.astype(BF16)
    return hi, (x - hi.astype(F32)).astype(BF16)


def split3(x):
    hi = x.astype(BF16)
    rest = x - hi.astype(F32)
    mid = rest.astype(BF16)
    return hi, mid, (rest - mid.astype(F32)).astype(BF16)


def smem():
    return pl.BlockSpec(memory_space=pltpu.SMEM)


def vmem():
    return pl.BlockSpec(memory_space=pltpu.VMEM)


def hbm():
    return pl.BlockSpec(memory_space=pltpu.HBM)


def params(mib=16):
    return pltpu.CompilerParams(vmem_limit_bytes=mib * MIB)


def totals_kernel(counts_ref, out_ref, rows, stage, arrived, sent):
    blocks, size = rows.shape[0], rows.shape[1]

    def copy(b):
        return pltpu.make_async_copy(
            counts_ref.at[pl.ds(b * size, size), :], rows.at[b], arrived.at[b]
        )

    for b in range(blocks):
        copy(b).start()
    total = jnp.zeros((8, rows.shape[2]), F32)
    for b in range(blocks):
        copy(b).wait()
        part = rows[b, :8, :]
        for i in range(8, size, 8):
            part = part + rows[b, i : i + 8, :]
        total = total + part.astype(F32)
    total = jnp.sum(total, axis=0, keepdims=True)
    for i in range(8):
        stage[i : i + 1, :] = total[:, 128 * i : 128 * (i + 1)]
    sends = [
        pltpu.make_async_copy(stage, out_ref.at[z], sent.at[z]) for z in range(out_ref.shape[0])
    ]
    for send in sends:
        send.start()
    for send in sends:
        send.wait()


def cell_totals(counts, peers):
    genes, cells = counts.shape
    blocks = 12
    return pl.pallas_call(
        totals_kernel,
        in_specs=[hbm()],
        out_specs=hbm(),
        out_shape=pltpu.HBM((peers, 8, 128), F32),
        scratch_shapes=[
            pltpu.VMEM((blocks, genes // blocks, cells), jnp.int32),
            pltpu.VMEM((8, 128), F32),
            pltpu.SemaphoreType.DMA((blocks,)),
            pltpu.SemaphoreType.DMA((peers,)),
        ],
        compiler_params=params(),
        name="cell_totals",
    )(pltpu.with_memory_space_constraint(counts, pltpu.HBM))


def prepare_kernel(
    live_ref, counts_hbm, knot_hbm, frac_hbm, batch_hbm, cov_hbm, coef_hbm, shift_hbm,
    load_hbm, fact_hbm,
    rest_ref, design_ref, score_ref, by_load_ref, by_fact_ref,
    counts_all, knot_all, frac_all, batch_all, cov_all, coef, shift, load, fact_all, arrived,
):
    pairs = (
        (knot_hbm, knot_all), (frac_hbm, frac_all), (batch_hbm, batch_all), (cov_hbm, cov_all),
        (coef_hbm, coef), (shift_hbm, shift), (load_hbm, load), (fact_hbm, fact_all),
    )
    copies = [
        pltpu.make_async_copy(source, target, arrived.at[i])
        for i, (source, target) in enumerate(pairs)
    ]
    cells = rest_ref.shape[1]
    blocks = [
        pltpu.make_async_copy(
            counts_hbm.at[:, pl.ds(at, CHUNK)], counts_all.at[:, pl.ds(at, CHUNK)],
            arrived.at[len(pairs) + at // CHUNK],
        )
        for at in range(0, cells, CHUNK)
    ]
    for copy in copies + blocks:
        copy.start()
    for copy in copies:
        copy.wait()
    c1, c2, c3 = split3(coef[...])
    b1, b2, b3 = split3(shift[...])
    left = jnp.concatenate([c1, c1, c2, c2, c1, c3, b1, b2, b3, load[...]], axis=0)
    score, by_fact = 0.0, 0.0
    for at in range(0, cells, CHUNK):
        here = pl.ds(at, CHUNK)
        knot, frac = knot_all[:, here], frac_all[:, here]
        cov, fact = cov_all[:, here], fact_all[:, here]
        levels = lax.broadcasted_iota(jnp.int32, (SPL, CHUNK), 0)
        hat = jnp.where(levels == knot, 1.0 - frac, 0.0)
        hat = hat + jnp.where(levels == knot + 1, frac, 0.0)
        d1, d2, d3 = split3(jnp.concatenate([hat, cov], axis=0))
        terms = jnp.concatenate([d1, d2, d3], axis=0)
        design_ref[:, here] = terms
        batches = lax.broadcasted_iota(jnp.int32, (64, CHUNK), 0)
        onehot = (batches == batch_all[:, here]).astype(F32).astype(BF16)
        right = jnp.concatenate([d1, d2, d1, d2, d3, d1, onehot, onehot, onehot, fact], axis=0)
        rest_ref[:, here] = dot(left, right, TN)

        blocks[at // CHUNK].wait()
        slot = lax.broadcasted_iota(jnp.int32, (1, CHUNK), 1) + at
        mask = (slot < live_ref[0]).astype(F32)
        counts = (counts_all[:, here].astype(F32) * mask).astype(BF16)
        by_load_ref[:, here] = dot(load[...], counts, NN)
        by_fact = by_fact + dot(fact, counts, NT)
        score = score + dot(counts, terms, NT)
    by_fact_ref[...] = by_fact
    value = score[:, :32] + score[:, 32:64] + score[:, 64:96]
    blank = jnp.zeros((value.shape[0], 96), F32)
    score_ref[...] = jnp.concatenate([blank, value], axis=1)


def prepare(live, counts, knot, frac, batch, cov, coef, shift, load, fact):
    genes, cells = counts.shape
    arrays = [
        pltpu.with_memory_space_constraint(a, pltpu.HBM)
        for a in (counts, knot, frac, batch, cov, coef, shift, load, fact)
    ]
    return pl.pallas_call(
        prepare_kernel,
        in_specs=[smem()] + [hbm()] * len(arrays),
        out_specs=[vmem()] * 5,
        out_shape=[
            jax.ShapeDtypeStruct((genes, cells), F32),
            jax.ShapeDtypeStruct((96, cells), BF16),
            jax.ShapeDtypeStruct((genes, 128), F32),
            jax.ShapeDtypeStruct((FACT, cells), F32),
            jax.ShapeDtypeStruct((FACT, genes), F32),
        ],
        scratch_shapes=[pltpu.VMEM(a.shape, a.dtype) for a in arrays]
        + [pltpu.SemaphoreType.DMA((len(arrays) - 1 + cells // CHUNK,))],
        compiler_params=params(),
        name="prepare",
    )(live, *arrays)


def half_rows(ref, half, here):
    rows = [
        ref[pl.ds(pl.multiple_of(32 * g + 16 * half, 16), 16), here] for g in range(12)
    ]
    return jnp.concatenate(rows, axis=0)


def half_sums(live_ref, half, pred_ref, score_ref, hi_ref, lo_ref, out_ref, acc, at):
    here = pl.ds(at, CHUNK)
    slot = lax.broadcasted_iota(jnp.int32, (1, CHUNK), 1) + at
    mask = (slot < live_ref[0]).astype(F32)
    w1, w2 = split2(jnp.exp(half_rows(pred_ref, half, here)) * mask)
    hi, lo = hi_ref[:, here], lo_ref[:, here]
    gram = dot(w1, hi, NT) + dot(w1, lo, NT) + dot(w2, hi, NT)
    for t in range(4):
        part = gram[:, 128 * t : 128 * (t + 1)]
        if at > 0:
            acc[t] += part
        else:
            acc[t] = part + half_rows(score_ref, half, slice(None)) if t == 3 else part
    if at + CHUNK == pred_ref.shape[1]:
        for chip in range(16):
            for t in range(4):
                out_ref[chip, 12 * t : 12 * (t + 1), :] = acc[t, pl.ds(chip, 12, stride=16), :]


def given_kernel(
    live_ref, half_ref, tot_ref, rest_ref, design_ref, score_ref,
    pred_ref, hi_ref, lo_ref, out_ref, offset, acc,
):
    total = jnp.sum(tot_ref[...], axis=0)
    value = jnp.log((1.0 + total) / GENES)
    for i in range(8):
        offset[:, 128 * i : 128 * (i + 1)] = value[i : i + 1, :]

    for at in range(0, rest_ref.shape[1], CHUNK):
        here = pl.ds(at, CHUNK)

        def put(row, value):
            hi, lo = split2(value)
            hi_ref[row : row + value.shape[0], here] = hi
            lo_ref[row : row + value.shape[0], here] = lo

        d1, d2, d3 = (design_ref[32 * i : 32 * (i + 1), here] for i in range(3))
        design = (d1.astype(F32) + d2.astype(F32)) + d3.astype(F32)
        hat, cov = design[:SPL], design[SPL:]
        put(0, hat * hat)
        put(16, hat * pltpu.roll(hat, SPL - 1, axis=0))
        for p in range(SPL):
            put(32 + 16 * p, hat[p : p + 1, :] * cov)
        low, high = cov[:8], cov[8:]
        for i in range(0, 8, 2):
            for row, left, right in ((288, low, low), (352, low, high), (416, high, high)):
                both = [left[i : i + 1] * right, left[i + 1 : i + 2] * right]
                put(row + 8 * i, jnp.concatenate(both, axis=0))
        put(480, -design)
        pred_ref[:, here] = rest_ref[:, here] + offset[:, here]
        half_sums(live_ref, half_ref[0], pred_ref, score_ref, hi_ref, lo_ref, out_ref, acc, at)


def kept_kernel(live_ref, half_ref, pred_ref, score_ref, hi_ref, lo_ref, out_ref, acc):
    for at in range(0, pred_ref.shape[1], CHUNK):
        half_sums(live_ref, half_ref[0], pred_ref, score_ref, hi_ref, lo_ref, out_ref, acc, at)


def gram_sums(live, core, tot, rest, design, score):
    genes, cells = rest.shape
    packed = jax.ShapeDtypeStruct((16, 48, 128), F32)
    acc = pltpu.VMEM((4, genes // 2, 128), F32)
    pred, hi, lo, given = pl.pallas_call(
        given_kernel,
        in_specs=[smem(), smem(), vmem(), vmem(), vmem(), vmem()],
        out_specs=[vmem()] * 4,
        out_shape=[
            jax.ShapeDtypeStruct((genes, cells), F32),
            jax.ShapeDtypeStruct((512, cells), BF16),
            jax.ShapeDtypeStruct((512, cells), BF16),
            packed,
        ],
        scratch_shapes=[pltpu.VMEM((1, cells), F32), acc],
        compiler_params=params(),
        name="gram_given",
    )(live, 1 - core, tot, rest, design, score)
    arrived = lax.ppermute(given, "cell", OTHER_CORE)
    kept = pl.pallas_call(
        kept_kernel,
        in_specs=[smem(), smem(), vmem(), vmem(), vmem(), vmem()],
        out_specs=vmem(),
        out_shape=packed,
        scratch_shapes=[acc],
        compiler_params=params(),
        name="gram_kept",
    )(live, core, pred, score, hi, lo)
    return pred, kept + arrived


def solve_kernel(parts_ref, out_ref, table):
    total = parts_ref[0]
    for j in range(1, parts_ref.shape[0]):
        total = total + parts_ref[j]
    turned = jnp.concatenate([total, jnp.zeros((80, 128), F32)], axis=0).T
    for t in range(4):
        moved = turned if t == 0 else pltpu.roll(turned, 128 - 12 * t, axis=1)
        table[128 * t : 128 * (t + 1), :] = moved
    row16 = lax.broadcasted_iota(jnp.int32, (SPL, 128), 0)
    row32 = lax.broadcasted_iota(jnp.int32, (COLS, 128), 0)
    diag, near = table[0:16, :] + 1.0, table[16:32, :]
    below = pltpu.roll(near, 1, axis=0)
    system = []
    for j in range(SPL):
        top = jnp.where(row16 == j, diag, 0.0)
        top = jnp.where(row16 == j - 1, near, top)
        top = jnp.where(row16 == j + 1, below, top)
        system.append(jnp.concatenate([top, table[32 + 16 * j : 48 + 16 * j, :]], axis=0))
    for q in range(SPL):
        top = table[pl.ds(32 + q, 16, stride=16), :]
        if q < 8:
            first = table[288 + 8 * q : 296 + 8 * q, :]
            second = table[352 + 8 * q : 360 + 8 * q, :]
        else:
            first = table[pl.ds(344 + q, 8, stride=8), :]
            second = table[352 + 8 * q : 360 + 8 * q, :]
        column = jnp.concatenate([top, first, second], axis=0)
        system.append(jnp.where(row32 == 16 + q, column + 1.0, column))
    rhs = table[480:512, :]
    scale = jnp.zeros((COLS, 128), F32)
    for k in range(COLS):
        column = system[k]
        inverse = 1.0 / column[k : k + 1, :]
        scale = jnp.where(row32 == k, inverse, scale)
        ratio = jnp.where(row32 == k, 0.0, column * inverse)
        touched = [j for j in range(k + 1, COLS) if j >= SPL or j == k + 1]
        for j in touched:
            system[j] = system[j] - ratio * column[j : j + 1, :]
        rhs = rhs - ratio * rhs[k : k + 1, :]
    answer = rhs * scale
    flat = jnp.concatenate([answer, jnp.zeros((96, 128), F32)], axis=0).T
    line = jnp.concatenate([flat[g : g + 1, :COLS] for g in range(12)], axis=1)
    out_ref[...] = jnp.broadcast_to(line[None], out_ref.shape)


def solve(parts):
    return pl.pallas_call(
        solve_kernel,
        in_specs=[vmem()],
        out_specs=vmem(),
        out_shape=jax.ShapeDtypeStruct((32, 1, 384), F32),
        scratch_shapes=[pltpu.VMEM((512, 128), F32)],
        compiler_params=params(),
        name="solve",
    )(parts)


def update_kernel(
    live_ref, core_ref, steps_ref, pred_ref, design_ref, load_ref, fact_ref,
    by_load_ref, by_fact_ref,
    out_hbm, kept_ref, given_ref, beta_hbm, left, loads, sums, out, beta_out, sent,
):
    steps = steps_ref[...]
    beta = jnp.concatenate([steps[:, COLS * g : COLS * (g + 1)] for g in range(12)], axis=0)
    b1, b2, b3 = split3(beta)
    left[...] = jnp.concatenate([b1, b1, b2, b2, b1, b3], axis=1)
    load = load_ref[...]
    wide = load.astype(F32)
    l1, l2 = split2(wide * wide)
    loads[...] = jnp.concatenate([load, l1, l2], axis=0)

    cells = pred_ref.shape[1]
    sends = []
    for at in range(0, cells, CHUNK):
        here = pl.ds(at, CHUNK)
        d1, d2, d3 = (design_ref[32 * i : 32 * (i + 1), here] for i in range(3))
        change = dot(left[...], jnp.concatenate([d1, d2, d1, d2, d3, d1], axis=0), NN)
        slot = lax.broadcasted_iota(jnp.int32, (1, CHUNK), 1) + at
        mask = (slot < live_ref[0]).astype(F32)
        w1, w2 = split2(jnp.exp(pred_ref[:, here] + change) * mask)
        first = dot(loads[...], w1, NN)
        second = dot(loads[: 2 * FACT], w2, NN)
        grad = by_load_ref[:, here] - (first[:FACT] + second[:FACT])
        curv = (first[FACT : 2 * FACT] + first[2 * FACT :]) + second[FACT:]
        for z in range(8):
            out[z, :8, here] = grad[8 * z : 8 * (z + 1), :]
            out[z, 8:, here] = curv[8 * z : 8 * (z + 1), :]
        send = pltpu.make_async_copy(
            out.at[:, :, here], out_hbm.at[:, :, here], sent.at[at // CHUNK]
        )
        send.start()
        sends.append(send)
        fact = fact_ref[:, here]
        wide = fact.astype(F32)
        f1, f2 = split2(wide * wide)
        first = dot(jnp.concatenate([fact, f1, f2], axis=0), w1, NT)
        second = dot(jnp.concatenate([fact, f1], axis=0), w2, NT)
        grad = first[:FACT] + second[:FACT]
        curv = (first[FACT : 2 * FACT] + first[2 * FACT :]) + second[FACT:]
        for h in range(2):
            rows = slice(32 * h, 32 * (h + 1))
            if at > 0:
                sums[h, :32, :] -= grad[rows]
                sums[h, 32:, :] += curv[rows]
            else:
                sums[h, :32, :] = by_fact_ref[rows, :] - grad[rows]
                sums[h, 32:, :] = curv[rows]

    beta_out[...] = beta.T
    send = pltpu.make_async_copy(beta_out, beta_hbm, sent.at[cells // CHUNK])
    send.start()
    sends.append(send)
    kept_ref[...] = sums[core_ref[0]]
    given_ref[...] = sums[1 - core_ref[0]]
    for send in sends:
        send.wait()


def update(live, core, steps, pred, design, load, fact, by_load, by_fact):
    genes, cells = pred.shape
    return pl.pallas_call(
        update_kernel,
        in_specs=[smem(), smem()] + [vmem()] * 7,
        out_specs=[hbm(), vmem(), vmem(), hbm()],
        out_shape=[
            pltpu.HBM((8, 16, cells), F32),
            jax.ShapeDtypeStruct((FACT, genes), F32),
            jax.ShapeDtypeStruct((FACT, genes), F32),
            pltpu.HBM((COLS, genes), F32),
        ],
        scratch_shapes=[
            pltpu.VMEM((genes, 6 * COLS), BF16), pltpu.VMEM((3 * FACT, genes), BF16),
            pltpu.VMEM((2, FACT, genes), F32), pltpu.VMEM((8, 16, cells), F32),
            pltpu.VMEM((COLS, genes), F32),
            pltpu.SemaphoreType.DMA((cells // CHUNK + 1,)),
        ],
        compiler_params=params(),
        name="update",
    )(live, core, steps, pred, design, load, fact, by_load, by_fact)


def score_kernel(core_ref, mine_ref, other_ref, out_hbm, sent):
    core = core_ref[0]
    sends = [
        pltpu.make_async_copy(
            ref, out_hbm.at[pl.ds(pl.multiple_of(32 * half, 32), 32), :], sent.at[i]
        )
        for i, (half, ref) in enumerate(((core, mine_ref), (1 - core, other_ref)))
    ]
    for send in sends:
        send.start()
    for send in sends:
        send.wait()


def joined_score(core, mine, other):
    return pl.pallas_call(
        score_kernel,
        in_specs=[smem(), vmem(), vmem()],
        out_specs=hbm(),
        out_shape=pltpu.HBM((FACT, mine.shape[1]), F32),
        scratch_shapes=[pltpu.SemaphoreType.DMA((2,))],
        compiler_params=params(),
        name="joined_score",
    )(core, mine, other)


def factor_kernel(parts_ref, out_hbm, stage, sent):
    total = parts_ref[0]
    for j in range(1, parts_ref.shape[0]):
        total = total + parts_ref[j]
    stage[...] = total[:8, :] / (total[8:, :] + 1.0)
    sends = [
        pltpu.make_async_copy(stage, out_hbm.at[z], sent.at[z]) for z in range(out_hbm.shape[0])
    ]
    for send in sends:
        send.start()
    for send in sends:
        send.wait()


def factor_share(parts):
    peers, _, cells = parts.shape
    return pl.pallas_call(
        factor_kernel,
        in_specs=[vmem()],
        out_specs=hbm(),
        out_shape=pltpu.HBM((peers, 8, cells), F32),
        scratch_shapes=[pltpu.VMEM((8, cells), F32), pltpu.SemaphoreType.DMA((peers,))],
        compiler_params=params(),
        name="factor_share",
    )(parts)


def settle_kernel(value_ref, out_hbm, sent):
    sends = [
        pltpu.make_async_copy(value_ref.at[z], out_hbm.at[z], sent.at[z])
        for z in range(value_ref.shape[0])
    ]
    for send in sends:
        send.start()
    for send in sends:
        send.wait()


def settled(value):
    return pl.pallas_call(
        settle_kernel,
        in_specs=[vmem()],
        out_specs=hbm(),
        out_shape=pltpu.HBM(value.shape, value.dtype),
        scratch_shapes=[pltpu.SemaphoreType.DMA((value.shape[0],))],
        compiler_params=params(),
        name="settled",
    )(value)


def exchange(value, axis, groups=None):
    return lax.all_to_all(
        value, axis, split_axis=0, concat_axis=0, tiled=True, axis_index_groups=groups
    )


def partners(move):
    def index(x, y, core):
        return (x * 4 + y) * 2 + core

    return [
        (index(x, y, core), index(*move(x, y, core)))
        for x in range(4)
        for y in range(4)
        for core in range(2)
    ]


def around(at, size):
    return [min((i - at) % size, (at - i) % size) for i in range(size)]


def nearest_first(x, y, core):
    far_x, far_y = around(x, 4), around(y, 4)
    chips = [(i, j) if core == 0 else (j, i) for i in range(4) for j in range(4)]
    return sorted(chips, key=lambda chip: far_x[chip[0]] + far_y[chip[1]])


FIRST = (3, 2, 5)
SAME_CORE = [
    [(4 * x + y) * 2 + core for x, y in nearest_first(*FIRST[:2], core)]
    for core in range(2)
]
CORE_FIRST = [SAME_CORE[0] + SAME_CORE[1]]
RING = [[(FIRST[2] + step) % 8 for step in (0, 1, -1, 2, -2, 3, -3, 4)]]
OTHER_CORE = partners(lambda x, y, c: (x, y, 1 - c))
STAGES = [
    [
        partners(lambda x, y, c, k=k: (x ^ k, y, c) if c == swap else (x, y ^ k, c))
        for k in (1, 2, 3)
    ]
    for swap in (0, 1)
]


def local(
    counts, batch_id, live_cells, knot_bin, depth_frac, cell_covariates,
    coefficients, batch_effect, factors, loadings,
):
    fact, load = factors.T, loadings.T
    tot = exchange(cell_totals(counts, 8), "gene", RING)
    rest, design, score, by_load, by_fact = prepare(
        live_cells, counts, knot_bin[None], depth_frac[None], batch_id[None],
        cell_covariates, coefficients.T, batch_effect.T, load, fact,
    )
    core = (lax.axis_index("cell") % 2)[None]
    pred, packed = gram_sums(live_cells, core, tot, rest, design, score)
    steps = exchange(solve(exchange(packed, "cell", SAME_CORE)), "cell", CORE_FIRST)
    pieces, kept, given, beta = update(
        live_cells, core, steps.reshape(32, 384), pred, design, load, fact, by_load, by_fact
    )
    arrived = exchange(pieces, "gene", RING)

    value = kept + lax.ppermute(given, "cell", OTHER_CORE)
    for moves in STAGES:
        near, across, beside = (lax.ppermute(value, "cell", pairs) for pairs in moves)
        value = (value + near) + (across + beside)
    gathered = settled(exchange(factor_share(arrived), "gene", RING))
    mine = value[:32] / jnp.sqrt(value[32:] + 1.0)
    other = lax.ppermute(mine, "cell", OTHER_CORE)
    score = joined_score(core, mine, other)
    factor_step = gathered.reshape(FACT, -1)
    return beta.T, factor_step.T, score.T


def solution(mesh):
    placed = (
        P("gene", "cell"),
        P("cell"),
        P("cell"),
        P("cell"),
        P("cell"),
        P(None, "cell"),
        P("gene", None),
        P("gene", None),
        P("cell", None),
        P("gene", None),
    )
    return jax.shard_map(
        local,
        mesh=mesh,
        in_specs=placed,
        out_specs=(P("gene", None), P("cell", None), P("gene", None)),
        check_vma=False,
    )
```

```python
import functools

import jax
import jax.numpy as jnp
from jax import lax
from jax.experimental import pallas as pl
from jax.experimental.pallas import tpu as pltpu
from jax.sharding import PartitionSpec as P

GENES = 3072
SPL = 16
COLS = 32
FACT = 64
CHUNK = 256
F32 = jnp.float32
BF16 = jnp.bfloat16
NN = (((1,), (0,)), ((), ()))
NT = (((1,), (1,)), ((), ()))
TN = (((0,), (0,)), ((), ()))
MIB = 1024 * 1024


def dot(a, b, dims):
    return lax.dot_general(a, b, dims, preferred_element_type=F32)


def split2(x):
    hi = x.astype(BF16)
    return hi, (x - hi.astype(F32)).astype(BF16)


def split3(x):
    hi = x.astype(BF16)
    rest = x - hi.astype(F32)
    mid = rest.astype(BF16)
    return hi, mid, (rest - mid.astype(F32)).astype(BF16)


def smem():
    return pl.BlockSpec(memory_space=pltpu.SMEM)


def vmem():
    return pl.BlockSpec(memory_space=pltpu.VMEM)


def hbm():
    return pl.BlockSpec(memory_space=pltpu.HBM)


def params(mib=16):
    return pltpu.CompilerParams(vmem_limit_bytes=mib * MIB)


def totals_kernel(counts_ref, out_ref, rows, stage, arrived, sent):
    blocks, size = rows.shape[0], rows.shape[1]

    def copy(b):
        return pltpu.make_async_copy(
            counts_ref.at[pl.ds(b * size, size), :], rows.at[b], arrived.at[b]
        )

    for b in range(blocks):
        copy(b).start()
    total = jnp.zeros((8, rows.shape[2]), F32)
    for b in range(blocks):
        copy(b).wait()
        part = rows[b, :8, :]
        for i in range(8, size, 8):
            part = part + rows[b, i : i + 8, :]
        total = total + part.astype(F32)
    total = jnp.sum(total, axis=0, keepdims=True)
    for i in range(8):
        stage[i : i + 1, :] = total[:, 128 * i : 128 * (i + 1)]
    sends = [
        pltpu.make_async_copy(stage, out_ref.at[z], sent.at[z]) for z in range(out_ref.shape[0])
    ]
    for send in sends:
        send.start()
    for send in sends:
        send.wait()


def cell_totals(counts, peers):
    genes, cells = counts.shape
    blocks = 12
    return pl.pallas_call(
        totals_kernel,
        in_specs=[hbm()],
        out_specs=hbm(),
        out_shape=pltpu.HBM((peers, 8, 128), F32),
        scratch_shapes=[
            pltpu.VMEM((blocks, genes // blocks, cells), jnp.int32),
            pltpu.VMEM((8, 128), F32),
            pltpu.SemaphoreType.DMA((blocks,)),
            pltpu.SemaphoreType.DMA((peers,)),
        ],
        compiler_params=params(),
        name="cell_totals",
    )(pltpu.with_memory_space_constraint(counts, pltpu.HBM))


def prepare_kernel(
    live_ref, counts_hbm, knot_hbm, frac_hbm, batch_hbm, cov_hbm, coef_hbm, shift_hbm,
    load_hbm, fact_hbm,
    rest_ref, design_ref, score_ref, by_load_ref, by_fact_ref,
    counts_all, knot_all, frac_all, batch_all, cov_all, coef, shift, load, fact_all, arrived,
):
    pairs = (
        (knot_hbm, knot_all), (frac_hbm, frac_all), (batch_hbm, batch_all), (cov_hbm, cov_all),
        (coef_hbm, coef), (shift_hbm, shift), (load_hbm, load), (fact_hbm, fact_all),
    )
    copies = [
        pltpu.make_async_copy(source, target, arrived.at[i])
        for i, (source, target) in enumerate(pairs)
    ]
    cells = rest_ref.shape[1]
    blocks = [
        pltpu.make_async_copy(
            counts_hbm.at[:, pl.ds(at, CHUNK)], counts_all.at[:, pl.ds(at, CHUNK)],
            arrived.at[len(pairs) + at // CHUNK],
        )
        for at in range(0, cells, CHUNK)
    ]
    for copy in copies + blocks:
        copy.start()
    for copy in copies:
        copy.wait()
    c1, c2, c3 = split3(coef[...])
    b1, b2, b3 = split3(shift[...])
    left = jnp.concatenate([c1, c1, c2, c2, c1, c3, b1, b2, b3, load[...]], axis=0)
    score, by_fact = 0.0, 0.0
    for at in range(0, cells, CHUNK):
        here = pl.ds(at, CHUNK)
        knot, frac = knot_all[:, here], frac_all[:, here]
        cov, fact = cov_all[:, here], fact_all[:, here]
        levels = lax.broadcasted_iota(jnp.int32, (SPL, CHUNK), 0)
        hat = jnp.where(levels == knot, 1.0 - frac, 0.0)
        hat = hat + jnp.where(levels == knot + 1, frac, 0.0)
        d1, d2, d3 = split3(jnp.concatenate([hat, cov], axis=0))
        terms = jnp.concatenate([d1, d2, d3], axis=0)
        design_ref[:, here] = terms
        batches = lax.broadcasted_iota(jnp.int32, (64, CHUNK), 0)
        onehot = (batches == batch_all[:, here]).astype(F32).astype(BF16)
        right = jnp.concatenate([d1, d2, d1, d2, d3, d1, onehot, onehot, onehot, fact], axis=0)
        rest_ref[:, here] = dot(left, right, TN)

        blocks[at // CHUNK].wait()
        slot = lax.broadcasted_iota(jnp.int32, (1, CHUNK), 1) + at
        mask = (slot < live_ref[0]).astype(F32)
        counts = (counts_all[:, here].astype(F32) * mask).astype(BF16)
        by_load_ref[:, here] = dot(load[...], counts, NN)
        by_fact = by_fact + dot(fact, counts, NT)
        score = score + dot(counts, terms, NT)
    by_fact_ref[...] = by_fact
    value = score[:, :32] + score[:, 32:64] + score[:, 64:96]
    blank = jnp.zeros((value.shape[0], 96), F32)
    score_ref[...] = jnp.concatenate([blank, value], axis=1)


def prepare(live, counts, knot, frac, batch, cov, coef, shift, load, fact):
    genes, cells = counts.shape
    arrays = [
        pltpu.with_memory_space_constraint(a, pltpu.HBM)
        for a in (counts, knot, frac, batch, cov, coef, shift, load, fact)
    ]
    return pl.pallas_call(
        prepare_kernel,
        in_specs=[smem()] + [hbm()] * len(arrays),
        out_specs=[vmem()] * 5,
        out_shape=[
            jax.ShapeDtypeStruct((genes, cells), F32),
            jax.ShapeDtypeStruct((96, cells), BF16),
            jax.ShapeDtypeStruct((genes, 128), F32),
            jax.ShapeDtypeStruct((FACT, cells), F32),
            jax.ShapeDtypeStruct((FACT, genes), F32),
        ],
        scratch_shapes=[pltpu.VMEM(a.shape, a.dtype) for a in arrays]
        + [pltpu.SemaphoreType.DMA((len(arrays) - 1 + cells // CHUNK,))],
        compiler_params=params(),
        name="prepare",
    )(live, *arrays)


def half_rows(ref, half, here):
    rows = [
        ref[pl.ds(pl.multiple_of(32 * g + 16 * half, 16), 16), here] for g in range(12)
    ]
    return jnp.concatenate(rows, axis=0)


def half_sums(live_ref, half, pred_ref, score_ref, hi_ref, lo_ref, out_ref, acc, at):
    here = pl.ds(at, CHUNK)
    slot = lax.broadcasted_iota(jnp.int32, (1, CHUNK), 1) + at
    mask = (slot < live_ref[0]).astype(F32)
    w1, w2 = split2(jnp.exp(half_rows(pred_ref, half, here)) * mask)
    hi, lo = hi_ref[:, here], lo_ref[:, here]
    gram = dot(w1, hi, NT) + dot(w1, lo, NT) + dot(w2, hi, NT)
    for t in range(4):
        part = gram[:, 128 * t : 128 * (t + 1)]
        if at > 0:
            acc[t, : part.shape[0], :] += part
        else:
            start = part + half_rows(score_ref, half, slice(None)) if t == 3 else part
            acc[t, : part.shape[0], :] = start
    if at + CHUNK == pred_ref.shape[1]:
        for chip in range(16):
            for t in range(4):
                out_ref[chip, 12 * t : 12 * (t + 1), :] = acc[t, pl.ds(chip, 12, stride=16), :]


def given_kernel(
    live_ref, half_ref, tot_ref, rest_ref, design_ref, score_ref,
    pred_ref, hi_ref, lo_ref, out_ref, offset, acc,
):
    total = jnp.sum(tot_ref[...], axis=0)
    value = jnp.log((1.0 + total) / GENES)
    for i in range(8):
        offset[:, 128 * i : 128 * (i + 1)] = value[i : i + 1, :]

    for at in range(0, rest_ref.shape[1], CHUNK):
        here = pl.ds(at, CHUNK)

        def put(row, value):
            hi, lo = split2(value)
            hi_ref[row : row + value.shape[0], here] = hi
            lo_ref[row : row + value.shape[0], here] = lo

        d1, d2, d3 = (design_ref[32 * i : 32 * (i + 1), here] for i in range(3))
        design = (d1.astype(F32) + d2.astype(F32)) + d3.astype(F32)
        hat, cov = design[:SPL], design[SPL:]
        put(0, hat * hat)
        put(16, hat * pltpu.roll(hat, SPL - 1, axis=0))
        for p in range(SPL):
            put(32 + 16 * p, hat[p : p + 1, :] * cov)
        low, high = cov[:8], cov[8:]
        for i in range(0, 8, 2):
            for row, left, right in ((288, low, low), (352, low, high), (416, high, high)):
                both = [left[i : i + 1] * right, left[i + 1 : i + 2] * right]
                put(row + 8 * i, jnp.concatenate(both, axis=0))
        put(480, -design)
        pred_ref[:, here] = rest_ref[:, here] + offset[:, here]
        half_sums(live_ref, half_ref[0], pred_ref, score_ref, hi_ref, lo_ref, out_ref, acc, at)


def kept_kernel(live_ref, half_ref, pred_ref, score_ref, hi_ref, lo_ref, out_ref, acc):
    for at in range(0, pred_ref.shape[1], CHUNK):
        half_sums(live_ref, half_ref[0], pred_ref, score_ref, hi_ref, lo_ref, out_ref, acc, at)


def gram_sums(live, core, tot, rest, design, score):
    genes, cells = rest.shape
    packed = jax.ShapeDtypeStruct((16, 48, 128), F32)
    acc = pltpu.VMEM((4, 256, 128), F32)
    pred, hi, lo, given = pl.pallas_call(
        given_kernel,
        in_specs=[smem(), smem(), vmem(), vmem(), vmem(), vmem()],
        out_specs=[vmem()] * 4,
        out_shape=[
            jax.ShapeDtypeStruct((genes, cells), F32),
            jax.ShapeDtypeStruct((512, cells), BF16),
            jax.ShapeDtypeStruct((512, cells), BF16),
            packed,
        ],
        scratch_shapes=[pltpu.VMEM((1, cells), F32), acc],
        compiler_params=params(),
        name="gram_given",
    )(live, 1 - core, tot, rest, design, score)
    arrived = lax.ppermute(given, "cell", OTHER_CORE)
    kept = pl.pallas_call(
        kept_kernel,
        in_specs=[smem(), smem(), vmem(), vmem(), vmem(), vmem()],
        out_specs=vmem(),
        out_shape=packed,
        scratch_shapes=[acc],
        compiler_params=params(),
        name="gram_kept",
    )(live, core, pred, score, hi, lo)
    return pred, kept + arrived


def solve_kernel(parts_ref, out_ref, table):
    total = parts_ref[0]
    for j in range(1, parts_ref.shape[0]):
        total = total + parts_ref[j]
    turned = jnp.concatenate([total, jnp.zeros((80, 128), F32)], axis=0).T
    for t in range(4):
        moved = turned if t == 0 else pltpu.roll(turned, 128 - 12 * t, axis=1)
        table[128 * t : 128 * (t + 1), :] = moved
    row16 = lax.broadcasted_iota(jnp.int32, (SPL, 128), 0)
    row32 = lax.broadcasted_iota(jnp.int32, (COLS, 128), 0)
    diag, near = table[0:16, :] + 1.0, table[16:32, :]
    below = pltpu.roll(near, 1, axis=0)
    system = []
    for j in range(SPL):
        top = jnp.where(row16 == j, diag, 0.0)
        top = jnp.where(row16 == j - 1, near, top)
        top = jnp.where(row16 == j + 1, below, top)
        system.append(jnp.concatenate([top, table[32 + 16 * j : 48 + 16 * j, :]], axis=0))
    for q in range(SPL):
        top = table[pl.ds(32 + q, 16, stride=16), :]
        if q < 8:
            first = table[288 + 8 * q : 296 + 8 * q, :]
            second = table[352 + 8 * q : 360 + 8 * q, :]
        else:
            first = table[pl.ds(344 + q, 8, stride=8), :]
            second = table[352 + 8 * q : 360 + 8 * q, :]
        column = jnp.concatenate([top, first, second], axis=0)
        system.append(jnp.where(row32 == 16 + q, column + 1.0, column))
    rhs = table[480:512, :]
    scale = jnp.zeros((COLS, 128), F32)
    for k in range(COLS):
        column = system[k]
        inverse = 1.0 / column[k : k + 1, :]
        scale = jnp.where(row32 == k, inverse, scale)
        ratio = jnp.where(row32 == k, 0.0, column * inverse)
        touched = [j for j in range(k + 1, COLS) if j >= SPL or j == k + 1]
        for j in touched:
            system[j] = system[j] - ratio * column[j : j + 1, :]
        rhs = rhs - ratio * rhs[k : k + 1, :]
    answer = rhs * scale
    flat = jnp.concatenate([answer, jnp.zeros((96, 128), F32)], axis=0).T
    line = jnp.concatenate([flat[g : g + 1, :COLS] for g in range(12)], axis=1)
    out_ref[...] = jnp.broadcast_to(line[None], out_ref.shape)


def solve(parts):
    return pl.pallas_call(
        solve_kernel,
        in_specs=[vmem()],
        out_specs=vmem(),
        out_shape=jax.ShapeDtypeStruct((32, 1, 384), F32),
        scratch_shapes=[pltpu.VMEM((512, 128), F32)],
        compiler_params=params(),
        name="solve",
    )(parts)


def update_kernel(
    live_ref, core_ref, steps_ref, pred_ref, design_ref, load_ref, fact_ref,
    by_load_ref, by_fact_ref,
    out_hbm, kept_ref, given_ref, beta_hbm, left, loads, sums, out, beta_out, sent,
):
    steps = steps_ref[...]
    beta = jnp.concatenate([steps[:, COLS * g : COLS * (g + 1)] for g in range(12)], axis=0)
    b1, b2, b3 = split3(beta)
    left[...] = jnp.concatenate([b1, b1, b2, b2, b1, b3], axis=1)
    load = load_ref[...]
    wide = load.astype(F32)
    l1, l2 = split2(wide * wide)
    loads[...] = jnp.concatenate([load, l1, l2], axis=0)

    cells = pred_ref.shape[1]
    sends = []
    for at in range(0, cells, CHUNK):
        here = pl.ds(at, CHUNK)
        d1, d2, d3 = (design_ref[32 * i : 32 * (i + 1), here] for i in range(3))
        change = dot(left[...], jnp.concatenate([d1, d2, d1, d2, d3, d1], axis=0), NN)
        slot = lax.broadcasted_iota(jnp.int32, (1, CHUNK), 1) + at
        mask = (slot < live_ref[0]).astype(F32)
        w1, w2 = split2(jnp.exp(pred_ref[:, here] + change) * mask)
        first = dot(loads[...], w1, NN)
        second = dot(loads[: 2 * FACT], w2, NN)
        grad = by_load_ref[:, here] - (first[:FACT] + second[:FACT])
        curv = (first[FACT : 2 * FACT] + first[2 * FACT :]) + second[FACT:]
        for z in range(8):
            out[z, :8, here] = grad[8 * z : 8 * (z + 1), :]
            out[z, 8:, here] = curv[8 * z : 8 * (z + 1), :]
        send = pltpu.make_async_copy(
            out.at[:, :, here], out_hbm.at[:, :, here], sent.at[at // CHUNK]
        )
        send.start()
        sends.append(send)
        fact = fact_ref[:, here]
        wide = fact.astype(F32)
        f1, f2 = split2(wide * wide)
        first = dot(jnp.concatenate([fact, f1, f2], axis=0), w1, NT)
        second = dot(jnp.concatenate([fact, f1], axis=0), w2, NT)
        grad = first[:FACT] + second[:FACT]
        curv = (first[FACT : 2 * FACT] + first[2 * FACT :]) + second[FACT:]
        for h in range(2):
            rows = slice(32 * h, 32 * (h + 1))
            if at > 0:
                sums[h, :32, :] -= grad[rows]
                sums[h, 32:, :] += curv[rows]
            else:
                sums[h, :32, :] = by_fact_ref[rows, :] - grad[rows]
                sums[h, 32:, :] = curv[rows]

    beta_out[...] = beta.T
    send = pltpu.make_async_copy(beta_out, beta_hbm, sent.at[cells // CHUNK])
    send.start()
    sends.append(send)
    kept_ref[...] = sums[core_ref[0]]
    given_ref[...] = sums[1 - core_ref[0]]
    for send in sends:
        send.wait()


def update(live, core, steps, pred, design, load, fact, by_load, by_fact):
    genes, cells = pred.shape
    return pl.pallas_call(
        update_kernel,
        in_specs=[smem(), smem()] + [vmem()] * 7,
        out_specs=[hbm(), vmem(), vmem(), hbm()],
        out_shape=[
            pltpu.HBM((8, 16, cells), F32),
            jax.ShapeDtypeStruct((FACT, genes), F32),
            jax.ShapeDtypeStruct((FACT, genes), F32),
            pltpu.HBM((COLS, genes), F32),
        ],
        scratch_shapes=[
            pltpu.VMEM((genes, 6 * COLS), BF16), pltpu.VMEM((3 * FACT, genes), BF16),
            pltpu.VMEM((2, FACT, genes), F32), pltpu.VMEM((8, 16, cells), F32),
            pltpu.VMEM((COLS, genes), F32),
            pltpu.SemaphoreType.DMA((cells // CHUNK + 1,)),
        ],
        compiler_params=params(),
        name="update",
    )(live, core, steps, pred, design, load, fact, by_load, by_fact)


def score_kernel(core_ref, mine_ref, other_ref, out_hbm, sent):
    core = core_ref[0]
    sends = [
        pltpu.make_async_copy(
            ref, out_hbm.at[pl.ds(pl.multiple_of(32 * half, 32), 32), :], sent.at[i]
        )
        for i, (half, ref) in enumerate(((core, mine_ref), (1 - core, other_ref)))
    ]
    for send in sends:
        send.start()
    for send in sends:
        send.wait()


def joined_score(core, mine, other):
    return pl.pallas_call(
        score_kernel,
        in_specs=[smem(), vmem(), vmem()],
        out_specs=hbm(),
        out_shape=pltpu.HBM((FACT, mine.shape[1]), F32),
        scratch_shapes=[pltpu.SemaphoreType.DMA((2,))],
        compiler_params=params(),
        name="joined_score",
    )(core, mine, other)


def factor_kernel(parts_ref, out_hbm, stage, sent):
    total = parts_ref[0]
    for j in range(1, parts_ref.shape[0]):
        total = total + parts_ref[j]
    stage[...] = total[:8, :] / (total[8:, :] + 1.0)
    sends = [
        pltpu.make_async_copy(stage, out_hbm.at[z], sent.at[z]) for z in range(out_hbm.shape[0])
    ]
    for send in sends:
        send.start()
    for send in sends:
        send.wait()


def factor_share(parts):
    peers, _, cells = parts.shape
    return pl.pallas_call(
        factor_kernel,
        in_specs=[vmem()],
        out_specs=hbm(),
        out_shape=pltpu.HBM((peers, 8, cells), F32),
        scratch_shapes=[pltpu.VMEM((8, cells), F32), pltpu.SemaphoreType.DMA((peers,))],
        compiler_params=params(),
        name="factor_share",
    )(parts)


def settle_kernel(value_ref, out_hbm, sent):
    sends = [
        pltpu.make_async_copy(value_ref.at[z], out_hbm.at[z], sent.at[z])
        for z in range(value_ref.shape[0])
    ]
    for send in sends:
        send.start()
    for send in sends:
        send.wait()


def settled(value):
    return pl.pallas_call(
        settle_kernel,
        in_specs=[vmem()],
        out_specs=hbm(),
        out_shape=pltpu.HBM(value.shape, value.dtype),
        scratch_shapes=[pltpu.SemaphoreType.DMA((value.shape[0],))],
        compiler_params=params(),
        name="settled",
    )(value)


def exchange(value, axis, groups=None):
    return lax.all_to_all(
        value, axis, split_axis=0, concat_axis=0, tiled=True, axis_index_groups=groups
    )


def partners(move):
    def index(x, y, core):
        return (x * 4 + y) * 2 + core

    return [
        (index(x, y, core), index(*move(x, y, core)))
        for x in range(4)
        for y in range(4)
        for core in range(2)
    ]


def around(at, size):
    return [min((i - at) % size, (at - i) % size) for i in range(size)]


def nearest_first(x, y):
    far_x, far_y = around(x, 4), around(y, 4)
    chips = [(i, j) for i in range(4) for j in range(4)]
    return sorted(chips, key=lambda chip: far_x[chip[0]] + far_y[chip[1]])


FIRST = (3, 2, 5)
SAME_CORE = [[(4 * x + y) * 2 + core for x, y in nearest_first(*FIRST[:2])] for core in range(2)]
CORE_FIRST = [SAME_CORE[0] + SAME_CORE[1]]
RING = [[(FIRST[2] + step) % 8 for step in (0, 1, -1, 2, -2, 3, -3, 4)]]
OTHER_CORE = partners(lambda x, y, c: (x, y, 1 - c))
STAGES = [
    [
        partners(lambda x, y, c, k=k: (x ^ k, y, c) if c == swap else (x, y ^ k, c))
        for k in (1, 2, 3)
    ]
    for swap in (0, 1)
]


def local(
    counts, batch_id, live_cells, knot_bin, depth_frac, cell_covariates,
    coefficients, batch_effect, factors, loadings,
):
    fact, load = factors.T, loadings.T
    tot = exchange(cell_totals(counts, 8), "gene", RING)
    rest, design, score, by_load, by_fact = prepare(
        live_cells, counts, knot_bin[None], depth_frac[None], batch_id[None],
        cell_covariates, coefficients.T, batch_effect.T, load, fact,
    )
    core = (lax.axis_index("cell") % 2)[None]
    pred, packed = gram_sums(live_cells, core, tot, rest, design, score)
    steps = exchange(solve(exchange(packed, "cell", SAME_CORE)), "cell", CORE_FIRST)
    pieces, kept, given, beta = update(
        live_cells, core, steps.reshape(32, 384), pred, design, load, fact, by_load, by_fact
    )
    arrived = exchange(pieces, "gene", RING)

    value = kept + lax.ppermute(given, "cell", OTHER_CORE)
    for moves in STAGES:
        near, across, beside = (lax.ppermute(value, "cell", pairs) for pairs in moves)
        value = (value + near) + (across + beside)
    gathered = settled(exchange(factor_share(arrived), "gene", RING))
    mine = value[:32] / jnp.sqrt(value[32:] + 1.0)
    other = lax.ppermute(mine, "cell", OTHER_CORE)
    score = joined_score(core, mine, other)
    factor_step = gathered.reshape(FACT, -1)
    return beta.T, factor_step.T, score.T


def solution(mesh):
    placed = (
        P("gene", "cell"),
        P("cell"),
        P("cell"),
        P("cell"),
        P("cell"),
        P(None, "cell"),
        P("gene", None),
        P("gene", None),
        P("cell", None),
        P("gene", None),
    )
    return jax.shard_map(
        local,
        mesh=mesh,
        in_specs=placed,
        out_specs=(P("gene", None), P("cell", None), P("gene", None)),
        check_vma=False,
    )
```
